32 devices in a mesh: ctx: 8 (over y, x, core), fsdp: 4 (over z).
Axes of the slice: x: 2, y: 2, z: 4, core: 2. Of those that a mesh axis runs over, the one named last changes fastest.
Arguments:
- layer_input: bfloat16 [4, 2048, 2048], P('fsdp', 'ctx'), may hold values from -6 to 6
- dy: bfloat16 [4, 2048, 2048], P('fsdp', 'ctx'), may hold values from -6 to 6
- block_order: int32 [8, 2], replicated, may hold values from 0 to 15, as said below
- lengths: int32 [4], P('fsdp'), may hold values from 512 to 2048, as said below
- attn_gain: bfloat16 [2048], P('fsdp'), may hold values from 0.25 to 1.75
- wq: bfloat16 [2048, 2048], P('fsdp'), may hold values from -0.125 to 0.125
- wk: bfloat16 [2048, 1024], P('fsdp'), may hold values from -0.125 to 0.125
- wv: bfloat16 [2048, 1024], P('fsdp'), may hold values from -0.125 to 0.125
- q_gain: bfloat16 [128], replicated, may hold values from 0.5 to 3
- k_gain: bfloat16 [128], replicated, may hold values from 0.5 to 3
- wo: bfloat16 [2048, 2048], P('fsdp'), may hold values from -1.5 to 1.5
- mlp_gain: bfloat16 [2048], P('fsdp'), may hold values from 0.25 to 1.75
- wg: bfloat16 [2048, 6144], P('fsdp'), may hold values from -0.125 to 0.125
- wu: bfloat16 [2048, 6144], P('fsdp'), may hold values from -0.125 to 0.125
- wd: bfloat16 [2048, 6144], P('fsdp'), may hold values from -0.078125 to 0.078125
Outputs:
- layer_output: bfloat16 [4, 2048, 2048], P('fsdp', 'ctx')
- dx: float32 [4, 2048, 2048], P('fsdp', 'ctx')
- d_wq: float32 [2048, 2048], P(('ctx', 'fsdp'))
- d_wk: float32 [2048, 1024], P(('ctx', 'fsdp'))
- d_wv: float32 [2048, 1024], P(('ctx', 'fsdp'))
- d_wo: float32 [2048, 2048], P(('ctx', 'fsdp'))
- d_wg: float32 [2048, 6144], P(('ctx', 'fsdp'))
- d_wu: float32 [2048, 6144], P(('ctx', 'fsdp'))
- d_wd: float32 [2048, 6144], P(('ctx', 'fsdp'))
- d_attn_gain: float32 [2048], replicated
- d_mlp_gain: float32 [2048], replicated
- d_q_gain: float32 [128], replicated
- d_k_gain: float32 [128], replicated
The draws below stay inside these ranges and needn't reach their ends.
Inputs may be any that keep to these rules, and one draw needn't show every extreme that they name: `block_order`: row c holds a pair of blocks b and 15 - b; the first column is a permutation of 0 to 7. `lengths`: at least one sequence has the full length 2048.
All inputs are finite; a program needn't handle non-finite values.
Results may differ from the reference program's by a relative error of at most 0.023.
Values may be sent and summed in bfloat16 or wider, within the bound.
No kernel may reach another device: no remote copies, remote signals or barrier semaphores. Data moves between devices by JAX's collectives and lax.ppermute only.
A program may use at most 640 MiB of HBM per device.

```python
import math
import jax
import jax.numpy as jnp
from jax import lax

MODEL_WIDTH = 2048
QUERY_HEADS = 16
KEY_VALUE_HEADS = 8
HEAD_SIZE = 128
FF = 6144
BLK = 128
SEQ_LEN = 2048
SEQS = 4
N_CTX = 8


def draw_block_order(key, part):
    first = jax.random.permutation(key, N_CTX).astype(jnp.int32)
    return jnp.stack([first, 2 * N_CTX - 1 - first], axis=1).astype(jnp.int32)


def draw_lengths(key, part):
    key_one = jax.random.fold_in(key, 11)
    key_two = jax.random.fold_in(key, 23)
    drawn = jax.random.randint(key_one, (SEQS,), SEQ_LEN // 4, SEQ_LEN + 1).astype(jnp.int32)
    chosen = jax.random.randint(key_two, (), 0, SEQS).astype(jnp.int32)
    return jnp.where(jnp.arange(SEQS, dtype=jnp.int32) == chosen, SEQ_LEN, drawn).astype(jnp.int32)


def levels(stream_key, dims, cuts, smallest, top_value):
    loudness, own = 1.0, jax.random.fold_in(stream_key, 6)
    for dim, shards_of in cuts:
        heights = jnp.exp(jax.random.uniform(jax.random.fold_in(own, dim), (shards_of,), jnp.float32, smallest / len(cuts), top_value / len(cuts)))
        loudness = loudness * jnp.repeat(heights, dims[dim] // shards_of).reshape([-1 if axis == dim else 1 for axis in range(len(dims))])
    return loudness


def centred(own_key, extent, scale, limit, cuts=(), held_as=jnp.bfloat16):
    values = jax.random.normal(own_key, extent, jnp.float32) * scale
    if len(cuts) > 0:
        values = levels(own_key, extent, cuts, -0.22, 0.18) * values
    return jnp.clip(values, min=-limit, max=limit).astype(held_as)


def setup_inputs(seed: int = 0) -> dict:
    keys = jax.random.split(jax.random.key(seed), 16)
    return {
        "layer_input": centred(keys[0], (SEQS, SEQ_LEN, MODEL_WIDTH), 1.0, 6.0, ((0, 4), (1, 8))),
        "dy": centred(keys[1], (SEQS, SEQ_LEN, MODEL_WIDTH), 1.0, 6.0, ((0, 4), (1, 8))),
        "block_order": draw_block_order(jax.random.fold_in(keys[15], 71), 0),
        "lengths": draw_lengths(jax.random.fold_in(keys[15], 71), 0),
        "attn_gain": jnp.clip(1.0 + 0.15 * jax.random.normal(keys[4], (MODEL_WIDTH,), jnp.float32), 0.25, 1.75).astype(jnp.bfloat16),
        "wq": centred(keys[5], (MODEL_WIDTH, QUERY_HEADS * HEAD_SIZE), MODEL_WIDTH ** -0.5, 0.125, ((0, 4),)),
        "wk": centred(keys[6], (MODEL_WIDTH, KEY_VALUE_HEADS * HEAD_SIZE), MODEL_WIDTH ** -0.5, 0.125, ((0, 4),)),
        "wv": centred(keys[7], (MODEL_WIDTH, KEY_VALUE_HEADS * HEAD_SIZE), MODEL_WIDTH ** -0.5, 0.125, ((0, 4),)),
        "q_gain": jnp.clip(jnp.exp(jax.random.uniform(keys[8], (HEAD_SIZE,), jnp.float32, math.log(0.5), math.log(3.0))), 0.5, 3.0).astype(jnp.bfloat16),
        "k_gain": jnp.clip(jnp.exp(jax.random.uniform(keys[9], (HEAD_SIZE,), jnp.float32, math.log(0.5), math.log(3.0))), 0.5, 3.0).astype(jnp.bfloat16),
        "wo": centred(keys[10], (MODEL_WIDTH, QUERY_HEADS * HEAD_SIZE), (HEAD_SIZE // 8) ** -0.5, 1.5, ((0, 4),)),
        "mlp_gain": jnp.clip(1.0 + 0.15 * jax.random.normal(keys[11], (MODEL_WIDTH,), jnp.float32), 0.25, 1.75).astype(jnp.bfloat16),
        "wg": centred(keys[12], (MODEL_WIDTH, FF), MODEL_WIDTH ** -0.5, 0.125, ((0, 4),)),
        "wu": centred(keys[13], (MODEL_WIDTH, FF), MODEL_WIDTH ** -0.5, 0.125, ((0, 4),)),
        "wd": centred(keys[14], (MODEL_WIDTH, FF), FF ** -0.5, 0.078125, ((0, 4),)),
    }


epsilon = 1e-06
rope_base = 1000000.0
highest_precision = lax.Precision.HIGHEST

@jax.custom_vjp
def lower_precision(v):
    return lax.optimization_barrier(v.astype(jnp.bfloat16)).astype(jnp.float32)

@jax.custom_vjp
def lower_backward_precision(v):
    return v

def low_keep(v):
    return (lower_precision(v), None)

def low_pass(kept, grad):
    return (grad,)

def back_keep(v):
    return (v, None)

def back_low(kept, grad):
    return (lower_precision(grad),)
lower_precision.defvjp(low_keep, low_pass)
lower_backward_precision.defvjp(back_keep, back_low)

def rms_norm(values, gain_row):
    return values * lax.rsqrt(lax.optimization_barrier(jnp.mean(values * values, axis=-1, keepdims=True)) + epsilon) * gain_row

def rotate(values, places):
    half_width = values.shape[-1] // 2
    frequency = jnp.exp(-math.log(rope_base) * 2.0 * jnp.arange(half_width, dtype=jnp.float32) / values.shape[-1])
    angle = places[:, None].astype(jnp.float32) * frequency[None, :]
    cosine = jnp.cos(angle)[:, None, :]
    sine = jnp.sin(angle)[:, None, :]
    first = values[..., :half_width]
    second = values[..., half_width:]
    return jnp.concatenate([first * cosine - second * sine, second * cosine + first * sine], axis=-1)

def attend(query_block, key_b, value_half_rows, query_places, key_places, seq_length):
    raw = jnp.einsum('qkgd,nkd->qkgn', query_block, key_b, precision=highest_precision)
    allowed = (key_places[None, :] <= query_places[:, None]) & (key_places[None, :] < seq_length)
    scores = jnp.where(allowed[:, None, None, :], raw * (1.0 / math.sqrt(HEAD_SIZE)), -1e+30)
    scores = lower_backward_precision(scores)
    probs = jax.nn.softmax(scores, axis=-1)
    result = jnp.einsum('qkgn,nkd->qkgd', lower_precision(probs), value_half_rows, precision=highest_precision)
    return result.reshape(query_block.shape[0], QUERY_HEADS * HEAD_SIZE)

def attend_all(query_half_rows, key_b, value_half_rows, places, seq_length):
    total_length = query_half_rows.shape[0]
    query_row_matrix = math.gcd(total_length, 512)
    query_block_list = query_half_rows.reshape(total_length // query_row_matrix, query_row_matrix, KEY_VALUE_HEADS, QUERY_HEADS // KEY_VALUE_HEADS, HEAD_SIZE)
    place_blocks = places.reshape(total_length // query_row_matrix, query_row_matrix)

    def one_block(item):
        return attend(item[0], key_b, value_half_rows, item[1], places, seq_length)
    block_outputs = lax.map(jax.checkpoint(one_block), (query_block_list, place_blocks))
    return block_outputs.reshape(total_length, QUERY_HEADS * HEAD_SIZE)

def layer(x_seq, seq_length, places, params):
    attn_gain, wq, wk, wv, q_gain, k_gain, wo, mlp_gain, wg, wu, wd = params
    total_length = x_seq.shape[0]
    normalized_input = lower_precision(rms_norm(x_seq, attn_gain))
    query = lower_backward_precision(jnp.dot(normalized_input, wq, precision=highest_precision)).reshape(total_length, QUERY_HEADS, HEAD_SIZE)
    key_unnormed = lower_backward_precision(jnp.dot(normalized_input, wk, precision=highest_precision)).reshape(total_length, KEY_VALUE_HEADS, HEAD_SIZE)
    value_half_rows = lower_backward_precision(lower_precision(jnp.dot(normalized_input, wv, precision=highest_precision))).reshape(total_length, KEY_VALUE_HEADS, HEAD_SIZE)
    query_half_rows = lower_backward_precision(lower_precision(rotate(rms_norm(query, q_gain), places)))
    key_b = lower_backward_precision(lower_precision(rotate(rms_norm(key_unnormed, k_gain), places)))
    attn_out = attend_all(query_half_rows, key_b, value_half_rows, places, seq_length)
    attn_b = lower_backward_precision(lower_precision(attn_out))
    branch_one = lower_backward_precision(jnp.dot(attn_b, wo.T, precision=highest_precision))
    hidden_one = x_seq + branch_one
    normed_two = lower_precision(rms_norm(hidden_one, mlp_gain))
    gate = lower_backward_precision(jnp.dot(normed_two, wg, precision=highest_precision))
    up_val = lower_backward_precision(jnp.dot(normed_two, wu, precision=highest_precision))
    activated = lower_precision(jax.nn.silu(gate) * up_val)
    branch_two = lower_backward_precision(jnp.dot(activated, wd.T, precision=highest_precision))
    return hidden_one + branch_two

def reference(layer_input, dy, block_order, lengths, attn_gain, wq, wk, wv, q_gain, k_gain, wo, mlp_gain, wg, wu, wd):
    places = (block_order[:, :, None] * BLK + jnp.arange(BLK, dtype=jnp.int32)[None, None, :]).reshape(-1).astype(jnp.int32)
    params = tuple((w.astype(jnp.float32) for w in (attn_gain, wq, wk, wv, q_gain, k_gain, wo, mlp_gain, wg, wu, wd)))
    layer_saved = jax.checkpoint(layer)

    def forward(x_all, weights):

        def one_sequence(carry, item):
            return (carry, layer_saved(item[0], item[1], places, weights))
        unused, outputs = lax.scan(one_sequence, jnp.zeros((), jnp.float32), (x_all, lengths))
        return outputs
    outputs, pullback = jax.vjp(forward, layer_input.astype(jnp.float32), params)
    grad_x, grads = pullback(dy.astype(jnp.float32))
    g_attn_gain, g_wq, g_wk, g_wv, g_q_gain, g_k_gain, g_wo, g_mlp_gain, g_wg, g_wu, g_wd = grads
    return (outputs.astype(jnp.bfloat16), grad_x, g_wq, g_wk, g_wv, g_wo, g_wg, g_wu, g_wd, g_attn_gain, g_mlp_gain, g_q_gain, g_k_gain)
```

```python
import functools
import math

import jax
import jax.numpy as jnp
from jax import lax
from jax.experimental import pallas as pl
from jax.experimental.pallas import tpu as pltpu
from jax.sharding import PartitionSpec as P

QUERY_HEADS = 16
KEY_VALUE_HEADS = 8
HEAD_SIZE = 128

epsilon = 1e-06
rope_base = 1000000.0
large_negative = -1e30

bf16 = jnp.bfloat16
f32 = jnp.float32
VMEM_LIMIT = 56 * 1024 * 1024


def dot_nn(left, right):
    return lax.dot_general(left, right, (((1,), (0,)), ((), ())), preferred_element_type=f32)


def dot_nt(left, right):
    return lax.dot_general(left, right, (((1,), (1,)), ((), ())), preferred_element_type=f32)


def dot_tn(left, right):
    return lax.dot_general(left, right, (((0,), (0,)), ((), ())), preferred_element_type=f32)


def rms_scale(values):
    return lax.rsqrt(jnp.mean(values * values, axis=-1, keepdims=True) + epsilon)


def swap(values, n, bits):
    return lax.ppermute(values, "ctx", [(c, c ^ bits) for c in range(n)])


def slot_order(n):
    return lax.axis_index("ctx") ^ jnp.arange(n, dtype=jnp.int32)


def gather_slots(rows, n):
    if n != 8:
        full = lax.all_gather(rows, "ctx", axis=0)
        return jnp.take(full, slot_order(n), axis=0)
    half = rows.shape[0] // 2
    from_x = swap(rows, n, 2)
    from_y = swap(rows, n, 4)
    from_s = swap(rows, n, 1)
    diag_a = swap(from_x[:half], n, 4)
    diag_b = swap(from_y[half:], n, 2)
    sib_x = swap(from_x, n, 1)
    sib_y = swap(from_y, n, 1)
    sib_a = swap(diag_a, n, 1)
    sib_b = swap(diag_b, n, 1)
    whole = jnp.concatenate(
        [rows, from_s, from_x, sib_x, from_y, sib_y, diag_a, diag_b, sib_a, sib_b], axis=0
    )
    return whole.reshape(n, rows.shape[0], rows.shape[1])


def scatter_slots(product, left, n):
    rows = left.shape[1]
    if n != 8:
        part = product(left.reshape(n * rows, -1)).astype(bf16)
        part = jnp.take(part.reshape(n, rows, -1), slot_order(n), axis=0)
        return lax.psum_scatter(part, "ctx", scatter_dimension=0, tiled=True)[0].astype(f32)
    half = rows // 2
    pairs = left.reshape(4, 2, rows, -1)
    odd = product(pairs[:, 1].reshape(4 * rows, -1)).astype(bf16).reshape(4, rows, -1)
    even = product(pairs[:, 0].reshape(4 * rows, -1)).astype(bf16).reshape(4, rows, -1)
    got = swap(odd, n, 1)
    total = even.astype(f32) + got.astype(f32)
    send_x = jnp.stack([total[1, :half], total[3, :half]]).astype(bf16)
    send_y = jnp.stack([total[2, half:], total[3, half:]]).astype(bf16)
    got_x = swap(send_x, n, 2).astype(f32)
    got_y = swap(send_y, n, 4).astype(f32)
    last_y = (total[2, :half] + got_x[1]).astype(bf16)
    last_x = (total[1, half:] + got_y[1]).astype(bf16)
    fin_y = swap(last_y, n, 4).astype(f32)
    fin_x = swap(last_x, n, 2).astype(f32)
    return jnp.concatenate(
        [total[0, :half] + got_x[0] + fin_y, total[0, half:] + got_y[0] + fin_x], axis=0
    )


def exchange_columns(blocks, n):
    if n != 8:
        got = lax.all_to_all(blocks, "ctx", 0, 0, tiled=True)
    else:
        order = slot_order(n)
        ordered = jnp.take(blocks, order, axis=0)
        got = jnp.stack([ordered[0]] + [swap(ordered[s], n, s) for s in range(1, n)])
        got = jnp.take(got, order, axis=0)
    return got


def reduce_rows(grad, n, n_fsdp):
    depth, width = grad.shape
    rows = depth // (n * n_fsdp)
    parts = grad.astype(bf16).reshape(n, n_fsdp, rows, width).transpose(1, 0, 2, 3)
    summed = lax.psum_scatter(
        parts.reshape(depth, width), "fsdp", scatter_dimension=0, tiled=True
    )
    return exchange_columns(summed.reshape(n, rows, width), n)


def join_columns(got):
    n, rows, width = got.shape
    return got.transpose(1, 0, 2).reshape(rows, n * width).astype(f32)


def project_kernel(
    heads, place_ref, x_ref, gain_ref, w_ref, qg_ref, kg_ref, cos_ref, sin_ref,
    xn_ref, qraw_ref, kraw_ref, qb_ref, kb_ref, vb_ref,
):
    slot = pl.program_id(0)
    x = x_ref[0].astype(f32)
    xn = (x * rms_scale(x) * gain_ref[...]).astype(bf16)
    xn_ref[0] = xn
    y = jnp.dot(xn, w_ref[...], preferred_element_type=f32)
    blk = x.shape[0] // 2
    for half in range(2):
        place = place_ref[2 * slot + half]
        at = pl.ds(pl.multiple_of(place * blk, blk), blk)
        cosine, sine = cos_ref[at, :], sin_ref[at, :]
        rows = y[half * blk : (half + 1) * blk]
        for head in range(heads + 1):
            raw = rows[:, head * HEAD_SIZE : (head + 1) * HEAD_SIZE]
            gain = (qg_ref if head < heads else kg_ref)[...]
            normed = raw * rms_scale(raw) * gain
            turned = normed * cosine + pltpu.roll(normed, HEAD_SIZE // 2, 1) * sine
            if head < heads:
                cols = slice(head * HEAD_SIZE, (head + 1) * HEAD_SIZE)
                qraw_ref[at, cols] = raw
                qb_ref[at, cols] = turned.astype(bf16)
            else:
                kraw_ref[at, :] = raw
                kb_ref[at, :] = turned.astype(bf16)
        vb_ref[at, :] = rows[:, (heads + 1) * HEAD_SIZE :].astype(bf16)


def project(x_slots, places, gain, w, q_gain, k_gain, cosine, sine, heads):
    n, rows, depth = x_slots.shape
    total = n * rows
    const = lambda i, p: (0, 0)
    whole = lambda a: pl.BlockSpec(a.shape, const)
    out = [
        jax.ShapeDtypeStruct((n, rows, depth), bf16),
        jax.ShapeDtypeStruct((total, heads * HEAD_SIZE), f32),
        jax.ShapeDtypeStruct((total, HEAD_SIZE), f32),
        jax.ShapeDtypeStruct((total, heads * HEAD_SIZE), bf16),
        jax.ShapeDtypeStruct((total, HEAD_SIZE), bf16),
        jax.ShapeDtypeStruct((total, HEAD_SIZE), bf16),
    ]
    args = (gain, w, q_gain, k_gain, cosine, sine)
    return pl.pallas_call(
        functools.partial(project_kernel, heads),
        grid_spec=pltpu.PrefetchScalarGridSpec(
            num_scalar_prefetch=1,
            grid=(n,),
            in_specs=[pl.BlockSpec((1, rows, depth), lambda i, p: (i, 0, 0))]
            + [whole(a) for a in args],
            out_specs=[pl.BlockSpec((1, rows, depth), lambda i, p: (i, 0, 0))]
            + [pl.BlockSpec(o.shape, const) for o in out[1:]],
        ),
        out_shape=out,
        compiler_params=pltpu.CompilerParams(
            dimension_semantics=("arbitrary",), vmem_limit_bytes=VMEM_LIMIT
        ),
        cost_estimate=pl.CostEstimate(
            flops=2 * total * depth * w.shape[1],
            bytes_accessed=4 * total * depth + 16 * total * HEAD_SIZE,
            transcendentals=total,
        ),
        name="project",
    )(places, x_slots, *args)


def attend_kernel(heads, tile, length_ref, place_ref, q_ref, k_ref, v_ref, o_ref, a_ref, lse_ref):
    total = q_ref.shape[0]
    blk = total // place_ref.shape[0]
    scale = 1.0 / math.sqrt(HEAD_SIZE)
    length = length_ref[0]
    key_tiles = (length + tile - 1) // tile

    def q_step(i, unused):
        q_at = pl.ds(pl.multiple_of(i * tile, tile), tile)
        q = [q_ref[q_at, h * HEAD_SIZE : (h + 1) * HEAD_SIZE] for h in range(heads)]

        def tile_step(j, carry, masked):
            k_at = pl.ds(pl.multiple_of(j * tile, tile), tile)
            k, v = k_ref[k_at, :], v_ref[k_at, :]
            if masked:
                key = j * tile + lax.broadcasted_iota(jnp.int32, (tile, tile), 0)
                query = i * tile + lax.broadcasted_iota(jnp.int32, (tile, tile), 1)
                allowed = (key <= query) & (key < length)
            new = []
            for h in range(heads):
                top, tot, out = carry[h]
                s = dot_nt(k, q[h]) * scale
                if masked:
                    s = jnp.where(allowed, s, large_negative)
                top_new = jnp.maximum(top, jnp.max(s, axis=0, keepdims=True))
                shrink = jnp.exp(top - top_new)
                p = jnp.exp(s - top_new)
                tot = tot * shrink + jnp.sum(p, axis=0, keepdims=True)
                out = out * shrink + dot_tn(v, p.astype(bf16))
                new.append((top_new, tot, out))
            return tuple(new)

        start = tuple(
            (
                jnp.full((1, tile), large_negative, f32),
                jnp.zeros((1, tile), f32),
                jnp.zeros((HEAD_SIZE, tile), f32),
            )
            for _ in range(heads)
        )
        full = jnp.minimum(i, length // tile)
        carry = lax.fori_loop(0, full, functools.partial(tile_step, masked=False), start)
        carry = lax.fori_loop(
            full, jnp.minimum(i + 1, key_tiles), functools.partial(tile_step, masked=True), carry
        )
        for h in range(heads):
            top, tot, out = carry[h]
            lse_ref[pl.ds(h, 1), q_at] = top + jnp.log(tot)
            o = jnp.transpose(out / tot)
            cols = slice(h * HEAD_SIZE, (h + 1) * HEAD_SIZE)
            o_ref[q_at, cols] = o
        return unused

    lax.fori_loop(0, total // tile, q_step, 0)

    def place_step(b, unused):
        src = pl.ds(pl.multiple_of(place_ref[b] * blk, blk), blk)
        dst = pl.ds(pl.multiple_of(b * blk, blk), blk)
        a_ref[dst, :] = o_ref[src, :].astype(bf16)
        return unused

    lax.fori_loop(0, place_ref.shape[0], place_step, 0)


def attend(length, places, q, k, v, heads):
    total = q.shape[0]
    tile = min(512, total)
    vm = lambda: pl.BlockSpec(memory_space=pltpu.VMEM)
    sm = lambda: pl.BlockSpec(memory_space=pltpu.SMEM)
    return pl.pallas_call(
        functools.partial(attend_kernel, heads, tile),
        in_specs=[sm(), sm(), vm(), vm(), vm()],
        out_specs=[vm(), vm(), vm()],
        out_shape=[
            jax.ShapeDtypeStruct((total, heads * HEAD_SIZE), f32),
            jax.ShapeDtypeStruct((total, heads * HEAD_SIZE), bf16),
            jax.ShapeDtypeStruct((heads, total), f32),
        ],
        compiler_params=pltpu.CompilerParams(vmem_limit_bytes=VMEM_LIMIT),
        cost_estimate=pl.CostEstimate(
            flops=2 * heads * total * total * HEAD_SIZE,
            bytes_accessed=12 * total * heads * HEAD_SIZE,
            transcendentals=heads * total * total // 2,
        ),
        name="attend",
    )(length, places, q, k, v)


def unturn(grad, raw, gain, cosine, sine):
    grad = grad * cosine - pltpu.roll(grad, HEAD_SIZE // 2, 1) * sine
    scale = rms_scale(raw)
    hat = raw * scale
    inner = grad * gain
    out = scale * (inner - hat * jnp.mean(inner * hat, axis=-1, keepdims=True))
    return out, jnp.sum(grad * hat, axis=0, keepdims=True)


def attend_back_kernel(
    heads, tile, finish_keys, length_ref, place_ref, q_ref, k_ref, v_ref, da_ref, o_ref, lse_ref,
    qraw_ref, kraw_ref, qg_ref, kg_ref, cos_ref, sin_ref,
    d_ref, dqg_ref, dkg_ref, *rest,
):
    if finish_keys:
        da_s, delta_s, dq_s, dk_s, dv_s = rest
    else:
        dk_s, dv_s, da_s, delta_s, dq_s = rest
    total = q_ref.shape[0]
    blocks = place_ref.shape[0]
    blk = total // blocks
    scale = 1.0 / math.sqrt(HEAD_SIZE)
    length = length_ref[0]
    tiles = total // tile

    def sort_step(b, unused):
        dst = pl.ds(pl.multiple_of(place_ref[b] * blk, blk), blk)
        src = pl.ds(pl.multiple_of(b * blk, blk), blk)
        piece = da_ref[src, :]
        da_s[dst, :] = piece
        prod = piece.astype(f32) * o_ref[dst, :]
        for h in range(heads):
            cols = slice(h * HEAD_SIZE, (h + 1) * HEAD_SIZE)
            delta_s[pl.ds(h, 1), dst] = jnp.sum(jnp.transpose(prod[:, cols]), axis=0, keepdims=True)
        return unused

    lax.fori_loop(0, blocks, sort_step, 0)
    dq_s[...] = jnp.zeros_like(dq_s)
    dk_s[...] = jnp.zeros_like(dk_s)
    dv_s[...] = jnp.zeros_like(dv_s)

    def k_step(j, unused):
        k_at = pl.ds(pl.multiple_of(j * tile, tile), tile)
        k, v = k_ref[k_at, :], v_ref[k_at, :]

        def tile_step(i, carry, masked):
            dk, dv = carry
            q_at = pl.ds(pl.multiple_of(i * tile, tile), tile)
            if masked:
                key = j * tile + lax.broadcasted_iota(jnp.int32, (tile, tile), 0)
                query = i * tile + lax.broadcasted_iota(jnp.int32, (tile, tile), 1)
                allowed = (key <= query) & (key < length)
            for h in range(heads):
                cols = slice(h * HEAD_SIZE, (h + 1) * HEAD_SIZE)
                q, da = q_ref[q_at, cols], da_s[q_at, cols]
                s = dot_nt(k, q) * scale - lse_ref[pl.ds(h, 1), q_at]
                if masked:
                    s = jnp.where(allowed, s, large_negative)
                p = jnp.exp(s)
                dp = dot_nt(v, da)
                ds = (p * (dp - delta_s[pl.ds(h, 1), q_at])).astype(bf16)
                dv = dv + dot_nn(p.astype(bf16), da)
                dk = dk + dot_nn(ds, q)
                dq_s[q_at, cols] += dot_tn(ds, k)
            return dk, dv

        zero = jnp.zeros((tile, HEAD_SIZE), f32)
        carry = (zero, zero)
        whole_tile = (j + 1) * tile <= length
        carry = lax.fori_loop(j, j + 1, functools.partial(tile_step, masked=True), carry)
        first_full = jnp.where(whole_tile, j + 1, tiles)
        carry = lax.fori_loop(
            j + 1, first_full, functools.partial(tile_step, masked=True), carry
        )
        carry = lax.fori_loop(first_full, tiles, functools.partial(tile_step, masked=False), carry)
        dk_s[k_at, :], dv_s[k_at, :] = carry[0] * scale, carry[1]
        return unused

    lax.fori_loop(0, (length + tile - 1) // tile, k_step, 0)

    dqg_ref[...] = jnp.zeros_like(dqg_ref)
    dkg_ref[...] = jnp.zeros_like(dkg_ref)

    def last_step(b, unused):
        src = pl.ds(pl.multiple_of(place_ref[b] * blk, blk), blk)
        dst = pl.ds(pl.multiple_of(b * blk, blk), blk)
        cosine, sine = cos_ref[src, :], sin_ref[src, :]
        for h in range(heads):
            cols = slice(h * HEAD_SIZE, (h + 1) * HEAD_SIZE)
            grad = (dq_s[src, cols] * scale).astype(bf16).astype(f32)
            out, gain = unturn(grad, qraw_ref[src, cols], qg_ref[...], cosine, sine)
            d_ref[dst, cols] = out.astype(bf16)
            dqg_ref[...] += gain
        if finish_keys:
            grad = dk_s[src, :].astype(bf16).astype(f32)
            out, gain = unturn(grad, kraw_ref[src, :], kg_ref[...], cosine, sine)
            d_ref[dst, heads * HEAD_SIZE : (heads + 1) * HEAD_SIZE] = out.astype(bf16)
            dkg_ref[...] += gain
            d_ref[dst, (heads + 1) * HEAD_SIZE :] = dv_s[src, :].astype(bf16)
        return unused

    lax.fori_loop(0, blocks, last_step, 0)


def attend_back(length, places, q, k, v, da, o, lse, qraw, kraw, qg, kg, cosine, sine, heads):
    total = q.shape[0]
    tile = min(512, total)
    vm = lambda: pl.BlockSpec(memory_space=pltpu.VMEM)
    sm = lambda: pl.BlockSpec(memory_space=pltpu.SMEM)
    return pl.pallas_call(
        functools.partial(attend_back_kernel, heads, tile, True),
        in_specs=[sm(), sm()] + [vm() for _ in range(12)],
        out_specs=[vm(), vm(), vm()],
        out_shape=[
            jax.ShapeDtypeStruct((total, (heads + 2) * HEAD_SIZE), bf16),
            jax.ShapeDtypeStruct((1, HEAD_SIZE), f32),
            jax.ShapeDtypeStruct((1, HEAD_SIZE), f32),
        ],
        scratch_shapes=[
            pltpu.VMEM((total, heads * HEAD_SIZE), bf16),
            pltpu.VMEM((heads, total), f32),
            pltpu.VMEM((total, heads * HEAD_SIZE), f32),
            pltpu.VMEM((total, HEAD_SIZE), f32),
            pltpu.VMEM((total, HEAD_SIZE), f32),
        ],
        compiler_params=pltpu.CompilerParams(vmem_limit_bytes=VMEM_LIMIT),
        cost_estimate=pl.CostEstimate(
            flops=5 * heads * total * total * HEAD_SIZE,
            bytes_accessed=24 * total * heads * HEAD_SIZE,
            transcendentals=heads * total * total // 2,
        ),
        name="attend_back",
    )(length, places, q, k, v, da, o, lse, qraw, kraw, qg, kg, cosine, sine)


def per_device(
    n, n_fsdp, layer_input, dy, block_order, lengths, attn_gain, wq, wk, wv, q_gain, k_gain, wo,
    mlp_gain, wg, wu, wd,
):
    me = lax.axis_index("ctx")
    rows = layer_input.shape[1]
    blk = rows // 2
    depth = layer_input.shape[2]
    shard = wq.shape[0]
    heads = QUERY_HEADS // n
    kv_share = n // KEY_VALUE_HEADS
    ff = wg.shape[1] // n
    q_cols = heads * HEAD_SIZE

    def cols(w, width, index):
        return lax.dynamic_slice_in_dim(w, index * width, width, axis=1)

    def whole(w):
        return lax.all_gather(w, "fsdp", axis=0, tiled=True)

    kv_index = me // kv_share
    w_in = jnp.concatenate(
        [cols(wq, q_cols, me), cols(wk, HEAD_SIZE, kv_index), cols(wv, HEAD_SIZE, kv_index)], axis=1
    )
    width = w_in.shape[1]
    gains = jnp.concatenate([attn_gain, mlp_gain])
    gain_rows = -(-gains.shape[0] // (16 * width)) * 16
    gains = jnp.pad(gains, (0, gain_rows * width - gains.shape[0])).reshape(gain_rows, width)
    pack = lax.all_gather(jnp.concatenate([w_in, gains], axis=0), "fsdp", axis=0)
    w_in = pack[:, :shard].reshape(n_fsdp * shard, width)
    gains = pack[:, shard:].reshape(n_fsdp, -1)
    attn_gain = gains[:, :shard].reshape(1, depth).astype(f32)
    mlp_gain = gains[:, shard : 2 * shard].reshape(1, depth).astype(f32)
    wo_c = whole(cols(wo, q_cols, me))
    wg_c = whole(cols(wg, ff, me))
    wu_c = whole(cols(wu, ff, me))
    wd_c = whole(cols(wd, ff, me))

    places = jnp.take(block_order, slot_order(n), axis=0).reshape(-1)
    half = HEAD_SIZE // 2
    lane = jnp.arange(HEAD_SIZE, dtype=jnp.int32)
    frequency = jnp.exp(-math.log(rope_base) * 2.0 * (lane % half).astype(f32) / HEAD_SIZE)
    angle = jnp.arange(n * rows, dtype=f32)[:, None] * frequency[None, :]
    cosine = jnp.cos(angle)
    sine = jnp.sin(angle) * jnp.where(lane < half, -1.0, 1.0)[None, :]
    qg = q_gain.astype(f32).reshape(1, HEAD_SIZE)
    kg = k_gain.astype(f32).reshape(1, HEAD_SIZE)

    x_slots = gather_slots(layer_input[0], n)
    dy_slots = gather_slots(dy[0], n)
    xn, q_raw, k_raw, qb, kb, vb = project(
        x_slots, places, attn_gain, w_in, qg, kg, cosine, sine, heads
    )
    o, a, lse = attend(lengths, places, qb, kb, vb, heads)
    z = scatter_slots(lambda v: dot_nt(v, wo_c), a.reshape(n, rows, q_cols), n)

    x = layer_input[0].astype(f32)
    h1 = x + z
    scale_two = rms_scale(h1)
    hat_two = h1 * scale_two
    xn2 = gather_slots((hat_two * mlp_gain).astype(bf16), n).reshape(n * rows, depth)
    gate = dot_nn(xn2, wg_c)
    up = dot_nn(xn2, wu_c)
    sigma = jax.nn.sigmoid(gate)
    silu = gate * sigma
    hm = (silu * up).astype(bf16)
    m = scatter_slots(lambda v: dot_nt(v, wd_c), hm.reshape(n, rows, ff), n)
    output = (h1 + m).astype(bf16)

    dy_all = dy_slots.reshape(n * rows, depth)
    d_wd = reduce_rows(dot_tn(dy_all, hm), n, n_fsdp)
    d_hm = dot_nn(dy_all, wd_c)
    d_gate = (d_hm * up * sigma * (1.0 + gate * (1.0 - sigma))).astype(bf16)
    d_up = (d_hm * silu).astype(bf16)
    d_gu = jnp.concatenate([d_gate, d_up], axis=1).reshape(n, rows, 2 * ff)
    d_xn2 = scatter_slots(lambda v: dot_nt(v[:, :ff], wg_c) + dot_nt(v[:, ff:], wu_c), d_gu, n)
    d_wg = reduce_rows(dot_tn(xn2, d_gate), n, n_fsdp)
    d_wu = reduce_rows(dot_tn(xn2, d_up), n, n_fsdp)
    d_mlp_gain = jnp.sum(d_xn2 * hat_two, axis=0)
    e = d_xn2 * mlp_gain
    d_h1 = dy[0].astype(f32) + scale_two * (
        e - hat_two * jnp.mean(e * hat_two, axis=-1, keepdims=True)
    )

    dz = gather_slots(d_h1.astype(bf16), n).reshape(n * rows, depth)
    da = dot_nn(dz, wo_c).astype(bf16)
    d_wo = reduce_rows(dot_tn(dz, a), n, n_fsdp)
    d_qkv, d_qg, d_kg = attend_back(
        lengths, places, qb, kb, vb, da, o, lse, q_raw, k_raw, qg, kg, cosine, sine, heads
    )
    d_xn = scatter_slots(lambda v: dot_nt(v, w_in), d_qkv.reshape(n, rows, width), n)
    d_win = reduce_rows(dot_tn(xn.reshape(n * rows, depth), d_qkv), n, n_fsdp)
    scale_one = rms_scale(x)
    hat_one = x * scale_one
    d_attn_gain = jnp.sum(d_xn * hat_one, axis=0)
    e = d_xn * attn_gain
    dx = d_h1 + scale_one * (e - hat_one * jnp.mean(e * hat_one, axis=-1, keepdims=True))

    sums = lax.psum(
        jnp.concatenate([d_attn_gain, d_mlp_gain, d_qg[0], d_kg[0]]), ("ctx", "fsdp")
    )
    kv = d_win[:: max(kv_share, 1)]
    return (
        output[None],
        dx[None],
        join_columns(d_win[:, :, :q_cols]),
        join_columns(kv[:, :, q_cols : q_cols + HEAD_SIZE]),
        join_columns(kv[:, :, q_cols + HEAD_SIZE :]),
        join_columns(d_wo),
        join_columns(d_wg),
        join_columns(d_wu),
        join_columns(d_wd),
        sums[:depth],
        sums[depth : 2 * depth],
        sums[2 * depth : 2 * depth + HEAD_SIZE],
        sums[2 * depth + HEAD_SIZE :],
    )


def solution(mesh):
    n, n_fsdp = mesh.shape["ctx"], mesh.shape["fsdp"]
    row, act = P("fsdp", None), P("fsdp", "ctx", None)
    own = P(("ctx", "fsdp"), None)
    return jax.shard_map(
        functools.partial(per_device, n, n_fsdp),
        mesh=mesh,
        in_specs=(
            act, act, P(), P("fsdp"), P("fsdp"), row, row, row, P(), P(), row, P("fsdp"), row, row, row,
        ),
        out_specs=(act, act) + (own,) * 7 + (P(),) * 4,
        check_vma=False,
    )
```

```python
import functools
import math

import jax
import jax.numpy as jnp
from jax import lax
from jax.experimental import pallas as pl
from jax.experimental.pallas import tpu as pltpu
from jax.sharding import PartitionSpec as P

QUERY_HEADS = 16
KEY_VALUE_HEADS = 8
HEAD_SIZE = 128

epsilon = 1e-06
rope_base = 1000000.0
large_negative = -1e30

bf16 = jnp.bfloat16
f32 = jnp.float32
VMEM_LIMIT = 56 * 1024 * 1024


def cost_of(microseconds):
    return pl.CostEstimate(
        flops=int(microseconds * 1.1e9), bytes_accessed=1 << 20, transcendentals=0
    )


def dot_nn(left, right):
    return lax.dot_general(left, right, (((1,), (0,)), ((), ())), preferred_element_type=f32)


def dot_nt(left, right):
    return lax.dot_general(left, right, (((1,), (1,)), ((), ())), preferred_element_type=f32)


def dot_tn(left, right):
    return lax.dot_general(left, right, (((0,), (0,)), ((), ())), preferred_element_type=f32)


def rms_scale(values):
    return lax.rsqrt(jnp.mean(values * values, axis=-1, keepdims=True) + epsilon)


def swap(values, n, bits, axis="ctx"):
    return lax.ppermute(values, axis, [(c, c ^ bits) for c in range(n)])


def swap_first(values, n, first):
    return lax.ppermute(
        values, "ctx", [(c, c ^ (2 if (c % 2 == 0) == first else 4)) for c in range(n)]
    )


def slot_order(n):
    me = lax.axis_index("ctx")
    slots = jnp.arange(n, dtype=jnp.int32)
    if n == 8:
        even = jnp.array([0, 2, 4, 6, 1, 5, 3, 7], jnp.int32)
        odd = jnp.array([0, 4, 2, 6, 1, 3, 5, 7], jnp.int32)
        slots = jnp.where(me % 2 == 0, even, odd)
    return me ^ slots


def any_spec():
    return pl.BlockSpec(memory_space=pl.ANY)


def gather_pieces(rows, n):
    if n != 8:
        full = lax.all_gather(rows, "ctx", axis=0)
        return [jnp.take(full, slot_order(n), axis=0).reshape(-1, rows.shape[1])]
    pair = jnp.concatenate([rows, swap_first(rows, n, True)], axis=0)
    other = swap_first(pair, n, False)
    return [pair, other, swap(pair, n, 1), swap(other, n, 1)]


def piece_copies(pieces, out, sem, rows):
    copies, at = [], 0
    for piece in pieces:
        size = piece.shape[0]
        slot, start = at // rows, at % rows
        if size > rows:
            for k in range(size // rows):
                copies.append(
                    pltpu.make_async_copy(
                        piece.at[pl.ds(k * rows, rows)], out.at[slot + k], sem.at[slot + k]
                    )
                )
        else:
            copies.append(
                pltpu.make_async_copy(piece, out.at[slot, pl.ds(start, size)], sem.at[slot])
            )
        at += size
    return copies


def assemble_kernel(count, rows, *refs):
    out, held, sem, out_sem = refs[count:]
    for copy in piece_copies(refs[:count], held, sem, rows):
        copy.start()
    slots = range(out.shape[0])
    for slot in slots:
        pltpu.make_async_copy(held.at[slot], held.at[slot], sem.at[slot]).wait()
        pltpu.make_async_copy(held.at[slot], out.at[slot], out_sem.at[slot]).start()
    for slot in slots:
        pltpu.make_async_copy(held.at[slot], out.at[slot], out_sem.at[slot]).wait()


def assemble(pieces, n):
    total = sum(p.shape[0] for p in pieces)
    rows, width = total // n, pieces[0].shape[1]
    if len(pieces) == 1:
        return pieces[0].reshape(n, rows, width)
    return pl.pallas_call(
        functools.partial(assemble_kernel, len(pieces), rows),
        in_specs=[any_spec() for _ in pieces],
        out_specs=any_spec(),
        out_shape=jax.ShapeDtypeStruct((n, rows, width), pieces[0].dtype),
        scratch_shapes=[
            pltpu.VMEM((n, rows, width), pieces[0].dtype),
            pltpu.SemaphoreType.DMA((n,)),
            pltpu.SemaphoreType.DMA((n,)),
        ],
        compiler_params=pltpu.CompilerParams(vmem_limit_bytes=VMEM_LIMIT),
        cost_estimate=cost_of(6.0 * total * width / 2**22),
        name="assemble",
    )(*pieces)


def mm_kernel(count, *refs):
    total = dot_nt(refs[0][0], refs[count][...])
    for k in range(1, count):
        total = total + dot_nt(refs[k][0], refs[count + k][...])
    refs[2 * count][0] = total.astype(bf16)


def mm_slots(lefts, ws, column, start, count):
    rows = lefts[0].shape[1]
    width = ws[0].shape[0]
    depths = [left.shape[2] for left in lefts]
    return pl.pallas_call(
        functools.partial(mm_kernel, len(lefts)),
        grid=(count,),
        in_specs=[pl.BlockSpec((1, rows, d), lambda i: (i + start, 0, 0)) for d in depths]
        + [pl.BlockSpec((width, d), lambda i: (0, column)) for d in depths],
        out_specs=pl.BlockSpec((1, rows, width), lambda i: (i, 0, 0)),
        out_shape=jax.ShapeDtypeStruct((count, rows, width), bf16),
        compiler_params=pltpu.CompilerParams(vmem_limit_bytes=VMEM_LIMIT),
        cost_estimate=cost_of(3.5 + 8.0 * count * rows * sum(depths) * width / (1024 * 1536 * 2048)),
        name="mm_slots",
    )(*lefts, *ws)


def add_kernel(mine_ref, got_ref, send_ref, keep_ref):
    half = send_ref.shape[0]
    for i in range(half):
        keep_ref[i] = mine_ref[i].astype(f32) + got_ref[i].astype(f32)
        send_ref[i] = (mine_ref[half + i].astype(f32) + got_ref[half + i].astype(f32)).astype(bf16)


def add_halves(mine, got):
    slots, rows, width = mine.shape
    half, tile = slots // 2, min(width, 512)
    read = pl.BlockSpec((slots, rows, tile), lambda i: (0, 0, i))
    write = pl.BlockSpec((half, rows, tile), lambda i: (0, 0, i))
    return pl.pallas_call(
        add_kernel,
        grid=(width // tile,),
        in_specs=[read, read],
        out_specs=[write, write],
        out_shape=[
            jax.ShapeDtypeStruct((half, rows, width), bf16),
            jax.ShapeDtypeStruct((half, rows, width), f32),
        ],
        compiler_params=pltpu.CompilerParams(vmem_limit_bytes=VMEM_LIMIT),
        cost_estimate=cost_of(6.5 * slots * rows * width / 2**21),
        name="add_halves",
    )(mine, got)


def scatter_slots(lefts, ws, column, n):
    if n != 8:
        index = jnp.argsort(slot_order(n))
        part = jnp.take(mm_slots(lefts, ws, column, 0, n), index, axis=0)
        return lax.psum_scatter(part, "ctx", scatter_dimension=0, tiled=True)[0].astype(f32)
    far = mm_slots(lefts, ws, column, 4, 4)
    got = swap(far, n, 1)
    near = mm_slots(lefts, ws, column, 0, 4)
    send, keep = add_halves(near, got)
    got = swap_first(send, n, False)
    last = (keep[1] + got[1].astype(f32)).astype(bf16)
    return keep[0] + got[0].astype(f32) + swap_first(last, n, True).astype(f32)


def exchange(blocks):
    return lax.all_to_all(blocks, "ctx", 0, 0, tiled=True)


def weight_kernel(counts, *refs):
    refs, out_ref = refs[:-1], refs[-1]
    tops, at = [], 0
    for count in counts:
        left = jnp.concatenate([r[...] for r in refs[at : at + count]], axis=0)
        tops.append(dot_tn(left, refs[at + count][...]))
        at += count + 1
    shards, _, rows, width = out_ref.shape
    out_ref[...] = jnp.concatenate(tops, axis=1).astype(bf16).reshape(shards, 1, rows, width)


def weight_grad(pairs, n, n_fsdp):
    depth = pairs[0][0][0].shape[1]
    rows, tile = depth // (n * n_fsdp), depth // n
    width = sum(right.shape[1] for _, right in pairs)
    total = pairs[0][1].shape[0]
    specs, args = [], []
    for pieces, right in pairs:
        specs += [pl.BlockSpec((p.shape[0], tile), lambda j: (0, j)) for p in pieces]
        specs.append(pl.BlockSpec(right.shape, lambda j: (0, 0)))
        args += [*pieces, right]
    out = pl.pallas_call(
        functools.partial(weight_kernel, [len(pieces) for pieces, _ in pairs]),
        grid=(n,),
        in_specs=specs,
        out_specs=pl.BlockSpec((n_fsdp, 1, rows, width), lambda j: (0, j, 0, 0)),
        out_shape=jax.ShapeDtypeStruct((n_fsdp, n, rows, width), bf16),
        compiler_params=pltpu.CompilerParams(vmem_limit_bytes=VMEM_LIMIT),
        cost_estimate=cost_of(16.0 * total * depth * width / (2048 * 2048 * 1152)),
        name="weight_grad",
    )(*args)
    return out.reshape(depth, width)


def reduce_rows(grad, n):
    summed = lax.psum_scatter(grad, "fsdp", scatter_dimension=0, tiled=True)
    return summed.reshape(n, -1, grad.shape[1])


def join_kernel(parts, got_ref, *out_refs):
    for out_ref, slices in zip(out_refs, parts):
        out_ref[...] = jnp.concatenate(
            [got_ref[0, :, lo:hi].astype(f32) for lo, hi in slices], axis=1
        )


def join_columns(got, parts):
    n, rows, width = got.shape
    sizes = [sum(hi - lo for lo, hi in slices) for slices in parts]
    return pl.pallas_call(
        functools.partial(join_kernel, parts),
        grid=(n,),
        in_specs=[pl.BlockSpec((1, rows, width), lambda i: (i, 0, 0))],
        out_specs=[pl.BlockSpec((rows, size), lambda i: (0, i)) for size in sizes],
        out_shape=[jax.ShapeDtypeStruct((rows, n * size), f32) for size in sizes],
        cost_estimate=cost_of(5.0),
        name="join_columns",
    )(got)


def sum_all(values, n, n_fsdp):
    bits = 1
    while bits < n:
        values = values + swap(values, n, bits)
        bits *= 2
    bits = 1
    while bits < n_fsdp:
        values = values + swap(values, n_fsdp, bits, "fsdp")
        bits *= 2
    return values


def after(values, *others):
    return lax.optimization_barrier((values,) + others)[0]


def project_kernel(count, heads, place_ref, *refs):
    pieces, refs = refs[:count], refs[count:]
    gain_ref, w_ref, qg_ref, kg_ref, cos_ref, sin_ref = refs[:6]
    xn_ref, qraw_ref, kraw_ref, qb_ref, kb_ref, vb_ref, x_all, sem = refs[6:]
    slot = pl.program_id(0)

    @pl.when(slot == 0)
    def _():
        for copy in piece_copies(pieces, x_all, sem, x_all.shape[1]):
            copy.start()

    pltpu.make_async_copy(x_all.at[slot], x_all.at[slot], sem.at[slot]).wait()
    x = x_all[slot].astype(f32)
    xn = (x * rms_scale(x) * gain_ref[...]).astype(bf16)
    xn_ref[0] = xn
    w = w_ref[...].reshape(x.shape[1], w_ref.shape[2])
    y = jnp.dot(xn, w, preferred_element_type=f32)
    blk = x.shape[0] // 2
    for half in range(2):
        place = place_ref[2 * slot + half]
        at = pl.ds(pl.multiple_of(place * blk, blk), blk)
        cosine, sine = cos_ref[at, :], sin_ref[at, :]
        rows = y[half * blk : (half + 1) * blk]
        for head in range(heads + 1):
            raw = rows[:, head * HEAD_SIZE : (head + 1) * HEAD_SIZE]
            gain = (qg_ref if head < heads else kg_ref)[...]
            normed = raw * rms_scale(raw) * gain
            turned = normed * cosine + pltpu.roll(normed, HEAD_SIZE // 2, 1) * sine
            if head < heads:
                cols = slice(head * HEAD_SIZE, (head + 1) * HEAD_SIZE)
                qraw_ref[at, cols] = raw
                qb_ref[at, cols] = turned.astype(bf16)
            else:
                kraw_ref[at, :] = raw
                kb_ref[at, :] = turned.astype(bf16)
        vb_ref[at, :] = rows[:, (heads + 1) * HEAD_SIZE :].astype(bf16)


def project(pieces, n, places, gain, pack, q_gain, k_gain, cosine, sine, heads):
    depth = pieces[0].shape[1]
    total = sum(p.shape[0] for p in pieces)
    rows = total // n
    const = lambda i, p: (0, 0)
    whole = lambda a: pl.BlockSpec(a.shape, const)
    shards = pack.shape[0]
    in_cols = (heads + 2) * HEAD_SIZE
    out = [
        jax.ShapeDtypeStruct((n, rows, depth), bf16),
        jax.ShapeDtypeStruct((total, heads * HEAD_SIZE), f32),
        jax.ShapeDtypeStruct((total, HEAD_SIZE), f32),
        jax.ShapeDtypeStruct((total, heads * HEAD_SIZE), bf16),
        jax.ShapeDtypeStruct((total, HEAD_SIZE), bf16),
        jax.ShapeDtypeStruct((total, HEAD_SIZE), bf16),
    ]
    args = (q_gain, k_gain, cosine, sine)
    return pl.pallas_call(
        functools.partial(project_kernel, len(pieces), heads),
        grid_spec=pltpu.PrefetchScalarGridSpec(
            num_scalar_prefetch=1,
            grid=(n,),
            in_specs=[any_spec() for _ in pieces]
            + [
                whole(gain),
                pl.BlockSpec((shards, depth // shards, in_cols), lambda i, p: (0, 0, 0)),
            ]
            + [whole(a) for a in args],
            out_specs=[pl.BlockSpec((1, rows, depth), lambda i, p: (i, 0, 0))]
            + [pl.BlockSpec(o.shape, const) for o in out[1:]],
            scratch_shapes=[
                pltpu.VMEM((n, rows, depth), bf16),
                pltpu.SemaphoreType.DMA((n,)),
            ],
        ),
        out_shape=out,
        compiler_params=pltpu.CompilerParams(
            dimension_semantics=("arbitrary",), vmem_limit_bytes=VMEM_LIMIT
        ),
        cost_estimate=cost_of(16.0 * total * heads / 4096),
        name="project",
    )(places, *pieces, gain, pack, *args)


def attend_kernel(
    heads, tile, length_ref, place_ref, index_ref, q_ref, k_ref, v_ref, o_ref, a_ref, ai_ref, lse_ref
):
    total = q_ref.shape[0]
    blk = total // place_ref.shape[0]
    scale = 1.0 / math.sqrt(HEAD_SIZE)
    length = length_ref[0]
    key_tiles = (length + tile - 1) // tile

    def q_step(i, unused):
        q_at = pl.ds(pl.multiple_of(i * tile, tile), tile)
        q = [q_ref[q_at, h * HEAD_SIZE : (h + 1) * HEAD_SIZE] for h in range(heads)]

        def tile_step(j, carry, masked):
            k_at = pl.ds(pl.multiple_of(j * tile, tile), tile)
            k, v = k_ref[k_at, :], v_ref[k_at, :]
            if masked:
                key = j * tile + lax.broadcasted_iota(jnp.int32, (tile, tile), 0)
                query = i * tile + lax.broadcasted_iota(jnp.int32, (tile, tile), 1)
                allowed = (key <= query) & (key < length)
            new = []
            for h in range(heads):
                top, tot, out = carry[h]
                s = dot_nt(k, q[h]) * scale
                if masked:
                    s = jnp.where(allowed, s, large_negative)
                top_new = jnp.maximum(top, jnp.max(s, axis=0, keepdims=True))
                shrink = jnp.exp(top - top_new)
                p = jnp.exp(s - top_new)
                tot = tot * shrink + jnp.sum(p, axis=0, keepdims=True)
                out = out * shrink + dot_tn(v, p.astype(bf16))
                new.append((top_new, tot, out))
            return tuple(new)

        start = tuple(
            (
                jnp.full((1, tile), large_negative, f32),
                jnp.zeros((1, tile), f32),
                jnp.zeros((HEAD_SIZE, tile), f32),
            )
            for _ in range(heads)
        )
        full = jnp.minimum(i, length // tile)
        carry = lax.fori_loop(0, full, functools.partial(tile_step, masked=False), start)
        carry = lax.fori_loop(
            full, jnp.minimum(i + 1, key_tiles), functools.partial(tile_step, masked=True), carry
        )
        for h in range(heads):
            top, tot, out = carry[h]
            lse_ref[pl.ds(h, 1), q_at] = top + jnp.log(tot)
            o = jnp.transpose(out / tot)
            cols = slice(h * HEAD_SIZE, (h + 1) * HEAD_SIZE)
            o_ref[q_at, cols] = o
        return unused

    lax.fori_loop(0, total // tile, q_step, 0)

    def place_step(b, unused):
        src = pl.ds(pl.multiple_of(place_ref[b] * blk, blk), blk)
        dst = pl.ds(pl.multiple_of(b * blk, blk), blk)
        a_ref[dst, :] = o_ref[src, :].astype(bf16)
        src = pl.ds(pl.multiple_of(index_ref[b] * blk, blk), blk)
        ai_ref[dst, :] = o_ref[src, :].astype(bf16)
        return unused

    lax.fori_loop(0, place_ref.shape[0], place_step, 0)


def attend(length, places, by_index, q, k, v, heads):
    total = q.shape[0]
    tile = min(512, total)
    vm = lambda: pl.BlockSpec(memory_space=pltpu.VMEM)
    sm = lambda: pl.BlockSpec(memory_space=pltpu.SMEM)
    return pl.pallas_call(
        functools.partial(attend_kernel, heads, tile),
        in_specs=[sm(), sm(), sm(), vm(), vm(), vm()],
        out_specs=[vm(), vm(), vm(), vm()],
        out_shape=[
            jax.ShapeDtypeStruct((total, heads * HEAD_SIZE), f32),
            jax.ShapeDtypeStruct((total, heads * HEAD_SIZE), bf16),
            jax.ShapeDtypeStruct((total, heads * HEAD_SIZE), bf16),
            jax.ShapeDtypeStruct((heads, total), f32),
        ],
        compiler_params=pltpu.CompilerParams(vmem_limit_bytes=VMEM_LIMIT),
        cost_estimate=cost_of(18.5 * total * heads / 4096),
        name="attend",
    )(length, places, by_index, q, k, v)


def unturn(grad, raw, gain, cosine, sine):
    grad = grad * cosine - pltpu.roll(grad, HEAD_SIZE // 2, 1) * sine
    scale = rms_scale(raw)
    hat = raw * scale
    inner = grad * gain
    out = scale * (inner - hat * jnp.mean(inner * hat, axis=-1, keepdims=True))
    return out, jnp.sum(grad * hat, axis=0, keepdims=True)


def attend_back_kernel(
    heads, tile, finish_keys, length_ref, place_ref, index_ref, q_ref, k_ref, v_ref, da_ref, o_ref,
    lse_ref, qraw_ref, kraw_ref, qg_ref, kg_ref, cos_ref, sin_ref,
    d_ref, dqg_ref, dkg_ref, *rest,
):
    if finish_keys:
        da_s, delta_s, dq_s, turned_s, dk_s, dv_s = rest
    else:
        dk_s, dv_s, da_s, delta_s, dq_s, turned_s = rest
    total = q_ref.shape[0]
    blocks = place_ref.shape[0]
    blk = total // blocks
    scale = 1.0 / math.sqrt(HEAD_SIZE)
    length = length_ref[0]
    tiles = total // tile

    def sort_step(b, unused):
        dst = pl.ds(pl.multiple_of(index_ref[b] * blk, blk), blk)
        src = pl.ds(pl.multiple_of(b * blk, blk), blk)
        piece = da_ref[src, :]
        da_s[dst, :] = piece
        prod = piece.astype(f32) * o_ref[dst, :]
        for h in range(heads):
            cols = slice(h * HEAD_SIZE, (h + 1) * HEAD_SIZE)
            delta_s[pl.ds(h, 1), dst] = jnp.sum(jnp.transpose(prod[:, cols]), axis=0, keepdims=True)
        return unused

    lax.fori_loop(0, blocks, sort_step, 0)
    dq_s[...] = jnp.zeros_like(dq_s)
    dk_s[...] = jnp.zeros_like(dk_s)
    dv_s[...] = jnp.zeros_like(dv_s)

    def k_step(j, unused):
        k_at = pl.ds(pl.multiple_of(j * tile, tile), tile)
        k, v = k_ref[k_at, :], v_ref[k_at, :]

        def tile_step(i, carry, masked):
            dk, dv = carry
            q_at = pl.ds(pl.multiple_of(i * tile, tile), tile)
            if masked:
                key = j * tile + lax.broadcasted_iota(jnp.int32, (tile, tile), 0)
                query = i * tile + lax.broadcasted_iota(jnp.int32, (tile, tile), 1)
                allowed = (key <= query) & (key < length)
            for h in range(heads):
                cols = slice(h * HEAD_SIZE, (h + 1) * HEAD_SIZE)
                q, da = q_ref[q_at, cols], da_s[q_at, cols]
                s = dot_nt(k, q) * scale - lse_ref[pl.ds(h, 1), q_at]
                if masked:
                    s = jnp.where(allowed, s, large_negative)
                p = jnp.exp(s)
                dp = dot_nt(v, da)
                ds = (p * (dp - delta_s[pl.ds(h, 1), q_at])).astype(bf16)
                dv = dv + dot_nn(p.astype(bf16), da)
                dk = dk + dot_nn(ds, q)
                dq_s[q_at, cols] += dot_tn(ds, k)
            return dk, dv

        zero = jnp.zeros((tile, HEAD_SIZE), f32)
        carry = (zero, zero)
        whole_tile = (j + 1) * tile <= length
        carry = lax.fori_loop(j, j + 1, functools.partial(tile_step, masked=True), carry)
        first_full = jnp.where(whole_tile, j + 1, tiles)
        carry = lax.fori_loop(
            j + 1, first_full, functools.partial(tile_step, masked=True), carry
        )
        carry = lax.fori_loop(first_full, tiles, functools.partial(tile_step, masked=False), carry)
        dk_s[k_at, :], dv_s[k_at, :] = carry[0] * scale, carry[1]
        return unused

    lax.fori_loop(0, (length + tile - 1) // tile, k_step, 0)

    dqg_ref[...] = jnp.zeros_like(dqg_ref)
    dkg_ref[...] = jnp.zeros_like(dkg_ref)

    def last_step(b, unused):
        src = pl.ds(pl.multiple_of(b * blk, blk), blk)
        cosine, sine = cos_ref[src, :], sin_ref[src, :]
        for h in range(heads):
            cols = slice(h * HEAD_SIZE, (h + 1) * HEAD_SIZE)
            grad = (dq_s[src, cols] * scale).astype(bf16).astype(f32)
            out, gain = unturn(grad, qraw_ref[src, cols], qg_ref[...], cosine, sine)
            turned_s[src, cols] = out.astype(bf16)
            dqg_ref[...] += gain
        if finish_keys:
            grad = dk_s[src, :].astype(bf16).astype(f32)
            out, gain = unturn(grad, kraw_ref[src, :], kg_ref[...], cosine, sine)
            turned_s[src, heads * HEAD_SIZE : (heads + 1) * HEAD_SIZE] = out.astype(bf16)
            dkg_ref[...] += gain
            turned_s[src, (heads + 1) * HEAD_SIZE :] = dv_s[src, :].astype(bf16)
        return unused

    lax.fori_loop(0, blocks, last_step, 0)

    def place_step(b, unused):
        dst = pl.ds(pl.multiple_of(b * blk, blk), blk)
        d_ref[dst, :] = turned_s[pl.ds(pl.multiple_of(place_ref[b] * blk, blk), blk), :]
        return unused

    lax.fori_loop(0, blocks, place_step, 0)


def attend_back(
    length, places, by_index, q, k, v, da, o, lse, qraw, kraw, qg, kg, cosine, sine, heads, finish_keys
):
    total = q.shape[0]
    tile = min(512, total)
    vm = lambda: pl.BlockSpec(memory_space=pltpu.VMEM)
    sm = lambda: pl.BlockSpec(memory_space=pltpu.SMEM)
    width = (heads + 2 if finish_keys else heads) * HEAD_SIZE
    sums = [jax.ShapeDtypeStruct((total, HEAD_SIZE), f32)] * 2
    out = [
        jax.ShapeDtypeStruct((total, width), bf16),
        jax.ShapeDtypeStruct((1, HEAD_SIZE), f32),
        jax.ShapeDtypeStruct((1, HEAD_SIZE), f32),
    ] + ([] if finish_keys else sums)
    scratch = [
        pltpu.VMEM((total, heads * HEAD_SIZE), bf16),
        pltpu.VMEM((heads, total), f32),
        pltpu.VMEM((total, heads * HEAD_SIZE), f32),
        pltpu.VMEM((total, width), bf16),
    ] + ([pltpu.VMEM(s.shape, s.dtype) for s in sums] if finish_keys else [])
    return pl.pallas_call(
        functools.partial(attend_back_kernel, heads, tile, finish_keys),
        in_specs=[sm(), sm(), sm()] + [vm() for _ in range(12)],
        out_specs=[vm() for _ in out],
        out_shape=out,
        scratch_shapes=scratch,
        compiler_params=pltpu.CompilerParams(vmem_limit_bytes=VMEM_LIMIT),
        cost_estimate=cost_of(33.0 * total * heads / 4096),
        name="attend_back",
    )(length, places, by_index, q, k, v, da, o, lse, qraw, kraw, qg, kg, cosine, sine)


def branch_kernel(order_ref, a_ref, wo_ref, x_ref, gain_ref, h1_ref, xn_ref, acc):
    step = pl.program_id(0)

    @pl.when(step == 0)
    def _():
        acc[...] = x_ref[...].astype(f32)

    acc[...] += dot_nt(a_ref[0], wo_ref[0])

    @pl.when(step == pl.num_programs(0) - 1)
    def _():
        h1 = acc[...]
        h1_ref[...] = h1
        xn_ref[...] = (h1 * rms_scale(h1) * gain_ref[...]).astype(bf16)


def branch(order, a_tok, wo_slots, x, gain):
    n, rows, q_cols = a_tok.shape
    depth = x.shape[1]
    const = lambda i, p: (0, 0)
    return pl.pallas_call(
        branch_kernel,
        grid_spec=pltpu.PrefetchScalarGridSpec(
            num_scalar_prefetch=1,
            grid=(n,),
            in_specs=[
                pl.BlockSpec((1, rows, q_cols), lambda i, p: (p[i], 0, 0)),
                pl.BlockSpec((1, depth, q_cols), lambda i, p: (i, 0, 0)),
                pl.BlockSpec((rows, depth), const),
                pl.BlockSpec((1, depth), const),
            ],
            out_specs=[pl.BlockSpec((rows, depth), const)] * 2,
            scratch_shapes=[pltpu.VMEM((rows, depth), f32)],
        ),
        out_shape=[
            jax.ShapeDtypeStruct((rows, depth), f32),
            jax.ShapeDtypeStruct((rows, depth), bf16),
        ],
        compiler_params=pltpu.CompilerParams(vmem_limit_bytes=VMEM_LIMIT),
        cost_estimate=cost_of(11.0),
        name="branch",
    )(order, a_tok, wo_slots, x, gain)


def branch_back_kernel(
    order_ref, dxn_ref, h1_ref, dy_ref, gain_ref, wo_ref, dh_ref, dz_ref, dg_ref, da_ref, dz_s
):
    @pl.when(pl.program_id(0) == 0)
    def _():
        h1, dxn = h1_ref[...], dxn_ref[...]
        scale = rms_scale(h1)
        hat = h1 * scale
        dg_ref[...] = jnp.sum(dxn * hat, axis=0, keepdims=True)
        e = dxn * gain_ref[...]
        dh = dy_ref[...].astype(f32) + scale * (e - hat * jnp.mean(e * hat, axis=-1, keepdims=True))
        dh_ref[...] = dh
        dz = dh.astype(bf16)
        dz_ref[...] = dz
        dz_s[...] = dz

    da_ref[0] = dot_nn(dz_s[...], wo_ref[0]).astype(bf16)


def branch_back(order, dxn, h1, dy, gain, wo_slots):
    n, depth, q_cols = wo_slots.shape
    rows = dxn.shape[0]
    const = lambda i, p: (0, 0)
    own = pl.BlockSpec((rows, depth), const)
    return pl.pallas_call(
        branch_back_kernel,
        grid_spec=pltpu.PrefetchScalarGridSpec(
            num_scalar_prefetch=1,
            grid=(n,),
            in_specs=[
                own, own, own, pl.BlockSpec((1, depth), const),
                pl.BlockSpec((1, depth, q_cols), lambda i, p: (i, 0, 0)),
            ],
            out_specs=[
                own, own, pl.BlockSpec((1, depth), const),
                pl.BlockSpec((1, rows, q_cols), lambda i, p: (p[i], 0, 0)),
            ],
            scratch_shapes=[pltpu.VMEM((rows, depth), bf16)],
        ),
        out_shape=[
            jax.ShapeDtypeStruct((rows, depth), f32),
            jax.ShapeDtypeStruct((rows, depth), bf16),
            jax.ShapeDtypeStruct((1, depth), f32),
            jax.ShapeDtypeStruct((n, rows, q_cols), bf16),
        ],
        compiler_params=pltpu.CompilerParams(vmem_limit_bytes=VMEM_LIMIT),
        cost_estimate=cost_of(13.0),
        name="branch_back",
    )(order, dxn, h1, dy, gain, wo_slots)


def feed_kernel(count, *refs):
    x_pieces, y_pieces = refs[:count], refs[count : 2 * count]
    w_ref, d_ref, hm_ref, x_all, y_all, x_sem, y_sem = refs[2 * count :]
    step = pl.program_id(0)
    _, rows, depth = x_all.shape
    ff = hm_ref.shape[2]

    @pl.when(step == 0)
    def _():
        for xc, yc in zip(
            piece_copies(x_pieces, x_all, x_sem, rows), piece_copies(y_pieces, y_all, y_sem, rows)
        ):
            xc.start()
            yc.start()

    for k in range(2):
        slot = 2 * step + k
        pltpu.make_async_copy(x_all.at[slot], x_all.at[slot], x_sem.at[slot]).wait()
    at = pl.ds(2 * step, 2)
    y = dot_nn(x_all[at].reshape(2 * rows, depth), w_ref[:, : 2 * ff])
    for k in range(2):
        slot = 2 * step + k
        pltpu.make_async_copy(y_all.at[slot], y_all.at[slot], y_sem.at[slot]).wait()
    dhm = dot_nn(y_all[at].reshape(2 * rows, depth), w_ref[:, 2 * ff :])
    g, u = y[:, :ff], y[:, ff:]
    sigma = jax.nn.sigmoid(g)
    silu = g * sigma
    hm_ref[...] = (silu * u).astype(bf16).reshape(2, rows, ff)
    d_ref[:, :, :ff] = (
        (dhm * u * sigma * (1.0 + g * (1.0 - sigma))).astype(bf16).reshape(2, rows, ff)
    )
    d_ref[:, :, ff:] = (dhm * silu).astype(bf16).reshape(2, rows, ff)


def feed(x_pieces, y_pieces, n, w):
    depth, ff = w.shape[0], w.shape[1] // 3
    total = sum(p.shape[0] for p in x_pieces)
    rows = total // n
    return pl.pallas_call(
        functools.partial(feed_kernel, len(x_pieces)),
        grid=(n // 2,),
        in_specs=[any_spec() for _ in x_pieces + y_pieces]
        + [pl.BlockSpec(w.shape, lambda i: (0, 0))],
        out_specs=[
            pl.BlockSpec((2, rows, 2 * ff), lambda i: (i, 0, 0)),
            pl.BlockSpec((2, rows, ff), lambda i: (i, 0, 0)),
        ],
        out_shape=[
            jax.ShapeDtypeStruct((n, rows, 2 * ff), bf16),
            jax.ShapeDtypeStruct((n, rows, ff), bf16),
        ],
        scratch_shapes=[
            pltpu.VMEM((n, rows, depth), bf16),
            pltpu.VMEM((n, rows, depth), bf16),
            pltpu.SemaphoreType.DMA((n,)),
            pltpu.SemaphoreType.DMA((n,)),
        ],
        compiler_params=pltpu.CompilerParams(vmem_limit_bytes=VMEM_LIMIT),
        cost_estimate=cost_of(17.0 * total * ff / (2048 * 384)),
        name="feed",
    )(*x_pieces, *y_pieces, w)


def per_device(
    n, n_fsdp, layer_input, dy, block_order, lengths, attn_gain, wq, wk, wv, q_gain, k_gain, wo,
    mlp_gain, wg, wu, wd,
):
    me = lax.axis_index("ctx")
    x, dy = layer_input[0], dy[0]
    rows, depth = x.shape
    total = n * rows
    shard = wq.shape[0]
    heads = QUERY_HEADS // n
    kv_share = max(n // KEY_VALUE_HEADS, 1)
    ff = wg.shape[1] // n
    q_cols = heads * HEAD_SIZE
    parts = 2 if ff % 256 == 0 else 1
    ff_part = ff // parts

    def cols(w, width, index):
        return lax.dynamic_slice_in_dim(w, index * width, width, axis=1)

    def whole(w):
        return lax.all_gather(w, "fsdp", axis=0, tiled=True)

    kv_index = me // kv_share
    w_in = jnp.concatenate(
        [cols(wq, q_cols, me), cols(wk, HEAD_SIZE, kv_index), cols(wv, HEAD_SIZE, kv_index)], axis=1
    )
    in_cols = w_in.shape[1]
    w_attn = jnp.concatenate([w_in, cols(wo, q_cols, me)], axis=1)
    width = w_attn.shape[1]
    gains = jnp.concatenate([attn_gain, mlp_gain])
    gain_rows = -(-gains.shape[0] // (16 * width)) * 16
    gains = jnp.pad(gains, (0, gain_rows * width - gains.shape[0])).reshape(gain_rows, width)
    pack = lax.all_gather(jnp.concatenate([w_attn, gains], axis=0), "fsdp", axis=0)
    w_in = pack[:, :shard, :in_cols].reshape(depth, in_cols)
    wo_c = pack[:, :shard, in_cols:].reshape(depth, q_cols)
    gains = pack[:, shard:].reshape(n_fsdp, -1)
    attn_gain = gains[:, :shard].reshape(1, depth).astype(f32)
    mlp_gain = gains[:, shard : 2 * shard].reshape(1, depth).astype(f32)
    x_pieces = gather_pieces(x, n)

    def feed_weights(part, gate):
        at = parts * me + part
        w = jnp.concatenate([cols(w, ff_part, at) for w in (wg, wu, wd)], axis=1)
        return whole(after(w, gate))

    w_ff = [feed_weights(0, x_pieces[0])]

    order = slot_order(n)
    by_index = block_order.reshape(-1)
    places = jnp.take(block_order, order, axis=0).reshape(-1)
    half = HEAD_SIZE // 2
    lane = jnp.arange(HEAD_SIZE, dtype=jnp.int32)
    frequency = jnp.exp(-math.log(rope_base) * 2.0 * (lane % half).astype(f32) / HEAD_SIZE)
    angle = jnp.arange(total, dtype=f32)[:, None] * frequency[None, :]
    cosine = jnp.cos(angle)
    sine = jnp.sin(angle) * jnp.where(lane < half, -1.0, 1.0)[None, :]
    qg = q_gain.astype(f32).reshape(1, HEAD_SIZE)
    kg = k_gain.astype(f32).reshape(1, HEAD_SIZE)

    xn, q_raw, k_raw, qb, kb, vb = project(
        x_pieces, n, places, attn_gain, pack, qg, kg, cosine, sine, heads
    )
    w_ff += [feed_weights(part, qb) for part in range(1, parts)]
    wo_pieces = gather_pieces(after(wo_c, x_pieces[-1]), n)
    wo_slots = assemble(wo_pieces, n)
    dy_pieces = gather_pieces(after(dy, wo_pieces[len(wo_pieces) // 2]), n)
    o, a, a_index, lse = attend(lengths, places, by_index, qb, kb, vb, heads)
    a_tok = exchange(a_index.reshape(n, rows, q_cols))
    a_tok = after(a_tok, dy_pieces[len(dy_pieces) // 2])
    h1, xn2 = branch(order, a_tok, wo_slots, x, mlp_gain)

    xn2_pieces = gather_pieces(xn2, n)
    d_gu, hm, grads = [], [], []
    for w in w_ff:
        if grads:
            xn2_pieces = [after(xn2_pieces[0], grads[-1])] + xn2_pieces[1:]
        d_part, hm_part = feed(xn2_pieces, dy_pieces, n, w)
        grads.append(
            weight_grad(
                [
                    (xn2_pieces, d_part.reshape(total, 2 * ff_part)),
                    (dy_pieces, hm_part.reshape(total, ff_part)),
                ],
                n, n_fsdp,
            )
        )
        d_gu.append(d_part)
        hm.append(hm_part)
    d_ff = [reduce_rows(grad, n) for grad in grads]
    d_xn2 = scatter_slots(d_gu, w_ff, 0, n)

    d_h1, dz, d_mlp_gain, da = branch_back(
        order, after(d_xn2, grads[-1]), h1, dy, mlp_gain, wo_slots
    )
    da = exchange(da).reshape(total, q_cols)
    m = scatter_slots([after(hm[0], d_h1)] + hm[1:], w_ff, 2, n)
    output = (h1 + m).astype(bf16)
    dz_pieces = gather_pieces(dz, n)
    d_qkv, d_qg, d_kg, *key_sums = attend_back(
        lengths, places, by_index, qb, kb, vb, da, o, lse, q_raw, k_raw, qg, kg, cosine, sine,
        heads, kv_share == 1,
    )
    if kv_share > 1:
        groups = [list(range(g, g + kv_share)) for g in range(0, n, kv_share)]
        first = (me % kv_share == 0).astype(f32)
        dk, dv = (
            lax.psum(t, "ctx", axis_index_groups=groups).astype(bf16).astype(f32) * first
            for t in key_sums
        )
        grad = dk * cosine - jnp.roll(dk, half, axis=1) * sine
        scale = rms_scale(k_raw)
        hat = k_raw * scale
        d_kg = jnp.sum(grad * hat, axis=0, keepdims=True)
        grad = grad * kg
        dk = scale * (grad - hat * jnp.mean(grad * hat, axis=-1, keepdims=True))
        d_kv = jnp.concatenate([dk, dv], axis=1).astype(bf16).reshape(2 * n, -1, 2 * HEAD_SIZE)
        d_qkv = jnp.concatenate([d_qkv, d_kv[places].reshape(total, -1)], axis=1)
    d_attn = weight_grad([([xn.reshape(total, depth)], d_qkv), (dz_pieces, a)], n, n_fsdp)
    d_xn = scatter_slots([d_qkv.reshape(n, rows, in_cols)], [w_in], 0, n)
    d_attn = reduce_rows(d_attn, n)
    x_float = x.astype(f32)
    scale_one = rms_scale(x_float)
    hat_one = x_float * scale_one
    d_attn_gain = jnp.sum(d_xn * hat_one, axis=0)
    e = d_xn * attn_gain
    dx = d_h1 + scale_one * (e - hat_one * jnp.mean(e * hat_one, axis=-1, keepdims=True))

    sums = sum_all(
        jnp.concatenate([d_attn_gain, d_mlp_gain[0], d_qg[0], d_kg[0]]).reshape(-1, HEAD_SIZE),
        n, n_fsdp,
    ).reshape(-1)
    d_ff = exchange(after(jnp.concatenate(d_ff, axis=2), d_qkv))
    d_attn = exchange(d_attn)
    starts = range(0, 3 * ff, 3 * ff_part)
    d_wg, d_wu, d_wd = join_columns(
        d_ff, [[(t + k * ff_part, t + (k + 1) * ff_part) for t in starts] for k in range(3)]
    )
    k_cols, v_cols = q_cols + HEAD_SIZE, q_cols + 2 * HEAD_SIZE
    d_wq, d_wo = join_columns(d_attn, [[(0, q_cols)], [(v_cols, v_cols + q_cols)]])
    d_wk, d_wv = join_columns(d_attn[::kv_share], [[(q_cols, k_cols)], [(k_cols, v_cols)]])
    return (
        output[None],
        dx[None],
        d_wq,
        d_wk,
        d_wv,
        d_wo,
        d_wg,
        d_wu,
        d_wd,
        sums[:depth],
        sums[depth : 2 * depth],
        sums[2 * depth : 2 * depth + HEAD_SIZE],
        sums[2 * depth + HEAD_SIZE :],
    )


def solution(mesh):
    n, n_fsdp = mesh.shape["ctx"], mesh.shape["fsdp"]
    row, act = P("fsdp", None), P("fsdp", "ctx", None)
    own = P(("ctx", "fsdp"), None)
    return jax.shard_map(
        functools.partial(per_device, n, n_fsdp),
        mesh=mesh,
        in_specs=(
            act, act, P(), P("fsdp"), P("fsdp"), row, row, row, P(), P(), row, P("fsdp"), row, row, row,
        ),
        out_specs=(act, act) + (own,) * 7 + (P(),) * 4,
        check_vma=False,
    )
```

```python
import functools
import math

import jax
import jax.numpy as jnp
from jax import lax
from jax.experimental import pallas as pl
from jax.experimental.pallas import tpu as pltpu
from jax.sharding import PartitionSpec as P

QUERY_HEADS = 16
KEY_VALUE_HEADS = 8
HEAD_SIZE = 128

epsilon = 1e-06
rope_base = 1000000.0
large_negative = -1e30

bf16 = jnp.bfloat16
f32 = jnp.float32
VMEM_LIMIT = 56 * 1024 * 1024


def cost_of(microseconds):
    return pl.CostEstimate(
        flops=int(microseconds * 1.1e9), bytes_accessed=1 << 20, transcendentals=0
    )


def dot_nn(left, right):
    return lax.dot_general(left, right, (((1,), (0,)), ((), ())), preferred_element_type=f32)


def dot_nt(left, right):
    return lax.dot_general(left, right, (((1,), (1,)), ((), ())), preferred_element_type=f32)


def dot_tn(left, right):
    return lax.dot_general(left, right, (((0,), (0,)), ((), ())), preferred_element_type=f32)


def rms_scale(values):
    return lax.rsqrt(jnp.mean(values * values, axis=-1, keepdims=True) + epsilon)


def swap(values, n, bits, axis="ctx"):
    return lax.ppermute(values, axis, [(c, c ^ bits) for c in range(n)])


def swap_first(values, n, first):
    return lax.ppermute(
        values, "ctx", [(c, c ^ (2 if (c % 2 == 0) == first else 4)) for c in range(n)]
    )


def slot_order(n):
    me = lax.axis_index("ctx")
    slots = jnp.arange(n, dtype=jnp.int32)
    if n == 8:
        even = jnp.array([0, 2, 4, 6, 1, 5, 3, 7], jnp.int32)
        odd = jnp.array([0, 4, 2, 6, 1, 3, 5, 7], jnp.int32)
        slots = jnp.where(me % 2 == 0, even, odd)
    return me ^ slots


def any_spec():
    return pl.BlockSpec(memory_space=pl.ANY)


def gather_pieces(rows, n, second=(), last=()):
    if n != 8:
        full = lax.all_gather(rows, "ctx", axis=0)
        return [jnp.take(full, slot_order(n), axis=0).reshape(-1, rows.shape[1])]
    pair = jnp.concatenate([rows, swap_first(rows, n, True)], axis=0)
    pair = after(pair, *second)
    other = after(swap_first(pair, n, False), *last)
    return [pair, other, swap(pair, n, 1), swap(other, n, 1)]


def piece_copies(pieces, out, sem, rows):
    copies, at = [], 0
    for piece in pieces:
        size = piece.shape[0]
        slot, start = at // rows, at % rows
        if size > rows:
            for k in range(size // rows):
                copies.append(
                    pltpu.make_async_copy(
                        piece.at[pl.ds(k * rows, rows)], out.at[slot + k], sem.at[slot + k]
                    )
                )
        else:
            copies.append(
                pltpu.make_async_copy(piece, out.at[slot, pl.ds(start, size)], sem.at[slot])
            )
        at += size
    return copies


def assemble_kernel(count, rows, *refs):
    out, held, sem, out_sem = refs[count:]
    for copy in piece_copies(refs[:count], held, sem, rows):
        copy.start()
    slots = range(out.shape[0])
    for slot in slots:
        pltpu.make_async_copy(held.at[slot], held.at[slot], sem.at[slot]).wait()
        pltpu.make_async_copy(held.at[slot], out.at[slot], out_sem.at[slot]).start()
    for slot in slots:
        pltpu.make_async_copy(held.at[slot], out.at[slot], out_sem.at[slot]).wait()


def assemble(pieces, n):
    total = sum(p.shape[0] for p in pieces)
    rows, width = total // n, pieces[0].shape[1]
    if len(pieces) == 1:
        return pieces[0].reshape(n, rows, width)
    return pl.pallas_call(
        functools.partial(assemble_kernel, len(pieces), rows),
        in_specs=[any_spec() for _ in pieces],
        out_specs=any_spec(),
        out_shape=jax.ShapeDtypeStruct((n, rows, width), pieces[0].dtype),
        scratch_shapes=[
            pltpu.VMEM((n, rows, width), pieces[0].dtype),
            pltpu.SemaphoreType.DMA((n,)),
            pltpu.SemaphoreType.DMA((n,)),
        ],
        compiler_params=pltpu.CompilerParams(vmem_limit_bytes=VMEM_LIMIT),
        cost_estimate=cost_of(0.3 * 6.0 * total * width / 2**22),
        name="assemble",
    )(*pieces)


def mm_kernel(count, *refs):
    total = dot_nt(refs[0][0], refs[count][...])
    for k in range(1, count):
        total = total + dot_nt(refs[k][0], refs[count + k][...])
    refs[2 * count][0] = total.astype(bf16)


def mm_slots(lefts, ws, column, start, count):
    rows = lefts[0].shape[1]
    width = ws[0].shape[0]
    depths = [left.shape[2] for left in lefts]
    return pl.pallas_call(
        functools.partial(mm_kernel, len(lefts)),
        grid=(count,),
        in_specs=[pl.BlockSpec((1, rows, d), lambda i: (i + start, 0, 0)) for d in depths]
        + [pl.BlockSpec((width, d), lambda i: (0, column)) for d in depths],
        out_specs=pl.BlockSpec((1, rows, width), lambda i: (i, 0, 0)),
        out_shape=jax.ShapeDtypeStruct((count, rows, width), bf16),
        compiler_params=pltpu.CompilerParams(vmem_limit_bytes=VMEM_LIMIT),
        cost_estimate=cost_of(3.5 + 8.0 * count * rows * sum(depths) * width / (1024 * 1536 * 2048)),
        name="mm_slots",
    )(*lefts, *ws)


def add_kernel(mine_ref, got_ref, send_ref, keep_ref):
    half = send_ref.shape[0]
    for i in range(half):
        keep_ref[i] = mine_ref[i].astype(f32) + got_ref[i].astype(f32)
        send_ref[i] = (mine_ref[half + i].astype(f32) + got_ref[half + i].astype(f32)).astype(bf16)


def add_halves(mine, got):
    slots, rows, width = mine.shape
    half, tile = slots // 2, min(width, 512)
    read = pl.BlockSpec((slots, rows, tile), lambda i: (0, 0, i))
    write = pl.BlockSpec((half, rows, tile), lambda i: (0, 0, i))
    return pl.pallas_call(
        add_kernel,
        grid=(width // tile,),
        in_specs=[read, read],
        out_specs=[write, write],
        out_shape=[
            jax.ShapeDtypeStruct((half, rows, width), bf16),
            jax.ShapeDtypeStruct((half, rows, width), f32),
        ],
        compiler_params=pltpu.CompilerParams(vmem_limit_bytes=VMEM_LIMIT),
        cost_estimate=cost_of(6.5 * slots * rows * width / 2**21),
        name="add_halves",
    )(mine, got)


def scatter_far(lefts, ws, column, n):
    if n != 8:
        index = jnp.argsort(slot_order(n))
        return jnp.take(mm_slots(lefts, ws, column, 0, n), index, axis=0)
    return swap(mm_slots(lefts, ws, column, 4, 4), n, 1)


def scatter_near(got, near):
    if near is None:
        return got, got
    return add_halves(near, got)


def near_product(lefts, ws, column, n):
    return mm_slots(lefts, ws, column, 0, 4) if n == 8 else None


def scatter_last(send, keep, n):
    if n != 8:
        return lax.psum_scatter(send, "ctx", scatter_dimension=0, tiled=True)[0].astype(f32)
    got = swap_first(send, n, False)
    last = (keep[1] + got[1].astype(f32)).astype(bf16)
    return keep[0] + got[0].astype(f32) + swap_first(last, n, True).astype(f32)


def exchange(blocks):
    return lax.all_to_all(blocks, "ctx", 0, 0, tiled=True)


def weight_kernel(counts, gained, *refs):
    if gained:
        refs, w_ref, gain_ref, dg_ref = refs[:-4] + refs[-2:-1], refs[-4], refs[-3], refs[-1]
    refs, out_ref = refs[:-1], refs[-1]
    tops, at = [], 0
    for count in counts:
        left = jnp.concatenate([r[...] for r in refs[at : at + count]], axis=0)
        tops.append(dot_tn(left, refs[at + count][...]))
        at += count + 1
    if gained:
        dg_ref[...] = jnp.sum(tops[0] * w_ref[...].astype(f32), axis=1, keepdims=True) / gain_ref[...]
    shards, _, rows, width = out_ref.shape
    out_ref[...] = jnp.concatenate(tops, axis=1).astype(bf16).reshape(shards, 1, rows, width)


def weight_grad(pairs, n, n_fsdp, w=None, gain=None):
    depth = pairs[0][0][0].shape[1]
    rows, tile = depth // (n * n_fsdp), depth // n
    width = sum(right.shape[1] for _, right in pairs)
    total = pairs[0][1].shape[0]
    specs, args = [], []
    for pieces, right in pairs:
        specs += [pl.BlockSpec((p.shape[0], tile), lambda j: (0, j)) for p in pieces]
        specs.append(pl.BlockSpec(right.shape, lambda j: (0, 0)))
        args += [*pieces, right]
    out_specs = [pl.BlockSpec((n_fsdp, 1, rows, width), lambda j: (0, j, 0, 0))]
    out_shape = [jax.ShapeDtypeStruct((n_fsdp, n, rows, width), bf16)]
    if w is not None:
        column = pl.BlockSpec((tile, 1), lambda j: (j, 0))
        specs += [pl.BlockSpec((tile, w.shape[1]), lambda j: (j, 0)), column]
        args += [w, gain]
        out_specs.append(column)
        out_shape.append(jax.ShapeDtypeStruct((depth, 1), f32))
    out = pl.pallas_call(
        functools.partial(weight_kernel, [len(pieces) for pieces, _ in pairs], w is not None),
        grid=(n,),
        in_specs=specs,
        out_specs=out_specs,
        out_shape=out_shape,
        compiler_params=pltpu.CompilerParams(vmem_limit_bytes=VMEM_LIMIT),
        cost_estimate=cost_of(0.3 * 16.0 * total * depth * width / (2048 * 2048 * 1152)),
        name="weight_grad",
    )(*args)
    return [out[0].reshape(depth, width)] + list(out[1:])


def reduce_rows(grad, n):
    summed = lax.psum_scatter(grad, "fsdp", scatter_dimension=0, tiled=True)
    return summed.reshape(n, -1, grad.shape[1])


def join_kernel(count, parts, *refs):
    for out_ref, slices in zip(refs[count:], parts):
        out_ref[...] = jnp.concatenate(
            [refs[k][0, :, lo:hi].astype(f32) for k, lo, hi in slices], axis=1
        )


def join_columns(gots, parts):
    n, rows, _ = gots[0].shape
    sizes = [sum(hi - lo for _, lo, hi in slices) for slices in parts]
    return pl.pallas_call(
        functools.partial(join_kernel, len(gots), parts),
        grid=(n,),
        in_specs=[pl.BlockSpec((1, rows, got.shape[2]), lambda i: (i, 0, 0)) for got in gots],
        out_specs=[pl.BlockSpec((rows, size), lambda i: (0, i)) for size in sizes],
        out_shape=[jax.ShapeDtypeStruct((rows, n * size), f32) for size in sizes],
        cost_estimate=cost_of(5.0),
        name="join_columns",
    )(*gots)


def sum_all(values, n, n_fsdp):
    bits = 1
    while bits < n:
        values = values + swap(values, n, bits)
        bits *= 2
    bits = 1
    while bits < n_fsdp:
        values = values + swap(values, n_fsdp, bits, "fsdp")
        bits *= 2
    return values


def after(values, *others):
    return lax.optimization_barrier((values,) + others)[0]


def project_kernel(count, heads, place_ref, *refs):
    pieces, refs = refs[:count], refs[count:]
    gain_ref, w_ref, qg_ref, kg_ref, cos_ref, sin_ref = refs[:6]
    xn_ref, qraw_ref, kraw_ref, qb_ref, kb_ref, vb_ref, x_all, sem = refs[6:]
    slot = pl.program_id(0)

    @pl.when(slot == 0)
    def _():
        for copy in piece_copies(pieces, x_all, sem, x_all.shape[1]):
            copy.start()

    pltpu.make_async_copy(x_all.at[slot], x_all.at[slot], sem.at[slot]).wait()
    x = x_all[slot].astype(f32)
    xn = (x * rms_scale(x) * gain_ref[...]).astype(bf16)
    xn_ref[0] = xn
    w = w_ref[...].reshape(x.shape[1], w_ref.shape[2])
    y = jnp.dot(xn, w, preferred_element_type=f32)
    blk = x.shape[0] // 2
    for half in range(2):
        place = place_ref[2 * slot + half]
        at = pl.ds(pl.multiple_of(place * blk, blk), blk)
        cosine, sine = cos_ref[at, :], sin_ref[at, :]
        rows = y[half * blk : (half + 1) * blk]
        for head in range(heads + 1):
            raw = rows[:, head * HEAD_SIZE : (head + 1) * HEAD_SIZE]
            gain = (qg_ref if head < heads else kg_ref)[...]
            normed = raw * rms_scale(raw) * gain
            turned = normed * cosine + pltpu.roll(normed, HEAD_SIZE // 2, 1) * sine
            if head < heads:
                cols = slice(head * HEAD_SIZE, (head + 1) * HEAD_SIZE)
                qraw_ref[at, cols] = raw
                qb_ref[at, cols] = turned.astype(bf16)
            else:
                kraw_ref[at, :] = raw
                kb_ref[at, :] = turned.astype(bf16)
        vb_ref[at, :] = rows[:, (heads + 1) * HEAD_SIZE :].astype(bf16)


def project(pieces, n, places, gain, pack, q_gain, k_gain, cosine, sine, heads):
    depth = pieces[0].shape[1]
    total = sum(p.shape[0] for p in pieces)
    rows = total // n
    const = lambda i, p: (0, 0)
    whole = lambda a: pl.BlockSpec(a.shape, const)
    shards = pack.shape[0]
    in_cols = (heads + 2) * HEAD_SIZE
    out = [
        jax.ShapeDtypeStruct((n, rows, depth), bf16),
        jax.ShapeDtypeStruct((total, heads * HEAD_SIZE), f32),
        jax.ShapeDtypeStruct((total, HEAD_SIZE), f32),
        jax.ShapeDtypeStruct((total, heads * HEAD_SIZE), bf16),
        jax.ShapeDtypeStruct((total, HEAD_SIZE), bf16),
        jax.ShapeDtypeStruct((total, HEAD_SIZE), bf16),
    ]
    args = (q_gain, k_gain, cosine, sine)
    return pl.pallas_call(
        functools.partial(project_kernel, len(pieces), heads),
        grid_spec=pltpu.PrefetchScalarGridSpec(
            num_scalar_prefetch=1,
            grid=(n,),
            in_specs=[any_spec() for _ in pieces]
            + [
                whole(gain),
                pl.BlockSpec((shards, depth // shards, in_cols), lambda i, p: (0, 0, 0)),
            ]
            + [whole(a) for a in args],
            out_specs=[pl.BlockSpec((1, rows, depth), lambda i, p: (i, 0, 0))]
            + [pl.BlockSpec(o.shape, const) for o in out[1:]],
            scratch_shapes=[
                pltpu.VMEM((n, rows, depth), bf16),
                pltpu.SemaphoreType.DMA((n,)),
            ],
        ),
        out_shape=out,
        compiler_params=pltpu.CompilerParams(
            dimension_semantics=("arbitrary",), vmem_limit_bytes=VMEM_LIMIT
        ),
        cost_estimate=cost_of(0.3 * 16.0 * total * heads / 4096),
        name="project",
    )(places, *pieces, gain, pack, *args)


def attend_kernel(
    heads, tile, length_ref, place_ref, index_ref, q_ref, k_ref, v_ref, o_ref, a_ref, ai_ref, lse_ref
):
    total = q_ref.shape[0]
    blk = total // place_ref.shape[0]
    scale = 1.0 / math.sqrt(HEAD_SIZE)
    length = length_ref[0]
    key_tiles = (length + tile - 1) // tile

    def q_step(i, unused):
        q_at = pl.ds(pl.multiple_of(i * tile, tile), tile)
        q = [q_ref[q_at, h * HEAD_SIZE : (h + 1) * HEAD_SIZE] for h in range(heads)]

        def tile_step(j, carry, masked):
            k_at = pl.ds(pl.multiple_of(j * tile, tile), tile)
            k, v = k_ref[k_at, :], v_ref[k_at, :]
            if masked:
                key = j * tile + lax.broadcasted_iota(jnp.int32, (tile, tile), 0)
                query = i * tile + lax.broadcasted_iota(jnp.int32, (tile, tile), 1)
                allowed = (key <= query) & (key < length)
            new = []
            for h in range(heads):
                top, tot, out = carry[h]
                s = dot_nt(k, q[h]) * scale
                if masked:
                    s = jnp.where(allowed, s, large_negative)
                top_new = jnp.maximum(top, jnp.max(s, axis=0, keepdims=True))
                shrink = jnp.exp(top - top_new)
                p = jnp.exp(s - top_new)
                tot = tot * shrink + jnp.sum(p, axis=0, keepdims=True)
                out = out * shrink + dot_tn(v, p.astype(bf16))
                new.append((top_new, tot, out))
            return tuple(new)

        start = tuple(
            (
                jnp.full((1, tile), large_negative, f32),
                jnp.zeros((1, tile), f32),
                jnp.zeros((HEAD_SIZE, tile), f32),
            )
            for _ in range(heads)
        )
        full = jnp.minimum(i, length // tile)
        carry = lax.fori_loop(0, full, functools.partial(tile_step, masked=False), start)
        carry = lax.fori_loop(
            full, jnp.minimum(i + 1, key_tiles), functools.partial(tile_step, masked=True), carry
        )
        for h in range(heads):
            top, tot, out = carry[h]
            lse_ref[pl.ds(h, 1), q_at] = top + jnp.log(tot)
            o = jnp.transpose(out / tot)
            cols = slice(h * HEAD_SIZE, (h + 1) * HEAD_SIZE)
            o_ref[q_at, cols] = o
        return unused

    lax.fori_loop(0, total // tile, q_step, 0)

    def place_step(b, unused):
        src = pl.ds(pl.multiple_of(place_ref[b] * blk, blk), blk)
        dst = pl.ds(pl.multiple_of(b * blk, blk), blk)
        a_ref[dst, :] = o_ref[src, :].astype(bf16)
        src = pl.ds(pl.multiple_of(index_ref[b] * blk, blk), blk)
        ai_ref[dst, :] = o_ref[src, :].astype(bf16)
        return unused

    lax.fori_loop(0, place_ref.shape[0], place_step, 0)


def attend(length, places, by_index, q, k, v, heads):
    total = q.shape[0]
    tile = min(512, total)
    vm = lambda: pl.BlockSpec(memory_space=pltpu.VMEM)
    sm = lambda: pl.BlockSpec(memory_space=pltpu.SMEM)
    return pl.pallas_call(
        functools.partial(attend_kernel, heads, tile),
        in_specs=[sm(), sm(), sm(), vm(), vm(), vm()],
        out_specs=[vm(), vm(), vm(), vm()],
        out_shape=[
            jax.ShapeDtypeStruct((total, heads * HEAD_SIZE), f32),
            jax.ShapeDtypeStruct((total, heads * HEAD_SIZE), bf16),
            jax.ShapeDtypeStruct((total, heads * HEAD_SIZE), bf16),
            jax.ShapeDtypeStruct((heads, total), f32),
        ],
        compiler_params=pltpu.CompilerParams(vmem_limit_bytes=VMEM_LIMIT),
        cost_estimate=cost_of(0.3 * 18.5 * total * heads / 4096),
        name="attend",
    )(length, places, by_index, q, k, v)


def unturn(grad, raw, gain, cosine, sine):
    grad = grad * cosine - pltpu.roll(grad, HEAD_SIZE // 2, 1) * sine
    scale = rms_scale(raw)
    hat = raw * scale
    inner = grad * gain
    out = scale * (inner - hat * jnp.mean(inner * hat, axis=-1, keepdims=True))
    return out, jnp.sum(grad * hat, axis=0, keepdims=True)


def attend_back_kernel(
    heads, tile, finish_keys, length_ref, place_ref, index_ref, q_ref, k_ref, v_ref, da_ref, o_ref,
    lse_ref, qraw_ref, kraw_ref, qg_ref, kg_ref, cos_ref, sin_ref,
    d_ref, dqg_ref, dkg_ref, *rest,
):
    if finish_keys:
        da_s, delta_s, dq_s, turned_s, dk_s, dv_s = rest
    else:
        dk_s, dv_s, da_s, delta_s, dq_s, turned_s = rest
    total = q_ref.shape[0]
    blocks = place_ref.shape[0]
    blk = total // blocks
    scale = 1.0 / math.sqrt(HEAD_SIZE)
    length = length_ref[0]
    tiles = total // tile

    def sort_step(b, unused):
        dst = pl.ds(pl.multiple_of(index_ref[b] * blk, blk), blk)
        src = pl.ds(pl.multiple_of(b * blk, blk), blk)
        piece = da_ref[src, :]
        da_s[dst, :] = piece
        prod = piece.astype(f32) * o_ref[dst, :]
        for h in range(heads):
            cols = slice(h * HEAD_SIZE, (h + 1) * HEAD_SIZE)
            delta_s[pl.ds(h, 1), dst] = jnp.sum(jnp.transpose(prod[:, cols]), axis=0, keepdims=True)
        return unused

    lax.fori_loop(0, blocks, sort_step, 0)
    dq_s[...] = jnp.zeros_like(dq_s)
    dk_s[...] = jnp.zeros_like(dk_s)
    dv_s[...] = jnp.zeros_like(dv_s)

    def k_step(j, unused):
        k_at = pl.ds(pl.multiple_of(j * tile, tile), tile)
        k, v = k_ref[k_at, :], v_ref[k_at, :]

        def tile_step(i, carry, masked):
            dk, dv = carry
            q_at = pl.ds(pl.multiple_of(i * tile, tile), tile)
            if masked:
                key = j * tile + lax.broadcasted_iota(jnp.int32, (tile, tile), 0)
                query = i * tile + lax.broadcasted_iota(jnp.int32, (tile, tile), 1)
                allowed = (key <= query) & (key < length)
            for h in range(heads):
                cols = slice(h * HEAD_SIZE, (h + 1) * HEAD_SIZE)
                q, da = q_ref[q_at, cols], da_s[q_at, cols]
                s = dot_nt(k, q) * scale - lse_ref[pl.ds(h, 1), q_at]
                if masked:
                    s = jnp.where(allowed, s, large_negative)
                p = jnp.exp(s)
                dp = dot_nt(v, da)
                ds = (p * (dp - delta_s[pl.ds(h, 1), q_at])).astype(bf16)
                dv = dv + dot_nn(p.astype(bf16), da)
                dk = dk + dot_nn(ds, q)
                dq_s[q_at, cols] += dot_tn(ds, k)
            return dk, dv

        zero = jnp.zeros((tile, HEAD_SIZE), f32)
        carry = (zero, zero)
        whole_tile = (j + 1) * tile <= length
        carry = lax.fori_loop(j, j + 1, functools.partial(tile_step, masked=True), carry)
        first_full = jnp.where(whole_tile, j + 1, tiles)
        carry = lax.fori_loop(
            j + 1, first_full, functools.partial(tile_step, masked=True), carry
        )
        carry = lax.fori_loop(first_full, tiles, functools.partial(tile_step, masked=False), carry)
        dk_s[k_at, :], dv_s[k_at, :] = carry[0] * scale, carry[1]
        return unused

    lax.fori_loop(0, (length + tile - 1) // tile, k_step, 0)

    dqg_ref[...] = jnp.zeros_like(dqg_ref)
    dkg_ref[...] = jnp.zeros_like(dkg_ref)

    def last_step(b, unused):
        src = pl.ds(pl.multiple_of(b * blk, blk), blk)
        cosine, sine = cos_ref[src, :], sin_ref[src, :]
        for h in range(heads):
            cols = slice(h * HEAD_SIZE, (h + 1) * HEAD_SIZE)
            grad = (dq_s[src, cols] * scale).astype(bf16).astype(f32)
            out, gain = unturn(grad, qraw_ref[src, cols], qg_ref[...], cosine, sine)
            turned_s[src, cols] = out.astype(bf16)
            dqg_ref[...] += gain
        if finish_keys:
            grad = dk_s[src, :].astype(bf16).astype(f32)
            out, gain = unturn(grad, kraw_ref[src, :], kg_ref[...], cosine, sine)
            turned_s[src, heads * HEAD_SIZE : (heads + 1) * HEAD_SIZE] = out.astype(bf16)
            dkg_ref[...] += gain
            turned_s[src, (heads + 1) * HEAD_SIZE :] = dv_s[src, :].astype(bf16)
        return unused

    lax.fori_loop(0, blocks, last_step, 0)

    def place_step(b, unused):
        dst = pl.ds(pl.multiple_of(b * blk, blk), blk)
        d_ref[dst, :] = turned_s[pl.ds(pl.multiple_of(place_ref[b] * blk, blk), blk), :]
        return unused

    lax.fori_loop(0, blocks, place_step, 0)


def attend_back(
    length, places, by_index, q, k, v, da, o, lse, qraw, kraw, qg, kg, cosine, sine, heads, finish_keys
):
    total = q.shape[0]
    tile = min(512, total)
    vm = lambda: pl.BlockSpec(memory_space=pltpu.VMEM)
    sm = lambda: pl.BlockSpec(memory_space=pltpu.SMEM)
    width = (heads + 2 if finish_keys else heads) * HEAD_SIZE
    sums = [jax.ShapeDtypeStruct((total, HEAD_SIZE), f32)] * 2
    out = [
        jax.ShapeDtypeStruct((total, width), bf16),
        jax.ShapeDtypeStruct((1, HEAD_SIZE), f32),
        jax.ShapeDtypeStruct((1, HEAD_SIZE), f32),
    ] + ([] if finish_keys else sums)
    scratch = [
        pltpu.VMEM((total, heads * HEAD_SIZE), bf16),
        pltpu.VMEM((heads, total), f32),
        pltpu.VMEM((total, heads * HEAD_SIZE), f32),
        pltpu.VMEM((total, width), bf16),
    ] + ([pltpu.VMEM(s.shape, s.dtype) for s in sums] if finish_keys else [])
    return pl.pallas_call(
        functools.partial(attend_back_kernel, heads, tile, finish_keys),
        in_specs=[sm(), sm(), sm()] + [vm() for _ in range(12)],
        out_specs=[vm() for _ in out],
        out_shape=out,
        scratch_shapes=scratch,
        compiler_params=pltpu.CompilerParams(vmem_limit_bytes=VMEM_LIMIT),
        cost_estimate=cost_of(33.0 * total * heads / 4096),
        name="attend_back",
    )(length, places, by_index, q, k, v, da, o, lse, qraw, kraw, qg, kg, cosine, sine)


def branch_kernel(order_ref, a_ref, wo_ref, x_ref, gain_ref, h1_ref, xn_ref, acc):
    step = pl.program_id(0)

    @pl.when(step == 0)
    def _():
        acc[...] = x_ref[...].astype(f32)

    acc[...] += dot_nt(a_ref[0], wo_ref[0])

    @pl.when(step == pl.num_programs(0) - 1)
    def _():
        h1 = acc[...]
        h1_ref[...] = h1
        xn_ref[...] = (h1 * rms_scale(h1) * gain_ref[...]).astype(bf16)


def branch(order, a_tok, wo_slots, x, gain):
    n, rows, q_cols = a_tok.shape
    depth = x.shape[1]
    const = lambda i, p: (0, 0)
    return pl.pallas_call(
        branch_kernel,
        grid_spec=pltpu.PrefetchScalarGridSpec(
            num_scalar_prefetch=1,
            grid=(n,),
            in_specs=[
                pl.BlockSpec((1, rows, q_cols), lambda i, p: (p[i], 0, 0)),
                pl.BlockSpec((1, depth, q_cols), lambda i, p: (i, 0, 0)),
                pl.BlockSpec((rows, depth), const),
                pl.BlockSpec((1, depth), const),
            ],
            out_specs=[pl.BlockSpec((rows, depth), const)] * 2,
            scratch_shapes=[pltpu.VMEM((rows, depth), f32)],
        ),
        out_shape=[
            jax.ShapeDtypeStruct((rows, depth), f32),
            jax.ShapeDtypeStruct((rows, depth), bf16),
        ],
        compiler_params=pltpu.CompilerParams(vmem_limit_bytes=VMEM_LIMIT),
        cost_estimate=cost_of(0.3 * 11.0),
        name="branch",
    )(order, a_tok, wo_slots, x, gain)


def branch_back_kernel(
    order_ref, dxn_ref, h1_ref, dy_ref, gain_ref, wo_ref, dh_ref, dz_ref, dg_ref, da_ref, dz_s
):
    @pl.when(pl.program_id(0) == 0)
    def _():
        h1, dxn = h1_ref[...], dxn_ref[...]
        scale = rms_scale(h1)
        hat = h1 * scale
        dg_ref[...] = jnp.sum(dxn * hat, axis=0, keepdims=True)
        e = dxn * gain_ref[...]
        dh = dy_ref[...].astype(f32) + scale * (e - hat * jnp.mean(e * hat, axis=-1, keepdims=True))
        dh_ref[...] = dh
        dz = dh.astype(bf16)
        dz_ref[...] = dz
        dz_s[...] = dz

    da_ref[0] = dot_nn(dz_s[...], wo_ref[0]).astype(bf16)


def branch_back(order, dxn, h1, dy, gain, wo_slots):
    n, depth, q_cols = wo_slots.shape
    rows = dxn.shape[0]
    const = lambda i, p: (0, 0)
    own = pl.BlockSpec((rows, depth), const)
    return pl.pallas_call(
        branch_back_kernel,
        grid_spec=pltpu.PrefetchScalarGridSpec(
            num_scalar_prefetch=1,
            grid=(n,),
            in_specs=[
                own, own, own, pl.BlockSpec((1, depth), const),
                pl.BlockSpec((1, depth, q_cols), lambda i, p: (i, 0, 0)),
            ],
            out_specs=[
                own, own, pl.BlockSpec((1, depth), const),
                pl.BlockSpec((1, rows, q_cols), lambda i, p: (p[i], 0, 0)),
            ],
            scratch_shapes=[pltpu.VMEM((rows, depth), bf16)],
        ),
        out_shape=[
            jax.ShapeDtypeStruct((rows, depth), f32),
            jax.ShapeDtypeStruct((rows, depth), bf16),
            jax.ShapeDtypeStruct((1, depth), f32),
            jax.ShapeDtypeStruct((n, rows, q_cols), bf16),
        ],
        compiler_params=pltpu.CompilerParams(vmem_limit_bytes=VMEM_LIMIT),
        cost_estimate=cost_of(13.0),
        name="branch_back",
    )(order, dxn, h1, dy, gain, wo_slots)


def feed_kernel(count, *refs):
    x_pieces, y_pieces = refs[:count], refs[count : 2 * count]
    w_ref, d_ref, hm_ref, x_all, y_all, x_sem, y_sem = refs[2 * count :]
    step = pl.program_id(0)
    _, rows, depth = x_all.shape
    ff = hm_ref.shape[2]

    @pl.when(step == 0)
    def _():
        for xc, yc in zip(
            piece_copies(x_pieces, x_all, x_sem, rows), piece_copies(y_pieces, y_all, y_sem, rows)
        ):
            xc.start()
            yc.start()

    for k in range(2):
        slot = 2 * step + k
        pltpu.make_async_copy(x_all.at[slot], x_all.at[slot], x_sem.at[slot]).wait()
    at = pl.ds(2 * step, 2)
    y = dot_nn(x_all[at].reshape(2 * rows, depth), w_ref[:, : 2 * ff])
    for k in range(2):
        slot = 2 * step + k
        pltpu.make_async_copy(y_all.at[slot], y_all.at[slot], y_sem.at[slot]).wait()
    dhm = dot_nn(y_all[at].reshape(2 * rows, depth), w_ref[:, 2 * ff :])
    g, u = y[:, :ff], y[:, ff:]
    sigma = jax.nn.sigmoid(g)
    silu = g * sigma
    hm_ref[...] = (silu * u).astype(bf16).reshape(2, rows, ff)
    d_ref[:, :, :ff] = (
        (dhm * u * sigma * (1.0 + g * (1.0 - sigma))).astype(bf16).reshape(2, rows, ff)
    )
    d_ref[:, :, ff:] = (dhm * silu).astype(bf16).reshape(2, rows, ff)


def feed(x_pieces, y_pieces, n, w):
    depth, ff = w.shape[0], w.shape[1] // 3
    total = sum(p.shape[0] for p in x_pieces)
    rows = total // n
    return pl.pallas_call(
        functools.partial(feed_kernel, len(x_pieces)),
        grid=(n // 2,),
        in_specs=[any_spec() for _ in x_pieces + y_pieces]
        + [pl.BlockSpec(w.shape, lambda i: (0, 0))],
        out_specs=[
            pl.BlockSpec((2, rows, 2 * ff), lambda i: (i, 0, 0)),
            pl.BlockSpec((2, rows, ff), lambda i: (i, 0, 0)),
        ],
        out_shape=[
            jax.ShapeDtypeStruct((n, rows, 2 * ff), bf16),
            jax.ShapeDtypeStruct((n, rows, ff), bf16),
        ],
        scratch_shapes=[
            pltpu.VMEM((n, rows, depth), bf16),
            pltpu.VMEM((n, rows, depth), bf16),
            pltpu.SemaphoreType.DMA((n,)),
            pltpu.SemaphoreType.DMA((n,)),
        ],
        compiler_params=pltpu.CompilerParams(vmem_limit_bytes=VMEM_LIMIT),
        cost_estimate=cost_of(0.3 * 17.0 * total * ff / (2048 * 384)),
        name="feed",
    )(*x_pieces, *y_pieces, w)


def per_device(
    n, n_fsdp, layer_input, dy, block_order, lengths, attn_gain, wq, wk, wv, q_gain, k_gain, wo,
    mlp_gain, wg, wu, wd,
):
    me = lax.axis_index("ctx")
    x, dy = layer_input[0], dy[0]
    rows, depth = x.shape
    total = n * rows
    shard = wq.shape[0]
    heads = QUERY_HEADS // n
    kv_share = max(n // KEY_VALUE_HEADS, 1)
    ff = wg.shape[1] // n
    q_cols = heads * HEAD_SIZE
    parts = 2 if ff % 256 == 0 else 1
    ff_part = ff // parts

    def cols(w, width, index):
        return lax.dynamic_slice_in_dim(w, index * width, width, axis=1)

    def whole(w):
        return lax.all_gather(w, "fsdp", axis=0, tiled=True)

    kv_index = me // kv_share
    w_in = jnp.concatenate(
        [cols(wq, q_cols, me), cols(wk, HEAD_SIZE, kv_index), cols(wv, HEAD_SIZE, kv_index)], axis=1
    )
    in_cols = w_in.shape[1]
    w_attn = jnp.concatenate([w_in, cols(wo, q_cols, me)], axis=1)
    width = w_attn.shape[1]
    gains = jnp.concatenate([attn_gain, mlp_gain])
    gain_rows = -(-gains.shape[0] // (16 * width)) * 16
    gains = jnp.pad(gains, (0, gain_rows * width - gains.shape[0])).reshape(gain_rows, width)
    pack = lax.all_gather(jnp.concatenate([w_attn, gains], axis=0), "fsdp", axis=0)
    x_pieces = gather_pieces(x, n)

    def feed_weights(part, gate):
        at = parts * me + part
        w = jnp.concatenate([cols(w, ff_part, at) for w in (wg, wu, wd)], axis=1)
        return whole(after(w, gate))

    w_ff = [feed_weights(0, x_pieces[0])]
    dy_pieces = gather_pieces(after(dy, x_pieces[0]), n, [x_pieces[len(x_pieces) // 4]])
    pack = after(pack, dy_pieces[0])
    w_in = pack[:, :shard, :in_cols].reshape(depth, in_cols)
    wo_c = pack[:, :shard, in_cols:].reshape(depth, q_cols)
    gains = pack[:, shard:].reshape(n_fsdp, -1)
    attn_gain = gains[:, :shard].reshape(1, depth).astype(f32)
    mlp_gain = gains[:, shard : 2 * shard].reshape(1, depth).astype(f32)

    order = slot_order(n)
    by_index = block_order.reshape(-1)
    places = jnp.take(block_order, order, axis=0).reshape(-1)
    half = HEAD_SIZE // 2
    lane = jnp.arange(HEAD_SIZE, dtype=jnp.int32)
    frequency = jnp.exp(-math.log(rope_base) * 2.0 * (lane % half).astype(f32) / HEAD_SIZE)
    angle = jnp.arange(total, dtype=f32)[:, None] * frequency[None, :]
    cosine = jnp.cos(angle)
    sine = jnp.sin(angle) * jnp.where(lane < half, -1.0, 1.0)[None, :]
    qg = q_gain.astype(f32).reshape(1, HEAD_SIZE)
    kg = k_gain.astype(f32).reshape(1, HEAD_SIZE)

    xn, q_raw, k_raw, qb, kb, vb = project(
        x_pieces, n, places, attn_gain, pack, qg, kg, cosine, sine, heads
    )
    w_ff += [feed_weights(part, qb) for part in range(1, parts)]
    o, a, a_index, lse = attend(
        lengths, places, by_index, after(qb, dy_pieces[len(dy_pieces) // 4]), kb, vb, heads
    )
    a_tok = exchange(a_index.reshape(n, rows, q_cols))
    wo_slots = assemble(gather_pieces(wo_c, n, [qb], [a_index]), n)
    h1, xn2 = branch(order, a_tok, wo_slots, x, mlp_gain)

    xn2_pieces = gather_pieces(xn2, n)
    d_gu, hm, grads = [], [], []

    def ff_grad(d_part, hm_part):
        return weight_grad(
            [
                (xn2_pieces, d_part.reshape(total, 2 * ff_part)),
                (dy_pieces, hm_part.reshape(total, ff_part)),
            ],
            n, n_fsdp,
        )

    for w in w_ff:
        if d_gu:
            grads += ff_grad(d_gu[-1], hm[-1])
            xn2_pieces = [after(xn2_pieces[0], grads[-1])] + xn2_pieces[1:]
        d_part, hm_part = feed(xn2_pieces, dy_pieces, n, w)
        d_gu.append(d_part)
        hm.append(hm_part)
    got = scatter_far(d_gu, w_ff, 0, n)
    send, keep = scatter_near(got, near_product(d_gu, w_ff, 0, n))
    grads += ff_grad(after(d_gu[-1], send), hm[-1])
    d_ff = [reduce_rows(grad, n) for grad in grads]
    hm = [after(hm[0], grads[-1])] + hm[1:]
    m_got = scatter_far(hm, w_ff, 2, n)
    m_near = near_product(hm, w_ff, 2, n)
    d_xn2 = scatter_last(send, keep, n)

    d_h1, dz, d_mlp_gain, da = branch_back(
        order, after(d_xn2, grads[-1], m_got if m_near is None else m_near), h1, dy, mlp_gain, wo_slots
    )
    da = exchange(da).reshape(total, q_cols)
    m_send, m_keep = scatter_near(after(m_got, d_h1), m_near)
    dz_pieces = gather_pieces(dz, n)
    da = after(da, dz_pieces[0])
    m = scatter_last(after(m_send, dz_pieces[len(dz_pieces) // 2]), m_keep, n)
    output = (h1 + m).astype(bf16)
    d_ff[0] = exchange(after(d_ff[0], da))
    d_qkv, d_qg, d_kg, *key_sums = attend_back(
        lengths, places, by_index, qb, kb, vb, da, o, lse, q_raw, k_raw, qg, kg, cosine, sine,
        heads, kv_share == 1,
    )
    if kv_share > 1:
        groups = [list(range(g, g + kv_share)) for g in range(0, n, kv_share)]
        first = (me % kv_share == 0).astype(f32)
        dk, dv = (
            lax.psum(t, "ctx", axis_index_groups=groups).astype(bf16).astype(f32) * first
            for t in key_sums
        )
        grad = dk * cosine - jnp.roll(dk, half, axis=1) * sine
        scale = rms_scale(k_raw)
        hat = k_raw * scale
        d_kg = jnp.sum(grad * hat, axis=0, keepdims=True)
        grad = grad * kg
        dk = scale * (grad - hat * jnp.mean(grad * hat, axis=-1, keepdims=True))
        d_kv = jnp.concatenate([dk, dv], axis=1).astype(bf16).reshape(2 * n, -1, 2 * HEAD_SIZE)
        d_qkv = jnp.concatenate([d_qkv, d_kv[places].reshape(total, -1)], axis=1)
    d_attn, d_attn_gain = weight_grad(
        [([xn.reshape(total, depth)], d_qkv), (dz_pieces, a)], n, n_fsdp, w_in,
        attn_gain.reshape(depth, 1),
    )
    d_attn = reduce_rows(d_attn, n)
    left = [after(d_qkv, d_ff[0]).reshape(n, rows, in_cols)]
    got = scatter_far(left, [w_in], 0, n)
    d_xn = scatter_last(*scatter_near(got, near_product(left, [w_in], 0, n)), n)
    x_float = x.astype(f32)
    scale_one = rms_scale(x_float)
    hat_one = x_float * scale_one
    e = d_xn * attn_gain
    dx = d_h1 + scale_one * (e - hat_one * jnp.mean(e * hat_one, axis=-1, keepdims=True))

    sums = sum_all(
        jnp.concatenate([d_attn_gain[:, 0], d_mlp_gain[0], d_qg[0], d_kg[0]]).reshape(-1, HEAD_SIZE),
        n, n_fsdp,
    ).reshape(-1)
    d_ff = d_ff[:1] + [exchange(d) for d in d_ff[1:]]
    d_attn = exchange(d_attn)
    d_wg, d_wu, d_wd = join_columns(
        d_ff,
        [[(p, k * ff_part, (k + 1) * ff_part) for p in range(parts)] for k in range(3)],
    )
    k_cols, v_cols = q_cols + HEAD_SIZE, q_cols + 2 * HEAD_SIZE
    kv_parts = [[(0, q_cols, k_cols)], [(0, k_cols, v_cols)]]
    d_wq, d_wo, *d_kv = join_columns(
        [d_attn],
        [[(0, 0, q_cols)], [(0, v_cols, v_cols + q_cols)]] + (kv_parts if kv_share == 1 else []),
    )
    d_wk, d_wv = d_kv or join_columns([d_attn[::kv_share]], kv_parts)
    return (
        output[None],
        dx[None],
        d_wq,
        d_wk,
        d_wv,
        d_wo,
        d_wg,
        d_wu,
        d_wd,
        sums[:depth],
        sums[depth : 2 * depth],
        sums[2 * depth : 2 * depth + HEAD_SIZE],
        sums[2 * depth + HEAD_SIZE :],
    )


def solution(mesh):
    n, n_fsdp = mesh.shape["ctx"], mesh.shape["fsdp"]
    row, act = P("fsdp", None), P("fsdp", "ctx", None)
    own = P(("ctx", "fsdp"), None)
    return jax.shard_map(
        functools.partial(per_device, n, n_fsdp),
        mesh=mesh,
        in_specs=(
            act, act, P(), P("fsdp"), P("fsdp"), row, row, row, P(), P(), row, P("fsdp"), row, row, row,
        ),
        out_specs=(act, act) + (own,) * 7 + (P(),) * 4,
        check_vma=False,
    )
```

```python
import functools
import math

import jax
import jax.numpy as jnp
from jax import lax
from jax.experimental import pallas as pl
from jax.experimental.pallas import tpu as pltpu
from jax.sharding import PartitionSpec as P

QUERY_HEADS = 16
KEY_VALUE_HEADS = 8
HEAD_SIZE = 128

epsilon = 1e-06
rope_base = 1000000.0
large_negative = -1e30

bf16 = jnp.bfloat16
f32 = jnp.float32
VMEM_LIMIT = 56 * 1024 * 1024


def cost_of(microseconds):
    return pl.CostEstimate(
        flops=int(microseconds * 1.1e9), bytes_accessed=1 << 20, transcendentals=0
    )


def dot_nn(left, right):
    return lax.dot_general(left, right, (((1,), (0,)), ((), ())), preferred_element_type=f32)


def dot_nt(left, right):
    return lax.dot_general(left, right, (((1,), (1,)), ((), ())), preferred_element_type=f32)


def dot_tn(left, right):
    return lax.dot_general(left, right, (((0,), (0,)), ((), ())), preferred_element_type=f32)


def rms_scale(values):
    return lax.rsqrt(jnp.mean(values * values, axis=-1, keepdims=True) + epsilon)


def swap(values, n, bits, axis="ctx"):
    return lax.ppermute(values, axis, [(c, c ^ bits) for c in range(n)])


def swap_first(values, n, first):
    return lax.ppermute(
        values, "ctx", [(c, c ^ (2 if (c % 2 == 0) == first else 4)) for c in range(n)]
    )


def slot_order(n):
    me = lax.axis_index("ctx")
    slots = jnp.arange(n, dtype=jnp.int32)
    if n == 8:
        even = jnp.array([0, 2, 4, 6, 1, 5, 3, 7], jnp.int32)
        odd = jnp.array([0, 4, 2, 6, 1, 3, 5, 7], jnp.int32)
        slots = jnp.where(me % 2 == 0, even, odd)
    return me ^ slots


def any_spec():
    return pl.BlockSpec(memory_space=pl.ANY)


def gather_pair(rows, n, gates=()):
    if n != 8:
        return rows
    return jnp.concatenate([after(rows, *gates), swap_first(rows, n, True)], axis=0)


def gather_rest(pair, n, second=(), last=(), other=None):
    if n != 8:
        full = lax.all_gather(pair, "ctx", axis=0)
        return [jnp.take(full, slot_order(n), axis=0).reshape(-1, pair.shape[1])]
    pair = after(pair, *second)
    if other is None:
        other = swap_first(pair, n, False)
    return [pair, after(other, *last), swap(pair, n, 1), swap(after(other, *last), n, 1)]


def piece_copies(pieces, out, sem, rows):
    copies, at = [], 0
    for piece in pieces:
        size = piece.shape[0]
        slot, start = at // rows, at % rows
        if size > rows:
            for k in range(size // rows):
                copies.append(
                    pltpu.make_async_copy(
                        piece.at[pl.ds(k * rows, rows)], out.at[slot + k], sem.at[slot + k]
                    )
                )
        else:
            copies.append(
                pltpu.make_async_copy(piece, out.at[slot, pl.ds(start, size)], sem.at[slot])
            )
        at += size
    return copies


def assemble_kernel(count, rows, *refs):
    out, held, sem, out_sem = refs[count:]
    for copy in piece_copies(refs[:count], held, sem, rows):
        copy.start()
    slots = range(out.shape[0])
    for slot in slots:
        pltpu.make_async_copy(held.at[slot], held.at[slot], sem.at[slot]).wait()
        pltpu.make_async_copy(held.at[slot], out.at[slot], out_sem.at[slot]).start()
    for slot in slots:
        pltpu.make_async_copy(held.at[slot], out.at[slot], out_sem.at[slot]).wait()


def assemble(pieces, n):
    total = sum(p.shape[0] for p in pieces)
    rows, width = total // n, pieces[0].shape[1]
    if len(pieces) == 1:
        return pieces[0].reshape(n, rows, width)
    return pl.pallas_call(
        functools.partial(assemble_kernel, len(pieces), rows),
        in_specs=[any_spec() for _ in pieces],
        out_specs=any_spec(),
        out_shape=jax.ShapeDtypeStruct((n, rows, width), pieces[0].dtype),
        scratch_shapes=[
            pltpu.VMEM((n, rows, width), pieces[0].dtype),
            pltpu.SemaphoreType.DMA((n,)),
            pltpu.SemaphoreType.DMA((n,)),
        ],
        compiler_params=pltpu.CompilerParams(vmem_limit_bytes=VMEM_LIMIT),
        cost_estimate=cost_of(0.3 * 6.0 * total * width / 2**22),
        name="assemble",
    )(*pieces)


def mm_kernel(count, added, *refs):
    out_refs = refs[2 * count + added :]
    slots, rows = refs[0].shape[:2]
    tile = out_refs[0].shape[2]
    total = None
    for k in range(count):
        left = refs[k][...].reshape(slots * rows, refs[k].shape[2])
        term = dot_nt(left, refs[count + k][...])
        total = term if total is None else total + term
    total = total.reshape(slots, rows, tile)
    if added:
        total = total + refs[2 * count][...].astype(f32)
    at = 0
    for out_ref in out_refs:
        out_ref[...] = total[at : at + out_ref.shape[0]].astype(out_ref.dtype)
        at += out_ref.shape[0]


def mm_slots(lefts, ws, column, start, count, add=None, dtypes=(bf16,), cover=1.0):
    rows = lefts[0].shape[1]
    width = ws[0].shape[0]
    tile = min(width, 512)
    depths = [left.shape[2] for left in lefts]
    each = count // len(dtypes)
    return pl.pallas_call(
        functools.partial(mm_kernel, len(lefts), int(add is not None)),
        grid=(width // tile,),
        in_specs=[
            pl.BlockSpec((count, rows, d), lambda j: (start // count, 0, 0)) for d in depths
        ]
        + [pl.BlockSpec((tile, d), lambda j: (j, column)) for d in depths]
        + ([] if add is None else [pl.BlockSpec((count, rows, tile), lambda j: (0, 0, j))]),
        out_specs=[pl.BlockSpec((each, rows, tile), lambda j: (0, 0, j)) for _ in dtypes],
        out_shape=[jax.ShapeDtypeStruct((each, rows, width), d) for d in dtypes],
        compiler_params=pltpu.CompilerParams(vmem_limit_bytes=VMEM_LIMIT),
        cost_estimate=cost_of(cover * (2.0 + 8.0 * count * rows * sum(depths) * width / (1024 * 1536 * 2048))),
        name="mm_slots",
    )(*lefts, *ws, *([] if add is None else [add]))


class SumScatter:
    def __init__(self, lefts, ws, column, n, halves=False, cover=1.0):
        self.n, self.args, self.halves, self.cover = n, (ws, column), halves, cover
        if n != 8:
            (part,) = mm_slots(lefts, ws, column, 0, n)
            self.far = self.send = jnp.take(part, jnp.argsort(slot_order(n)), axis=0)
        elif halves:
            self.far = [mm_slots(lefts, ws, column, at, 2)[0] for at in (6, 4)]
            self.got = [swap(far, n, 1) for far in self.far]
        else:
            (self.far,) = mm_slots(lefts, ws, column, 4, 4, cover=cover)
            self.got = swap(self.far, n, 1)

    def add_send(self, lefts):
        if self.n == 8 and self.halves:
            (self.send,) = mm_slots(lefts, *self.args, 2, 2, self.got[0])
        elif self.n == 8:
            self.keep, self.send = mm_slots(
                lefts, *self.args, 0, 4, self.got, (f32, bf16), self.cover
            )
        return self.send

    def add_keep(self, lefts):
        if self.n == 8:
            (self.keep,) = mm_slots(lefts, *self.args, 0, 2, self.got[1], (f32,))

    def step(self, *gates):
        if self.n == 8:
            self.got = swap_first(after(self.send, *gates), self.n, False)

    def second(self, *gates, held=None, stepped=False):
        if self.n == 8:
            if held is not None:
                self.keep = after(self.keep, held)
            if not stepped:
                self.step(*gates)
            got = self.got
            self.last = (self.keep[1] + got[1].astype(f32)).astype(bf16)
            self.part = self.keep[0] + got[0].astype(f32)
            return self.last
        self.last = self.send
        return self.last

    def result(self):
        if self.n == 8:
            return self.part + swap_first(self.last, self.n, True).astype(f32)
        return lax.psum_scatter(self.send, "ctx", scatter_dimension=0, tiled=True)[0].astype(f32)


def exchange(blocks):
    return lax.all_to_all(blocks, "ctx", 0, 0, tiled=True)


def weight_kernel(counts, gained, *refs):
    if gained:
        refs, w_ref, gain_ref, dg_ref = refs[:-4] + refs[-2:-1], refs[-4], refs[-3], refs[-1]
    refs, out_ref = refs[:-1], refs[-1]
    tops, at = [], 0
    for count in counts:
        left = jnp.concatenate([r[...] for r in refs[at : at + count]], axis=0)
        tops.append(dot_tn(left, refs[at + count][...]))
        at += count + 1
    if gained:
        dg_ref[...] = jnp.sum(tops[0] * w_ref[...].astype(f32), axis=1, keepdims=True) / gain_ref[...]
    shards, _, rows, width = out_ref.shape
    out_ref[...] = jnp.concatenate(tops, axis=1).astype(bf16).reshape(shards, 1, rows, width)


def weight_grad(pairs, n, n_fsdp, w=None, gain=None, cover=1.0):
    depth = pairs[0][0][0].shape[1]
    rows, tile = depth // (n * n_fsdp), depth // n
    width = sum(right.shape[1] for _, right in pairs)
    total = pairs[0][1].shape[0]
    specs, args = [], []
    for pieces, right in pairs:
        specs += [pl.BlockSpec((p.shape[0], tile), lambda j: (0, j)) for p in pieces]
        specs.append(pl.BlockSpec(right.shape, lambda j: (0, 0)))
        args += [*pieces, right]
    out_specs = [pl.BlockSpec((n_fsdp, 1, rows, width), lambda j: (0, j, 0, 0))]
    out_shape = [jax.ShapeDtypeStruct((n_fsdp, n, rows, width), bf16)]
    if w is not None:
        column = pl.BlockSpec((tile, 1), lambda j: (j, 0))
        specs += [pl.BlockSpec((tile, w.shape[1]), lambda j: (j, 0)), column]
        args += [w, gain]
        out_specs.append(column)
        out_shape.append(jax.ShapeDtypeStruct((depth, 1), f32))
    out = pl.pallas_call(
        functools.partial(weight_kernel, [len(pieces) for pieces, _ in pairs], w is not None),
        grid=(n,),
        in_specs=specs,
        out_specs=out_specs,
        out_shape=out_shape,
        compiler_params=pltpu.CompilerParams(vmem_limit_bytes=VMEM_LIMIT),
        cost_estimate=cost_of(cover * 16.0 * total * depth * width / (2048 * 2048 * 1152)),
        name="weight_grad",
    )(*args)
    return [out[0].reshape(depth, width)] + list(out[1:])


def reduce_rows(grad, n):
    summed = lax.psum_scatter(grad, "fsdp", scatter_dimension=0, tiled=True)
    return summed.reshape(n, -1, grad.shape[1])


def join_kernel(count, parts, *refs):
    for out_ref, slices in zip(refs[count:], parts):
        out_ref[...] = jnp.concatenate(
            [refs[k][0, :, lo:hi].astype(f32) for k, lo, hi in slices], axis=1
        )


def join_columns(gots, parts):
    n, rows, _ = gots[0].shape
    sizes = [sum(hi - lo for _, lo, hi in slices) for slices in parts]
    return pl.pallas_call(
        functools.partial(join_kernel, len(gots), parts),
        grid=(n,),
        in_specs=[pl.BlockSpec((1, rows, got.shape[2]), lambda i: (i, 0, 0)) for got in gots],
        out_specs=[pl.BlockSpec((rows, size), lambda i: (0, i)) for size in sizes],
        out_shape=[jax.ShapeDtypeStruct((rows, n * size), f32) for size in sizes],
        cost_estimate=cost_of(1.0),
        name="join_columns",
    )(*gots)


def sum_across(values, size, bits, axis):
    while bits < size:
        values = values + swap(values, size, bits, axis)
        bits *= 2
    return values


def after(values, *others):
    return lax.optimization_barrier((values,) + others)[0]


def project_kernel(count, heads, place_ref, *refs):
    pieces, refs = refs[:count], refs[count:]
    gain_ref, w_ref, qg_ref, kg_ref, cos_ref, sin_ref = refs[:6]
    xn_ref, qraw_ref, kraw_ref, qb_ref, kb_ref, vb_ref, x_all, sem = refs[6:]
    slot = pl.program_id(0)

    @pl.when(slot == 0)
    def _():
        for copy in piece_copies(pieces, x_all, sem, x_all.shape[1]):
            copy.start()

    pltpu.make_async_copy(x_all.at[slot], x_all.at[slot], sem.at[slot]).wait()
    x = x_all[slot].astype(f32)
    xn = (x * rms_scale(x) * gain_ref[...]).astype(bf16)
    xn_ref[0] = xn
    w = w_ref[...].reshape(x.shape[1], w_ref.shape[2])
    y = jnp.dot(xn, w, preferred_element_type=f32)
    blk = x.shape[0] // 2
    for half in range(2):
        place = place_ref[2 * slot + half]
        at = pl.ds(pl.multiple_of(place * blk, blk), blk)
        cosine, sine = cos_ref[at, :], sin_ref[at, :]
        rows = y[half * blk : (half + 1) * blk]
        for head in range(heads + 1):
            raw = rows[:, head * HEAD_SIZE : (head + 1) * HEAD_SIZE]
            gain = (qg_ref if head < heads else kg_ref)[...]
            normed = raw * rms_scale(raw) * gain
            turned = normed * cosine + pltpu.roll(normed, HEAD_SIZE // 2, 1) * sine
            if head < heads:
                cols = slice(head * HEAD_SIZE, (head + 1) * HEAD_SIZE)
                qraw_ref[at, cols] = raw
                qb_ref[at, cols] = turned.astype(bf16)
            else:
                kraw_ref[at, :] = raw
                kb_ref[at, :] = turned.astype(bf16)
        vb_ref[at, :] = rows[:, (heads + 1) * HEAD_SIZE :].astype(bf16)


def project(pieces, n, places, gain, pack, q_gain, k_gain, cosine, sine, heads):
    depth = pieces[0].shape[1]
    total = sum(p.shape[0] for p in pieces)
    rows = total // n
    const = lambda i, p: (0, 0)
    whole = lambda a: pl.BlockSpec(a.shape, const)
    shards = pack.shape[0]
    in_cols = (heads + 2) * HEAD_SIZE
    out = [
        jax.ShapeDtypeStruct((n, rows, depth), bf16),
        jax.ShapeDtypeStruct((total, heads * HEAD_SIZE), f32),
        jax.ShapeDtypeStruct((total, HEAD_SIZE), f32),
        jax.ShapeDtypeStruct((total, heads * HEAD_SIZE), bf16),
        jax.ShapeDtypeStruct((total, HEAD_SIZE), bf16),
        jax.ShapeDtypeStruct((total, HEAD_SIZE), bf16),
    ]
    args = (q_gain, k_gain, cosine, sine)
    return pl.pallas_call(
        functools.partial(project_kernel, len(pieces), heads),
        grid_spec=pltpu.PrefetchScalarGridSpec(
            num_scalar_prefetch=1,
            grid=(n,),
            in_specs=[any_spec() for _ in pieces]
            + [
                whole(gain),
                pl.BlockSpec((shards, depth // shards, in_cols), lambda i, p: (0, 0, 0)),
            ]
            + [whole(a) for a in args],
            out_specs=[pl.BlockSpec((1, rows, depth), lambda i, p: (i, 0, 0))]
            + [pl.BlockSpec(o.shape, const) for o in out[1:]],
            scratch_shapes=[
                pltpu.VMEM((n, rows, depth), bf16),
                pltpu.SemaphoreType.DMA((n,)),
            ],
        ),
        out_shape=out,
        compiler_params=pltpu.CompilerParams(
            dimension_semantics=("arbitrary",), vmem_limit_bytes=VMEM_LIMIT
        ),
        cost_estimate=cost_of(0.3 * 16.0 * total * heads / 4096),
        name="project",
    )(places, *pieces, gain, pack, *args)


def attend_kernel(
    heads, tile, length_ref, place_ref, index_ref, q_ref, k_ref, v_ref, o_ref, a_ref, ai_ref, lse_ref
):
    total = q_ref.shape[0]
    blk = total // place_ref.shape[0]
    scale = 1.0 / math.sqrt(HEAD_SIZE)
    length = length_ref[0]
    key_tiles = (length + tile - 1) // tile

    def q_step(i, unused):
        q_at = pl.ds(pl.multiple_of(i * tile, tile), tile)
        q = [q_ref[q_at, h * HEAD_SIZE : (h + 1) * HEAD_SIZE] for h in range(heads)]

        def tile_step(j, carry, masked):
            k_at = pl.ds(pl.multiple_of(j * tile, tile), tile)
            k, v = k_ref[k_at, :], v_ref[k_at, :]
            if masked:
                key = j * tile + lax.broadcasted_iota(jnp.int32, (tile, tile), 0)
                query = i * tile + lax.broadcasted_iota(jnp.int32, (tile, tile), 1)
                allowed = (key <= query) & (key < length)
            new = []
            for h in range(heads):
                top, tot, out = carry[h]
                s = dot_nt(k, q[h]) * scale
                if masked:
                    s = jnp.where(allowed, s, large_negative)
                top_new = jnp.maximum(top, jnp.max(s, axis=0, keepdims=True))
                shrink = jnp.exp(top - top_new)
                p = jnp.exp(s - top_new)
                tot = tot * shrink + jnp.sum(p, axis=0, keepdims=True)
                out = out * shrink + dot_tn(v, p.astype(bf16))
                new.append((top_new, tot, out))
            return tuple(new)

        start = tuple(
            (
                jnp.full((1, tile), large_negative, f32),
                jnp.zeros((1, tile), f32),
                jnp.zeros((HEAD_SIZE, tile), f32),
            )
            for _ in range(heads)
        )
        full = jnp.minimum(i, length // tile)
        carry = lax.fori_loop(0, full, functools.partial(tile_step, masked=False), start)
        carry = lax.fori_loop(
            full, jnp.minimum(i + 1, key_tiles), functools.partial(tile_step, masked=True), carry
        )
        for h in range(heads):
            top, tot, out = carry[h]
            lse_ref[pl.ds(h, 1), q_at] = top + jnp.log(tot)
            o = jnp.transpose(out / tot)
            cols = slice(h * HEAD_SIZE, (h + 1) * HEAD_SIZE)
            o_ref[q_at, cols] = o
        return unused

    lax.fori_loop(0, total // tile, q_step, 0)

    def place_step(b, unused):
        src = pl.ds(pl.multiple_of(place_ref[b] * blk, blk), blk)
        dst = pl.ds(pl.multiple_of(b * blk, blk), blk)
        a_ref[dst, :] = o_ref[src, :].astype(bf16)
        src = pl.ds(pl.multiple_of(index_ref[b] * blk, blk), blk)
        ai_ref[dst, :] = o_ref[src, :].astype(bf16)
        return unused

    lax.fori_loop(0, place_ref.shape[0], place_step, 0)


def attend(length, places, by_index, q, k, v, heads):
    total = q.shape[0]
    tile = min(512, total)
    vm = lambda: pl.BlockSpec(memory_space=pltpu.VMEM)
    sm = lambda: pl.BlockSpec(memory_space=pltpu.SMEM)
    return pl.pallas_call(
        functools.partial(attend_kernel, heads, tile),
        in_specs=[sm(), sm(), sm(), vm(), vm(), vm()],
        out_specs=[vm(), vm(), vm(), vm()],
        out_shape=[
            jax.ShapeDtypeStruct((total, heads * HEAD_SIZE), f32),
            jax.ShapeDtypeStruct((total, heads * HEAD_SIZE), bf16),
            jax.ShapeDtypeStruct((total, heads * HEAD_SIZE), bf16),
            jax.ShapeDtypeStruct((heads, total), f32),
        ],
        compiler_params=pltpu.CompilerParams(vmem_limit_bytes=VMEM_LIMIT),
        cost_estimate=cost_of(0.3 * 18.5 * total * heads / 4096),
        name="attend",
    )(length, places, by_index, q, k, v)


def unturn(grad, raw, gain, cosine, sine):
    grad = grad * cosine - pltpu.roll(grad, HEAD_SIZE // 2, 1) * sine
    scale = rms_scale(raw)
    hat = raw * scale
    inner = grad * gain
    out = scale * (inner - hat * jnp.mean(inner * hat, axis=-1, keepdims=True))
    return out, jnp.sum(grad * hat, axis=0, keepdims=True)


def attend_back_kernel(
    heads, tile, finish_keys, length_ref, place_ref, index_ref, q_ref, k_ref, v_ref, da_ref, o_ref,
    lse_ref, qraw_ref, kraw_ref, qg_ref, kg_ref, cos_ref, sin_ref,
    d_ref, dqg_ref, dkg_ref, *rest,
):
    if finish_keys:
        da_s, delta_s, dq_s, turned_s, dk_s, dv_s = rest
    else:
        dk_s, dv_s, da_s, delta_s, dq_s, turned_s = rest
    total = q_ref.shape[0]
    blocks = place_ref.shape[0]
    blk = total // blocks
    scale = 1.0 / math.sqrt(HEAD_SIZE)
    length = length_ref[0]
    tiles = total // tile

    def sort_step(b, unused):
        dst = pl.ds(pl.multiple_of(index_ref[b] * blk, blk), blk)
        src = pl.ds(pl.multiple_of(b * blk, blk), blk)
        piece = da_ref[src, :]
        da_s[dst, :] = piece
        prod = piece.astype(f32) * o_ref[dst, :]
        for h in range(heads):
            cols = slice(h * HEAD_SIZE, (h + 1) * HEAD_SIZE)
            delta_s[pl.ds(h, 1), dst] = jnp.sum(jnp.transpose(prod[:, cols]), axis=0, keepdims=True)
        return unused

    lax.fori_loop(0, blocks, sort_step, 0)
    dq_s[...] = jnp.zeros_like(dq_s)
    dk_s[...] = jnp.zeros_like(dk_s)
    dv_s[...] = jnp.zeros_like(dv_s)

    def k_step(j, unused):
        k_at = pl.ds(pl.multiple_of(j * tile, tile), tile)
        k, v = k_ref[k_at, :], v_ref[k_at, :]

        def tile_step(i, carry, masked):
            dk, dv = carry
            q_at = pl.ds(pl.multiple_of(i * tile, tile), tile)
            if masked:
                key = j * tile + lax.broadcasted_iota(jnp.int32, (tile, tile), 0)
                query = i * tile + lax.broadcasted_iota(jnp.int32, (tile, tile), 1)
                allowed = (key <= query) & (key < length)
            for h in range(heads):
                cols = slice(h * HEAD_SIZE, (h + 1) * HEAD_SIZE)
                q, da = q_ref[q_at, cols], da_s[q_at, cols]
                s = dot_nt(k, q) * scale - lse_ref[pl.ds(h, 1), q_at]
                if masked:
                    s = jnp.where(allowed, s, large_negative)
                p = jnp.exp(s)
                dp = dot_nt(v, da)
                ds = (p * (dp - delta_s[pl.ds(h, 1), q_at])).astype(bf16)
                dv = dv + dot_nn(p.astype(bf16), da)
                dk = dk + dot_nn(ds, q)
                dq_s[q_at, cols] += dot_tn(ds, k)
            return dk, dv

        zero = jnp.zeros((tile, HEAD_SIZE), f32)
        carry = (zero, zero)
        whole_tile = (j + 1) * tile <= length
        carry = lax.fori_loop(j, j + 1, functools.partial(tile_step, masked=True), carry)
        first_full = jnp.where(whole_tile, j + 1, tiles)
        carry = lax.fori_loop(
            j + 1, first_full, functools.partial(tile_step, masked=True), carry
        )
        carry = lax.fori_loop(first_full, tiles, functools.partial(tile_step, masked=False), carry)
        dk_s[k_at, :], dv_s[k_at, :] = carry[0] * scale, carry[1]
        return unused

    lax.fori_loop(0, (length + tile - 1) // tile, k_step, 0)

    dqg_ref[...] = jnp.zeros_like(dqg_ref)
    dkg_ref[...] = jnp.zeros_like(dkg_ref)

    def last_step(b, unused):
        src = pl.ds(pl.multiple_of(b * blk, blk), blk)
        cosine, sine = cos_ref[src, :], sin_ref[src, :]
        for h in range(heads):
            cols = slice(h * HEAD_SIZE, (h + 1) * HEAD_SIZE)
            grad = (dq_s[src, cols] * scale).astype(bf16).astype(f32)
            out, gain = unturn(grad, qraw_ref[src, cols], qg_ref[...], cosine, sine)
            turned_s[src, cols] = out.astype(bf16)
            dqg_ref[...] += gain
        if finish_keys:
            grad = dk_s[src, :].astype(bf16).astype(f32)
            out, gain = unturn(grad, kraw_ref[src, :], kg_ref[...], cosine, sine)
            turned_s[src, heads * HEAD_SIZE : (heads + 1) * HEAD_SIZE] = out.astype(bf16)
            dkg_ref[...] += gain
            turned_s[src, (heads + 1) * HEAD_SIZE :] = dv_s[src, :].astype(bf16)
        return unused

    lax.fori_loop(0, blocks, last_step, 0)

    def place_step(b, unused):
        dst = pl.ds(pl.multiple_of(b * blk, blk), blk)
        d_ref[dst, :] = turned_s[pl.ds(pl.multiple_of(place_ref[b] * blk, blk), blk), :]
        return unused

    lax.fori_loop(0, blocks, place_step, 0)


def attend_back(
    length, places, by_index, q, k, v, da, o, lse, qraw, kraw, qg, kg, cosine, sine, heads, finish_keys
):
    total = q.shape[0]
    tile = min(512, total)
    vm = lambda: pl.BlockSpec(memory_space=pltpu.VMEM)
    sm = lambda: pl.BlockSpec(memory_space=pltpu.SMEM)
    width = (heads + 2 if finish_keys else heads) * HEAD_SIZE
    sums = [jax.ShapeDtypeStruct((total, HEAD_SIZE), f32)] * 2
    out = [
        jax.ShapeDtypeStruct((total, width), bf16),
        jax.ShapeDtypeStruct((1, HEAD_SIZE), f32),
        jax.ShapeDtypeStruct((1, HEAD_SIZE), f32),
    ] + ([] if finish_keys else sums)
    scratch = [
        pltpu.VMEM((total, heads * HEAD_SIZE), bf16),
        pltpu.VMEM((heads, total), f32),
        pltpu.VMEM((total, heads * HEAD_SIZE), f32),
        pltpu.VMEM((total, width), bf16),
    ] + ([pltpu.VMEM(s.shape, s.dtype) for s in sums] if finish_keys else [])
    return pl.pallas_call(
        functools.partial(attend_back_kernel, heads, tile, finish_keys),
        in_specs=[sm(), sm(), sm()] + [vm() for _ in range(12)],
        out_specs=[vm() for _ in out],
        out_shape=out,
        scratch_shapes=scratch,
        compiler_params=pltpu.CompilerParams(vmem_limit_bytes=VMEM_LIMIT),
        cost_estimate=cost_of(33.0 * total * heads / 4096),
        name="attend_back",
    )(length, places, by_index, q, k, v, da, o, lse, qraw, kraw, qg, kg, cosine, sine)


def branch_kernel(order_ref, a_ref, wo_ref, x_ref, gain_ref, h1_ref, xn_ref, acc):
    step = pl.program_id(0)

    @pl.when(step == 0)
    def _():
        acc[...] = x_ref[...].astype(f32)

    acc[...] += dot_nt(a_ref[0], wo_ref[0])

    @pl.when(step == pl.num_programs(0) - 1)
    def _():
        h1 = acc[...]
        h1_ref[...] = h1
        xn_ref[...] = (h1 * rms_scale(h1) * gain_ref[...]).astype(bf16)


def branch(order, a_tok, wo_slots, x, gain):
    n, rows, q_cols = a_tok.shape
    depth = x.shape[1]
    const = lambda i, p: (0, 0)
    return pl.pallas_call(
        branch_kernel,
        grid_spec=pltpu.PrefetchScalarGridSpec(
            num_scalar_prefetch=1,
            grid=(n,),
            in_specs=[
                pl.BlockSpec((1, rows, q_cols), lambda i, p: (p[i], 0, 0)),
                pl.BlockSpec((1, depth, q_cols), lambda i, p: (i, 0, 0)),
                pl.BlockSpec((rows, depth), const),
                pl.BlockSpec((1, depth), const),
            ],
            out_specs=[pl.BlockSpec((rows, depth), const)] * 2,
            scratch_shapes=[pltpu.VMEM((rows, depth), f32)],
        ),
        out_shape=[
            jax.ShapeDtypeStruct((rows, depth), f32),
            jax.ShapeDtypeStruct((rows, depth), bf16),
        ],
        compiler_params=pltpu.CompilerParams(vmem_limit_bytes=VMEM_LIMIT),
        cost_estimate=cost_of(0.3 * 11.0),
        name="branch",
    )(order, a_tok, wo_slots, x, gain)


def branch_back_kernel(
    order_ref, dxn_ref, h1_ref, dy_ref, gain_ref, wo_ref, dh_ref, dz_ref, dg_ref, da_ref, dz_s
):
    @pl.when(pl.program_id(0) == 0)
    def _():
        h1, dxn = h1_ref[...], dxn_ref[...]
        scale = rms_scale(h1)
        hat = h1 * scale
        dg_ref[...] = jnp.sum(dxn * hat, axis=0, keepdims=True)
        e = dxn * gain_ref[...]
        dh = dy_ref[...].astype(f32) + scale * (e - hat * jnp.mean(e * hat, axis=-1, keepdims=True))
        dh_ref[...] = dh
        dz = dh.astype(bf16)
        dz_ref[...] = dz
        dz_s[...] = dz

    da_ref[0] = dot_nn(dz_s[...], wo_ref[0]).astype(bf16)


def branch_back(order, dxn, h1, dy, gain, wo_slots):
    n, depth, q_cols = wo_slots.shape
    rows = dxn.shape[0]
    const = lambda i, p: (0, 0)
    own = pl.BlockSpec((rows, depth), const)
    return pl.pallas_call(
        branch_back_kernel,
        grid_spec=pltpu.PrefetchScalarGridSpec(
            num_scalar_prefetch=1,
            grid=(n,),
            in_specs=[
                own, own, own, pl.BlockSpec((1, depth), const),
                pl.BlockSpec((1, depth, q_cols), lambda i, p: (i, 0, 0)),
            ],
            out_specs=[
                own, own, pl.BlockSpec((1, depth), const),
                pl.BlockSpec((1, rows, q_cols), lambda i, p: (p[i], 0, 0)),
            ],
            scratch_shapes=[pltpu.VMEM((rows, depth), bf16)],
        ),
        out_shape=[
            jax.ShapeDtypeStruct((rows, depth), f32),
            jax.ShapeDtypeStruct((rows, depth), bf16),
            jax.ShapeDtypeStruct((1, depth), f32),
            jax.ShapeDtypeStruct((n, rows, q_cols), bf16),
        ],
        compiler_params=pltpu.CompilerParams(vmem_limit_bytes=VMEM_LIMIT),
        cost_estimate=cost_of(13.0),
        name="branch_back",
    )(order, dxn, h1, dy, gain, wo_slots)


def feed_kernel(count, *refs):
    x_pieces, y_pieces = refs[:count], refs[count : 2 * count]
    w_ref, d_ref, hm_ref, x_all, y_all, x_sem, y_sem = refs[2 * count :]
    step = pl.program_id(0)
    _, rows, depth = x_all.shape
    ff = hm_ref.shape[2]

    @pl.when(step == 0)
    def _():
        for xc, yc in zip(
            piece_copies(x_pieces, x_all, x_sem, rows), piece_copies(y_pieces, y_all, y_sem, rows)
        ):
            xc.start()
            yc.start()

    for k in range(2):
        slot = 2 * step + k
        pltpu.make_async_copy(x_all.at[slot], x_all.at[slot], x_sem.at[slot]).wait()
    at = pl.ds(2 * step, 2)
    y = dot_nn(x_all[at].reshape(2 * rows, depth), w_ref[:, : 2 * ff])
    for k in range(2):
        slot = 2 * step + k
        pltpu.make_async_copy(y_all.at[slot], y_all.at[slot], y_sem.at[slot]).wait()
    dhm = dot_nn(y_all[at].reshape(2 * rows, depth), w_ref[:, 2 * ff :])
    g, u = y[:, :ff], y[:, ff:]
    sigma = jax.nn.sigmoid(g)
    silu = g * sigma
    hm_ref[...] = (silu * u).astype(bf16).reshape(2, rows, ff)
    d_ref[:, :, :ff] = (
        (dhm * u * sigma * (1.0 + g * (1.0 - sigma))).astype(bf16).reshape(2, rows, ff)
    )
    d_ref[:, :, ff:] = (dhm * silu).astype(bf16).reshape(2, rows, ff)


def feed(x_pieces, y_pieces, n, w):
    depth, ff = w.shape[0], w.shape[1] // 3
    total = sum(p.shape[0] for p in x_pieces)
    rows = total // n
    return pl.pallas_call(
        functools.partial(feed_kernel, len(x_pieces)),
        grid=(n // 2,),
        in_specs=[any_spec() for _ in x_pieces + y_pieces]
        + [pl.BlockSpec(w.shape, lambda i: (0, 0))],
        out_specs=[
            pl.BlockSpec((2, rows, 2 * ff), lambda i: (i, 0, 0)),
            pl.BlockSpec((2, rows, ff), lambda i: (i, 0, 0)),
        ],
        out_shape=[
            jax.ShapeDtypeStruct((n, rows, 2 * ff), bf16),
            jax.ShapeDtypeStruct((n, rows, ff), bf16),
        ],
        scratch_shapes=[
            pltpu.VMEM((n, rows, depth), bf16),
            pltpu.VMEM((n, rows, depth), bf16),
            pltpu.SemaphoreType.DMA((n,)),
            pltpu.SemaphoreType.DMA((n,)),
        ],
        compiler_params=pltpu.CompilerParams(vmem_limit_bytes=VMEM_LIMIT),
        cost_estimate=cost_of(0.05 * 17.0 * total * ff / (2048 * 384)),
        name="feed",
    )(*x_pieces, *y_pieces, w)


def per_device(
    n, n_fsdp, layer_input, dy, block_order, lengths, attn_gain, wq, wk, wv, q_gain, k_gain, wo,
    mlp_gain, wg, wu, wd,
):
    me = lax.axis_index("ctx")
    x, dy = layer_input[0], dy[0]
    rows, depth = x.shape
    total = n * rows
    shard = wq.shape[0]
    heads = QUERY_HEADS // n
    kv_share = max(n // KEY_VALUE_HEADS, 1)
    ff = wg.shape[1] // n
    q_cols = heads * HEAD_SIZE
    parts = [2 * ff // 3, ff // 3] if ff % 384 == 0 and ff > 384 else [ff]

    def cols(w, width, index):
        return lax.dynamic_slice_in_dim(w, index * width, width, axis=1)

    def whole(w):
        return lax.all_gather(w, "fsdp", axis=0, tiled=True)

    kv_index = me // kv_share
    w_in = jnp.concatenate(
        [cols(wq, q_cols, me), cols(wk, HEAD_SIZE, kv_index), cols(wv, HEAD_SIZE, kv_index)], axis=1
    )
    in_cols = w_in.shape[1]
    w_attn = jnp.concatenate([w_in, cols(wo, q_cols, me)], axis=1)
    width = w_attn.shape[1]
    gains = jnp.concatenate([attn_gain, mlp_gain])
    gain_rows = -(-gains.shape[0] // (16 * width)) * 16
    gains = jnp.pad(gains, (0, gain_rows * width - gains.shape[0])).reshape(gain_rows, width)
    pack = lax.all_gather(jnp.concatenate([w_attn, gains], axis=0), "fsdp", axis=0)
    x_pair = gather_pair(x, n)
    dy_pair = gather_pair(after(dy, x_pair), n)
    x_pieces = gather_rest(x_pair, n, last=[dy_pair])

    def feed_weights(part, gate):
        at = ff * me + sum(parts[:part])
        w = [lax.dynamic_slice_in_dim(w, at, parts[part], axis=1) for w in (wg, wu, wd)]
        return whole(after(jnp.concatenate(w, axis=1), gate))

    w_ff = [feed_weights(0, x_pair)]
    dy_pieces = gather_rest(dy_pair, n, [x_pieces[-1]])
    w_in = pack[:, :shard, :in_cols].reshape(depth, in_cols)
    wo_c = pack[:, :shard, in_cols:].reshape(depth, q_cols)
    gains = pack[:, shard:].reshape(n_fsdp, -1)
    attn_gain = gains[:, :shard].reshape(1, depth).astype(f32)
    mlp_gain = gains[:, shard : 2 * shard].reshape(1, depth).astype(f32)

    order = slot_order(n)
    by_index = block_order.reshape(-1)
    places = jnp.take(block_order, order, axis=0).reshape(-1)
    half = HEAD_SIZE // 2
    lane = jnp.arange(HEAD_SIZE, dtype=jnp.int32)
    frequency = jnp.exp(-math.log(rope_base) * 2.0 * (lane % half).astype(f32) / HEAD_SIZE)
    angle = jnp.arange(total, dtype=f32)[:, None] * frequency[None, :]
    cosine = jnp.cos(angle)
    sine = jnp.sin(angle) * jnp.where(lane < half, -1.0, 1.0)[None, :]
    qg = q_gain.astype(f32).reshape(1, HEAD_SIZE)
    kg = k_gain.astype(f32).reshape(1, HEAD_SIZE)

    xn, q_raw, k_raw, qb, kb, vb = project(
        x_pieces, n, places, attn_gain, pack, qg, kg, cosine, sine, heads
    )
    w_ff += [feed_weights(part, qb) for part in range(1, len(parts))]
    o, a, a_index, lse = attend(
        lengths, places, by_index, after(qb, dy_pieces[len(dy_pieces) // 4]), kb, vb, heads
    )
    a_tok = exchange(a_index.reshape(n, rows, q_cols))
    wo_slots = assemble(gather_rest(gather_pair(after(wo_c, x_pieces[-1]), n), n, [qb], [a_index]), n)
    h1, xn2 = branch(order, a_tok, wo_slots, x, mlp_gain)

    xn2_pieces = gather_rest(gather_pair(xn2, n), n)
    xn2_pieces = [after(xn2_pieces[0], w_in)] + xn2_pieces[1:]
    d_gu, hm, grads = [], [], []

    def ff_grad(d_part, hm_part, cover):
        return weight_grad(
            [
                (xn2_pieces, d_part.reshape(total, -1)),
                (dy_pieces, hm_part.reshape(total, -1)),
            ],
            n, n_fsdp, cover=cover,
        )

    for w in w_ff:
        if d_gu:
            grads += ff_grad(d_gu[-1], hm[-1], 0.05)
            xn2_pieces = [after(xn2_pieces[0], grads[-1])] + xn2_pieces[1:]
        d_part, hm_part = feed(xn2_pieces, dy_pieces, n, w)
        d_gu.append(d_part)
        hm.append(hm_part)
    to_xn2 = SumScatter(d_gu, w_ff, 0, n, halves=True)
    send = to_xn2.add_send(d_gu)
    grads += ff_grad(after(d_gu[-1], send), hm[-1], 1.0)
    d_ff = [reduce_rows(grad, n) for grad in grads]
    to_xn2.add_keep([after(d_gu[0], send)] + d_gu[1:])
    to_xn2.second(held=grads[-1])
    hm = [after(hm[0], to_xn2.last)] + hm[1:]
    to_m = SumScatter(hm, w_ff, 2, n)
    d_xn2 = after(to_xn2.result(), grads[-1], to_m.far)

    d_h1, dz, d_mlp_gain, da = branch_back(
        order, d_xn2, h1, dy, mlp_gain, wo_slots
    )
    da = exchange(da).reshape(total, q_cols)
    hm = [after(hm[0], d_h1)] + hm[1:]
    dz_pair = after(gather_pair(dz, n, [to_m.add_send(hm)]), da)
    dz_other = swap_first(dz_pair, n, False) if n == 8 else dz_pair
    da = after(da, dz_pair, d_ff[0])
    to_m.step(dz_pair)
    d_ff[0] = exchange(after(d_ff[0], da))
    d_qkv, d_qg, d_kg, *key_sums = attend_back(
        lengths, places, by_index, qb, kb, vb, da, o, lse, q_raw, k_raw, qg, kg, cosine, sine,
        heads, kv_share == 1,
    )
    if kv_share > 1:
        groups = [list(range(g, g + kv_share)) for g in range(0, n, kv_share)]
        first = (me % kv_share == 0).astype(f32)
        dk, dv = (
            lax.psum(t, "ctx", axis_index_groups=groups).astype(bf16).astype(f32) * first
            for t in key_sums
        )
        grad = dk * cosine - jnp.roll(dk, half, axis=1) * sine
        scale = rms_scale(k_raw)
        hat = k_raw * scale
        d_kg = jnp.sum(grad * hat, axis=0, keepdims=True)
        grad = grad * kg
        dk = scale * (grad - hat * jnp.mean(grad * hat, axis=-1, keepdims=True))
        d_kv = jnp.concatenate([dk, dv], axis=1).astype(bf16).reshape(2 * n, -1, 2 * HEAD_SIZE)
        d_qkv = jnp.concatenate([d_qkv, d_kv[places].reshape(total, -1)], axis=1)
    dz_pieces = gather_rest(dz_pair, n, last=[d_qkv], other=dz_other)
    d_attn, d_attn_gain = weight_grad(
        [([after(xn, d_ff[-1]).reshape(total, depth)], d_qkv), (dz_pieces, a)], n, n_fsdp, w_in,
        attn_gain.reshape(depth, 1),
    )
    d_attn_sum = reduce_rows(d_attn, n)
    to_m.second(held=d_attn, stepped=True)
    sums = jnp.concatenate([d_attn_gain[:, 0], d_mlp_gain[0], d_qg[0], d_kg[0]])
    sums = sum_across(sums.reshape(-1, HEAD_SIZE), n, 2, "ctx")
    left = after(d_qkv, d_attn, to_m.last, sums).reshape(n, rows, in_cols)
    to_xn = SumScatter([left], [w_in], 0, n, cover=0.1)
    to_xn.add_send([left])
    to_xn.second(d_ff[0])
    d_ff = d_ff[:1] + [exchange(after(d, to_xn.last)) for d in d_ff[1:]]
    sums = sum_across(sums + swap(sums, n, 1), n_fsdp, 1, "fsdp")
    d_xn = to_xn.result()
    output = (h1 + to_m.result()).astype(bf16)
    sums = sums.reshape(-1)
    x_float = x.astype(f32)
    scale_one = rms_scale(x_float)
    hat_one = x_float * scale_one
    e = d_xn * attn_gain
    dx = d_h1 + scale_one * (e - hat_one * jnp.mean(e * hat_one, axis=-1, keepdims=True))

    d_attn = exchange(d_attn_sum)
    d_wg, d_wu, d_wd = join_columns(
        d_ff,
        [[(p, k * size, (k + 1) * size) for p, size in enumerate(parts)] for k in range(3)],
    )
    k_cols, v_cols = q_cols + HEAD_SIZE, q_cols + 2 * HEAD_SIZE
    kv_parts = [[(0, q_cols, k_cols)], [(0, k_cols, v_cols)]]
    d_wq, d_wo, *d_kv = join_columns(
        [d_attn],
        [[(0, 0, q_cols)], [(0, v_cols, v_cols + q_cols)]] + (kv_parts if kv_share == 1 else []),
    )
    d_wk, d_wv = d_kv or join_columns([d_attn[::kv_share]], kv_parts)
    return (
        output[None],
        dx[None],
        d_wq,
        d_wk,
        d_wv,
        d_wo,
        d_wg,
        d_wu,
        d_wd,
        sums[:depth],
        sums[depth : 2 * depth],
        sums[2 * depth : 2 * depth + HEAD_SIZE],
        sums[2 * depth + HEAD_SIZE :],
    )


def solution(mesh):
    n, n_fsdp = mesh.shape["ctx"], mesh.shape["fsdp"]
    row, act = P("fsdp", None), P("fsdp", "ctx", None)
    own = P(("ctx", "fsdp"), None)
    return jax.shard_map(
        functools.partial(per_device, n, n_fsdp),
        mesh=mesh,
        in_specs=(
            act, act, P(), P("fsdp"), P("fsdp"), row, row, row, P(), P(), row, P("fsdp"), row, row, row,
        ),
        out_specs=(act, act) + (own,) * 7 + (P(),) * 4,
        check_vma=False,
    )
```

```python
import functools
import math

import jax
import jax.numpy as jnp
from jax import lax
from jax.experimental import pallas as pl
from jax.experimental.pallas import tpu as pltpu
from jax.sharding import PartitionSpec as P

QUERY_HEADS = 16
KEY_VALUE_HEADS = 8
HEAD_SIZE = 128

epsilon = 1e-06
rope_base = 1000000.0
large_negative = -1e30

bf16 = jnp.bfloat16
f32 = jnp.float32
VMEM_LIMIT = 56 * 1024 * 1024


def cost_of(microseconds):
    return pl.CostEstimate(
        flops=int(microseconds * 1.1e9), bytes_accessed=1 << 20, transcendentals=0
    )


def dot_nn(left, right):
    return lax.dot_general(left, right, (((1,), (0,)), ((), ())), preferred_element_type=f32)


def dot_nt(left, right):
    return lax.dot_general(left, right, (((1,), (1,)), ((), ())), preferred_element_type=f32)


def dot_tn(left, right):
    return lax.dot_general(left, right, (((0,), (0,)), ((), ())), preferred_element_type=f32)


def rms_scale(values):
    return lax.rsqrt(jnp.mean(values * values, axis=-1, keepdims=True) + epsilon)


def swap(values, n, bits, axis="ctx"):
    return lax.ppermute(values, axis, [(c, c ^ bits) for c in range(n)])


def swap_first(values, n, first):
    return lax.ppermute(
        values, "ctx", [(c, c ^ (2 if (c % 2 == 0) == first else 4)) for c in range(n)]
    )


def slot_order(n):
    me = lax.axis_index("ctx")
    slots = jnp.arange(n, dtype=jnp.int32)
    if n == 8:
        even = jnp.array([0, 2, 4, 6, 1, 5, 3, 7], jnp.int32)
        odd = jnp.array([0, 4, 2, 6, 1, 3, 5, 7], jnp.int32)
        slots = jnp.where(me % 2 == 0, even, odd)
    return me ^ slots


def any_spec():
    return pl.BlockSpec(memory_space=pl.ANY)


def gather_pair(rows, n, gates=()):
    if n != 8:
        return rows
    return jnp.concatenate([after(rows, *gates), swap_first(rows, n, True)], axis=0)


def gather_rest(pair, n, second=(), last=(), other=None):
    if n != 8:
        full = lax.all_gather(pair, "ctx", axis=0)
        return [jnp.take(full, slot_order(n), axis=0).reshape(-1, pair.shape[1])]
    pair = after(pair, *second)
    if other is None:
        other = swap_first(pair, n, False)
    return [pair, after(other, *last), swap(pair, n, 1), swap(after(other, *last), n, 1)]


def piece_copies(pieces, out, sem, rows):
    copies, at = [], 0
    for piece in pieces:
        size = piece.shape[0]
        slot, start = at // rows, at % rows
        if size > rows:
            for k in range(size // rows):
                copies.append(
                    pltpu.make_async_copy(
                        piece.at[pl.ds(k * rows, rows)], out.at[slot + k], sem.at[slot + k]
                    )
                )
        else:
            copies.append(
                pltpu.make_async_copy(piece, out.at[slot, pl.ds(start, size)], sem.at[slot])
            )
        at += size
    return copies


def assemble_kernel(count, rows, *refs):
    out, held, sem, out_sem = refs[count:]
    for copy in piece_copies(refs[:count], held, sem, rows):
        copy.start()
    slots = range(out.shape[0])
    for slot in slots:
        pltpu.make_async_copy(held.at[slot], held.at[slot], sem.at[slot]).wait()
        pltpu.make_async_copy(held.at[slot], out.at[slot], out_sem.at[slot]).start()
    for slot in slots:
        pltpu.make_async_copy(held.at[slot], out.at[slot], out_sem.at[slot]).wait()


def assemble(pieces, n):
    total = sum(p.shape[0] for p in pieces)
    rows, width = total // n, pieces[0].shape[1]
    if len(pieces) == 1:
        return pieces[0].reshape(n, rows, width)
    return pl.pallas_call(
        functools.partial(assemble_kernel, len(pieces), rows),
        in_specs=[any_spec() for _ in pieces],
        out_specs=any_spec(),
        out_shape=jax.ShapeDtypeStruct((n, rows, width), pieces[0].dtype),
        scratch_shapes=[
            pltpu.VMEM((n, rows, width), pieces[0].dtype),
            pltpu.SemaphoreType.DMA((n,)),
            pltpu.SemaphoreType.DMA((n,)),
        ],
        compiler_params=pltpu.CompilerParams(vmem_limit_bytes=VMEM_LIMIT),
        cost_estimate=cost_of(0.3 * 6.0 * total * width / 2**22),
        name="assemble",
    )(*pieces)


def mm_kernel(count, added, *refs):
    out_refs = refs[2 * count + added :]
    slots, rows = refs[0].shape[:2]
    tile = out_refs[0].shape[2]
    total = None
    for k in range(count):
        left = refs[k][...].reshape(slots * rows, refs[k].shape[2])
        term = dot_nt(left, refs[count + k][...])
        total = term if total is None else total + term
    total = total.reshape(slots, rows, tile)
    if added:
        total = total + refs[2 * count][...].astype(f32)
    at = 0
    for out_ref in out_refs:
        out_ref[...] = total[at : at + out_ref.shape[0]].astype(out_ref.dtype)
        at += out_ref.shape[0]


def mm_slots(lefts, ws, column, start, count, add=None, dtypes=(bf16,), cover=1.0):
    rows = lefts[0].shape[1]
    width = ws[0].shape[0]
    tile = min(width, 512)
    depths = [left.shape[2] for left in lefts]
    each = count // len(dtypes)
    return pl.pallas_call(
        functools.partial(mm_kernel, len(lefts), int(add is not None)),
        grid=(width // tile,),
        in_specs=[
            pl.BlockSpec((count, rows, d), lambda j: (start // count, 0, 0)) for d in depths
        ]
        + [pl.BlockSpec((tile, d), lambda j: (j, column)) for d in depths]
        + ([] if add is None else [pl.BlockSpec((count, rows, tile), lambda j: (0, 0, j))]),
        out_specs=[pl.BlockSpec((each, rows, tile), lambda j: (0, 0, j)) for _ in dtypes],
        out_shape=[jax.ShapeDtypeStruct((each, rows, width), d) for d in dtypes],
        compiler_params=pltpu.CompilerParams(vmem_limit_bytes=VMEM_LIMIT),
        cost_estimate=cost_of(cover * (2.0 + 8.0 * count * rows * sum(depths) * width / (1024 * 1536 * 2048))),
        name="mm_slots",
    )(*lefts, *ws, *([] if add is None else [add]))


class SumScatter:
    def __init__(self, lefts, ws, column, n, halves=False, cover=1.0):
        self.n, self.args, self.halves, self.cover = n, (ws, column), halves, cover
        if n != 8:
            (part,) = mm_slots(lefts, ws, column, 0, n)
            self.far = self.send = jnp.take(part, jnp.argsort(slot_order(n)), axis=0)
        elif halves:
            self.far = [mm_slots(lefts, ws, column, at, 2)[0] for at in (6, 4)]
            self.got = [swap(far, n, 1) for far in self.far]
        else:
            (self.far,) = mm_slots(lefts, ws, column, 4, 4, cover=cover)
            self.got = swap(self.far, n, 1)

    def add_send(self, lefts):
        if self.n == 8 and self.halves:
            (self.send,) = mm_slots(lefts, *self.args, 2, 2, self.got[0])
        elif self.n == 8:
            self.keep, self.send = mm_slots(
                lefts, *self.args, 0, 4, self.got, (f32, bf16), self.cover
            )
        return self.send

    def add_keep(self, lefts):
        if self.n == 8:
            (self.keep,) = mm_slots(lefts, *self.args, 0, 2, self.got[1], (f32,))

    def step(self, *gates):
        if self.n == 8:
            self.got = swap_first(after(self.send, *gates), self.n, False)

    def second(self, *gates, held=None, stepped=False):
        if self.n == 8:
            if held is not None:
                self.keep = after(self.keep, held)
            if not stepped:
                self.step(*gates)
            got = self.got
            self.last = (self.keep[1] + got[1].astype(f32)).astype(bf16)
            self.part = self.keep[0] + got[0].astype(f32)
            return self.last
        self.last = self.send
        return self.last

    def result(self):
        if self.n == 8:
            return self.part + swap_first(self.last, self.n, True).astype(f32)
        return lax.psum_scatter(self.send, "ctx", scatter_dimension=0, tiled=True)[0].astype(f32)


def exchange(blocks):
    return lax.all_to_all(blocks, "ctx", 0, 0, tiled=True)


def weight_kernel(counts, gained, *refs):
    if gained:
        refs, w_ref, gain_ref, dg_ref = refs[:-4] + refs[-2:-1], refs[-4], refs[-3], refs[-1]
    refs, out_ref = refs[:-1], refs[-1]
    tops, at = [], 0
    for count in counts:
        left = jnp.concatenate([r[...] for r in refs[at : at + count]], axis=0)
        tops.append(dot_tn(left, refs[at + count][...]))
        at += count + 1
    if gained:
        dg_ref[...] = jnp.sum(tops[0] * w_ref[...].astype(f32), axis=1, keepdims=True) / gain_ref[...]
    shards, _, rows, width = out_ref.shape
    out_ref[...] = jnp.concatenate(tops, axis=1).astype(bf16).reshape(shards, 1, rows, width)


def weight_grad(pairs, n, n_fsdp, w=None, gain=None, cover=1.0):
    depth = pairs[0][0][0].shape[1]
    rows, tile = depth // (n * n_fsdp), depth // n
    width = sum(right.shape[1] for _, right in pairs)
    total = pairs[0][1].shape[0]
    specs, args = [], []
    for pieces, right in pairs:
        specs += [pl.BlockSpec((p.shape[0], tile), lambda j: (0, j)) for p in pieces]
        specs.append(pl.BlockSpec(right.shape, lambda j: (0, 0)))
        args += [*pieces, right]
    out_specs = [pl.BlockSpec((n_fsdp, 1, rows, width), lambda j: (0, j, 0, 0))]
    out_shape = [jax.ShapeDtypeStruct((n_fsdp, n, rows, width), bf16)]
    if w is not None:
        column = pl.BlockSpec((tile, 1), lambda j: (j, 0))
        specs += [pl.BlockSpec((tile, w.shape[1]), lambda j: (j, 0)), column]
        args += [w, gain]
        out_specs.append(column)
        out_shape.append(jax.ShapeDtypeStruct((depth, 1), f32))
    out = pl.pallas_call(
        functools.partial(weight_kernel, [len(pieces) for pieces, _ in pairs], w is not None),
        grid=(n,),
        in_specs=specs,
        out_specs=out_specs,
        out_shape=out_shape,
        compiler_params=pltpu.CompilerParams(vmem_limit_bytes=VMEM_LIMIT),
        cost_estimate=cost_of(cover * 16.0 * total * depth * width / (2048 * 2048 * 1152)),
        name="weight_grad",
    )(*args)
    return [out[0].reshape(depth, width)] + list(out[1:])


def reduce_rows(grad, n):
    summed = lax.psum_scatter(grad, "fsdp", scatter_dimension=0, tiled=True)
    return summed.reshape(n, -1, grad.shape[1])


def join_kernel(count, parts, *refs):
    for out_ref, slices in zip(refs[count:], parts):
        out_ref[...] = jnp.concatenate(
            [refs[k][0, :, lo:hi].astype(f32) for k, lo, hi in slices], axis=1
        )


def join_columns(gots, parts):
    n, rows, _ = gots[0].shape
    sizes = [sum(hi - lo for _, lo, hi in slices) for slices in parts]
    return pl.pallas_call(
        functools.partial(join_kernel, len(gots), parts),
        grid=(n,),
        in_specs=[pl.BlockSpec((1, rows, got.shape[2]), lambda i: (i, 0, 0)) for got in gots],
        out_specs=[pl.BlockSpec((rows, size), lambda i: (0, i)) for size in sizes],
        out_shape=[jax.ShapeDtypeStruct((rows, n * size), f32) for size in sizes],
        cost_estimate=cost_of(1.0),
        name="join_columns",
    )(*gots)


def sum_across(values, size, bits, axis):
    while bits < size:
        values = values + swap(values, size, bits, axis)
        bits *= 2
    return values


def after(values, *others):
    return lax.optimization_barrier((values,) + others)[0]


def project_kernel(count, heads, place_ref, *refs):
    pieces, refs = refs[:count], refs[count:]
    gain_ref, w_ref, qg_ref, kg_ref, cos_ref, sin_ref = refs[:6]
    xn_ref, qraw_ref, kraw_ref, qb_ref, kb_ref, vb_ref, x_all, sem = refs[6:]
    slot = pl.program_id(0)

    @pl.when(slot == 0)
    def _():
        for copy in piece_copies(pieces, x_all, sem, x_all.shape[1]):
            copy.start()

    pltpu.make_async_copy(x_all.at[slot], x_all.at[slot], sem.at[slot]).wait()
    x = x_all[slot].astype(f32)
    xn = (x * rms_scale(x) * gain_ref[...]).astype(bf16)
    xn_ref[0] = xn
    w = w_ref[...].reshape(x.shape[1], w_ref.shape[2])
    y = jnp.dot(xn, w, preferred_element_type=f32)
    blk = x.shape[0] // 2
    for half in range(2):
        place = place_ref[2 * slot + half]
        at = pl.ds(pl.multiple_of(place * blk, blk), blk)
        cosine, sine = cos_ref[at, :], sin_ref[at, :]
        rows = y[half * blk : (half + 1) * blk]
        for head in range(heads + 1):
            raw = rows[:, head * HEAD_SIZE : (head + 1) * HEAD_SIZE]
            gain = (qg_ref if head < heads else kg_ref)[...]
            normed = raw * rms_scale(raw) * gain
            turned = normed * cosine + pltpu.roll(normed, HEAD_SIZE // 2, 1) * sine
            if head < heads:
                cols = slice(head * HEAD_SIZE, (head + 1) * HEAD_SIZE)
                qraw_ref[at, cols] = raw
                qb_ref[at, cols] = turned.astype(bf16)
            else:
                kraw_ref[at, :] = raw
                kb_ref[at, :] = turned.astype(bf16)
        vb_ref[at, :] = rows[:, (heads + 1) * HEAD_SIZE :].astype(bf16)


def project(pieces, n, places, gain, pack, q_gain, k_gain, cosine, sine, heads):
    depth = pieces[0].shape[1]
    total = sum(p.shape[0] for p in pieces)
    rows = total // n
    const = lambda i, p: (0, 0)
    whole = lambda a: pl.BlockSpec(a.shape, const)
    shards = pack.shape[0]
    in_cols = (heads + 2) * HEAD_SIZE
    out = [
        jax.ShapeDtypeStruct((n, rows, depth), bf16),
        jax.ShapeDtypeStruct((total, heads * HEAD_SIZE), f32),
        jax.ShapeDtypeStruct((total, HEAD_SIZE), f32),
        jax.ShapeDtypeStruct((total, heads * HEAD_SIZE), bf16),
        jax.ShapeDtypeStruct((total, HEAD_SIZE), bf16),
        jax.ShapeDtypeStruct((total, HEAD_SIZE), bf16),
    ]
    args = (q_gain, k_gain, cosine, sine)
    return pl.pallas_call(
        functools.partial(project_kernel, len(pieces), heads),
        grid_spec=pltpu.PrefetchScalarGridSpec(
            num_scalar_prefetch=1,
            grid=(n,),
            in_specs=[any_spec() for _ in pieces]
            + [
                whole(gain),
                pl.BlockSpec((shards, depth // shards, in_cols), lambda i, p: (0, 0, 0)),
            ]
            + [whole(a) for a in args],
            out_specs=[pl.BlockSpec((1, rows, depth), lambda i, p: (i, 0, 0))]
            + [pl.BlockSpec(o.shape, const) for o in out[1:]],
            scratch_shapes=[
                pltpu.VMEM((n, rows, depth), bf16),
                pltpu.SemaphoreType.DMA((n,)),
            ],
        ),
        out_shape=out,
        compiler_params=pltpu.CompilerParams(
            dimension_semantics=("arbitrary",), vmem_limit_bytes=VMEM_LIMIT
        ),
        cost_estimate=cost_of(0.3 * 16.0 * total * heads / 4096),
        name="project",
    )(places, *pieces, gain, pack, *args)


def attend_kernel(
    heads, tile, length_ref, place_ref, index_ref, q_ref, k_ref, v_ref, o_ref, a_ref, ai_ref, lse_ref
):
    total = q_ref.shape[0]
    blk = total // place_ref.shape[0]
    scale = 1.0 / math.sqrt(HEAD_SIZE)
    length = length_ref[0]
    key_tiles = (length + tile - 1) // tile

    def q_step(i, unused):
        q_at = pl.ds(pl.multiple_of(i * tile, tile), tile)
        q = [q_ref[q_at, h * HEAD_SIZE : (h + 1) * HEAD_SIZE] for h in range(heads)]

        def tile_step(j, carry, masked):
            k_at = pl.ds(pl.multiple_of(j * tile, tile), tile)
            k, v = k_ref[k_at, :], v_ref[k_at, :]
            if masked:
                key = j * tile + lax.broadcasted_iota(jnp.int32, (tile, tile), 0)
                query = i * tile + lax.broadcasted_iota(jnp.int32, (tile, tile), 1)
                allowed = (key <= query) & (key < length)
            new = []
            for h in range(heads):
                top, tot, out = carry[h]
                s = dot_nt(k, q[h]) * scale
                if masked:
                    s = jnp.where(allowed, s, large_negative)
                top_new = jnp.maximum(top, jnp.max(s, axis=0, keepdims=True))
                shrink = jnp.exp(top - top_new)
                p = jnp.exp(s - top_new)
                tot = tot * shrink + jnp.sum(p, axis=0, keepdims=True)
                out = out * shrink + dot_tn(v, p.astype(bf16))
                new.append((top_new, tot, out))
            return tuple(new)

        start = tuple(
            (
                jnp.full((1, tile), large_negative, f32),
                jnp.zeros((1, tile), f32),
                jnp.zeros((HEAD_SIZE, tile), f32),
            )
            for _ in range(heads)
        )
        full = jnp.minimum(i, length // tile)
        carry = lax.fori_loop(0, full, functools.partial(tile_step, masked=False), start)
        carry = lax.fori_loop(
            full, jnp.minimum(i + 1, key_tiles), functools.partial(tile_step, masked=True), carry
        )
        for h in range(heads):
            top, tot, out = carry[h]
            lse_ref[pl.ds(h, 1), q_at] = top + jnp.log(tot)
            o = jnp.transpose(out / tot)
            cols = slice(h * HEAD_SIZE, (h + 1) * HEAD_SIZE)
            o_ref[q_at, cols] = o
        return unused

    lax.fori_loop(0, total // tile, q_step, 0)

    def place_step(b, unused):
        src = pl.ds(pl.multiple_of(place_ref[b] * blk, blk), blk)
        dst = pl.ds(pl.multiple_of(b * blk, blk), blk)
        a_ref[dst, :] = o_ref[src, :].astype(bf16)
        src = pl.ds(pl.multiple_of(index_ref[b] * blk, blk), blk)
        ai_ref[dst, :] = o_ref[src, :].astype(bf16)
        return unused

    lax.fori_loop(0, place_ref.shape[0], place_step, 0)


def attend(length, places, by_index, q, k, v, heads):
    total = q.shape[0]
    tile = min(512, total)
    vm = lambda: pl.BlockSpec(memory_space=pltpu.VMEM)
    sm = lambda: pl.BlockSpec(memory_space=pltpu.SMEM)
    return pl.pallas_call(
        functools.partial(attend_kernel, heads, tile),
        in_specs=[sm(), sm(), sm(), vm(), vm(), vm()],
        out_specs=[vm(), vm(), vm(), vm()],
        out_shape=[
            jax.ShapeDtypeStruct((total, heads * HEAD_SIZE), f32),
            jax.ShapeDtypeStruct((total, heads * HEAD_SIZE), bf16),
            jax.ShapeDtypeStruct((total, heads * HEAD_SIZE), bf16),
            jax.ShapeDtypeStruct((heads, total), f32),
        ],
        compiler_params=pltpu.CompilerParams(vmem_limit_bytes=VMEM_LIMIT),
        cost_estimate=cost_of(0.3 * 18.5 * total * heads / 4096),
        name="attend",
    )(length, places, by_index, q, k, v)


def unturn(grad, raw, gain, cosine, sine):
    grad = grad * cosine - pltpu.roll(grad, HEAD_SIZE // 2, 1) * sine
    scale = rms_scale(raw)
    hat = raw * scale
    inner = grad * gain
    out = scale * (inner - hat * jnp.mean(inner * hat, axis=-1, keepdims=True))
    return out, jnp.sum(grad * hat, axis=0, keepdims=True)


def attend_back_kernel(
    heads, tile, finish_keys, length_ref, place_ref, index_ref, q_ref, k_ref, v_ref, da_ref, o_ref,
    lse_ref, qraw_ref, kraw_ref, qg_ref, kg_ref, cos_ref, sin_ref,
    d_ref, dqg_ref, dkg_ref, *rest,
):
    if finish_keys:
        da_s, delta_s, dq_s, turned_s, dk_s, dv_s = rest
    else:
        dk_s, dv_s, da_s, delta_s, dq_s, turned_s = rest
    total = q_ref.shape[0]
    blocks = place_ref.shape[0]
    blk = total // blocks
    scale = 1.0 / math.sqrt(HEAD_SIZE)
    length = length_ref[0]
    tiles = total // tile

    def sort_step(b, unused):
        dst = pl.ds(pl.multiple_of(index_ref[b] * blk, blk), blk)
        src = pl.ds(pl.multiple_of(b * blk, blk), blk)
        piece = da_ref[src, :]
        da_s[dst, :] = piece
        prod = piece.astype(f32) * o_ref[dst, :]
        for h in range(heads):
            cols = slice(h * HEAD_SIZE, (h + 1) * HEAD_SIZE)
            delta_s[pl.ds(h, 1), dst] = jnp.sum(jnp.transpose(prod[:, cols]), axis=0, keepdims=True)
        return unused

    lax.fori_loop(0, blocks, sort_step, 0)
    dq_s[...] = jnp.zeros_like(dq_s)
    dk_s[...] = jnp.zeros_like(dk_s)
    dv_s[...] = jnp.zeros_like(dv_s)

    def k_step(j, unused):
        k_at = pl.ds(pl.multiple_of(j * tile, tile), tile)
        k, v = k_ref[k_at, :], v_ref[k_at, :]

        def tile_step(i, carry, masked):
            dk, dv = carry
            q_at = pl.ds(pl.multiple_of(i * tile, tile), tile)
            if masked:
                key = j * tile + lax.broadcasted_iota(jnp.int32, (tile, tile), 0)
                query = i * tile + lax.broadcasted_iota(jnp.int32, (tile, tile), 1)
                allowed = (key <= query) & (key < length)
            for h in range(heads):
                cols = slice(h * HEAD_SIZE, (h + 1) * HEAD_SIZE)
                q, da = q_ref[q_at, cols], da_s[q_at, cols]
                s = dot_nt(k, q) * scale - lse_ref[pl.ds(h, 1), q_at]
                if masked:
                    s = jnp.where(allowed, s, large_negative)
                p = jnp.exp(s)
                dp = dot_nt(v, da)
                ds = (p * (dp - delta_s[pl.ds(h, 1), q_at])).astype(bf16)
                dv = dv + dot_nn(p.astype(bf16), da)
                dk = dk + dot_nn(ds, q)
                dq_s[q_at, cols] += dot_tn(ds, k)
            return dk, dv

        zero = jnp.zeros((tile, HEAD_SIZE), f32)
        carry = (zero, zero)
        whole_tile = (j + 1) * tile <= length
        carry = lax.fori_loop(j, j + 1, functools.partial(tile_step, masked=True), carry)
        first_full = jnp.where(whole_tile, j + 1, tiles)
        carry = lax.fori_loop(
            j + 1, first_full, functools.partial(tile_step, masked=True), carry
        )
        carry = lax.fori_loop(first_full, tiles, functools.partial(tile_step, masked=False), carry)
        dk_s[k_at, :], dv_s[k_at, :] = carry[0] * scale, carry[1]
        return unused

    lax.fori_loop(0, (length + tile - 1) // tile, k_step, 0)

    dqg_ref[...] = jnp.zeros_like(dqg_ref)
    dkg_ref[...] = jnp.zeros_like(dkg_ref)

    def last_step(b, unused):
        src = pl.ds(pl.multiple_of(b * blk, blk), blk)
        cosine, sine = cos_ref[src, :], sin_ref[src, :]
        for h in range(heads):
            cols = slice(h * HEAD_SIZE, (h + 1) * HEAD_SIZE)
            grad = (dq_s[src, cols] * scale).astype(bf16).astype(f32)
            out, gain = unturn(grad, qraw_ref[src, cols], qg_ref[...], cosine, sine)
            turned_s[src, cols] = out.astype(bf16)
            dqg_ref[...] += gain
        if finish_keys:
            grad = dk_s[src, :].astype(bf16).astype(f32)
            out, gain = unturn(grad, kraw_ref[src, :], kg_ref[...], cosine, sine)
            turned_s[src, heads * HEAD_SIZE : (heads + 1) * HEAD_SIZE] = out.astype(bf16)
            dkg_ref[...] += gain
            turned_s[src, (heads + 1) * HEAD_SIZE :] = dv_s[src, :].astype(bf16)
        return unused

    lax.fori_loop(0, blocks, last_step, 0)

    def place_step(b, unused):
        dst = pl.ds(pl.multiple_of(b * blk, blk), blk)
        d_ref[dst, :] = turned_s[pl.ds(pl.multiple_of(place_ref[b] * blk, blk), blk), :]
        return unused

    lax.fori_loop(0, blocks, place_step, 0)


def attend_back(
    length, places, by_index, q, k, v, da, o, lse, qraw, kraw, qg, kg, cosine, sine, heads, finish_keys
):
    total = q.shape[0]
    tile = min(512, total)
    vm = lambda: pl.BlockSpec(memory_space=pltpu.VMEM)
    sm = lambda: pl.BlockSpec(memory_space=pltpu.SMEM)
    width = (heads + 2 if finish_keys else heads) * HEAD_SIZE
    sums = [jax.ShapeDtypeStruct((total, HEAD_SIZE), f32)] * 2
    out = [
        jax.ShapeDtypeStruct((total, width), bf16),
        jax.ShapeDtypeStruct((1, HEAD_SIZE), f32),
        jax.ShapeDtypeStruct((1, HEAD_SIZE), f32),
    ] + ([] if finish_keys else sums)
    scratch = [
        pltpu.VMEM((total, heads * HEAD_SIZE), bf16),
        pltpu.VMEM((heads, total), f32),
        pltpu.VMEM((total, heads * HEAD_SIZE), f32),
        pltpu.VMEM((total, width), bf16),
    ] + ([pltpu.VMEM(s.shape, s.dtype) for s in sums] if finish_keys else [])
    return pl.pallas_call(
        functools.partial(attend_back_kernel, heads, tile, finish_keys),
        in_specs=[sm(), sm(), sm()] + [vm() for _ in range(12)],
        out_specs=[vm() for _ in out],
        out_shape=out,
        scratch_shapes=scratch,
        compiler_params=pltpu.CompilerParams(vmem_limit_bytes=VMEM_LIMIT),
        cost_estimate=cost_of(33.0 * total * heads / 4096),
        name="attend_back",
    )(length, places, by_index, q, k, v, da, o, lse, qraw, kraw, qg, kg, cosine, sine)


def branch_kernel(order_ref, a_ref, wo_ref, x_ref, gain_ref, h1_ref, xn_ref, acc):
    step = pl.program_id(0)

    @pl.when(step == 0)
    def _():
        acc[...] = x_ref[...].astype(f32)

    acc[...] += dot_nt(a_ref[0], wo_ref[0])

    @pl.when(step == pl.num_programs(0) - 1)
    def _():
        h1 = acc[...]
        h1_ref[...] = h1
        xn_ref[...] = (h1 * rms_scale(h1) * gain_ref[...]).astype(bf16)


def branch(order, a_tok, wo_slots, x, gain):
    n, rows, q_cols = a_tok.shape
    depth = x.shape[1]
    const = lambda i, p: (0, 0)
    return pl.pallas_call(
        branch_kernel,
        grid_spec=pltpu.PrefetchScalarGridSpec(
            num_scalar_prefetch=1,
            grid=(n,),
            in_specs=[
                pl.BlockSpec((1, rows, q_cols), lambda i, p: (p[i], 0, 0)),
                pl.BlockSpec((1, depth, q_cols), lambda i, p: (i, 0, 0)),
                pl.BlockSpec((rows, depth), const),
                pl.BlockSpec((1, depth), const),
            ],
            out_specs=[pl.BlockSpec((rows, depth), const)] * 2,
            scratch_shapes=[pltpu.VMEM((rows, depth), f32)],
        ),
        out_shape=[
            jax.ShapeDtypeStruct((rows, depth), f32),
            jax.ShapeDtypeStruct((rows, depth), bf16),
        ],
        compiler_params=pltpu.CompilerParams(vmem_limit_bytes=VMEM_LIMIT),
        cost_estimate=cost_of(0.3 * 11.0),
        name="branch",
    )(order, a_tok, wo_slots, x, gain)


def branch_back_kernel(
    order_ref, dxn_ref, h1_ref, dy_ref, gain_ref, wo_ref, dh_ref, dz_ref, dg_ref, da_ref, dz_s
):
    @pl.when(pl.program_id(0) == 0)
    def _():
        h1, dxn = h1_ref[...], dxn_ref[...]
        scale = rms_scale(h1)
        hat = h1 * scale
        dg_ref[...] = jnp.sum(dxn * hat, axis=0, keepdims=True)
        e = dxn * gain_ref[...]
        dh = dy_ref[...].astype(f32) + scale * (e - hat * jnp.mean(e * hat, axis=-1, keepdims=True))
        dh_ref[...] = dh
        dz = dh.astype(bf16)
        dz_ref[...] = dz
        dz_s[...] = dz

    da_ref[0] = dot_nn(dz_s[...], wo_ref[0]).astype(bf16)


def branch_back(order, dxn, h1, dy, gain, wo_slots):
    n, depth, q_cols = wo_slots.shape
    rows = dxn.shape[0]
    const = lambda i, p: (0, 0)
    own = pl.BlockSpec((rows, depth), const)
    return pl.pallas_call(
        branch_back_kernel,
        grid_spec=pltpu.PrefetchScalarGridSpec(
            num_scalar_prefetch=1,
            grid=(n,),
            in_specs=[
                own, own, own, pl.BlockSpec((1, depth), const),
                pl.BlockSpec((1, depth, q_cols), lambda i, p: (i, 0, 0)),
            ],
            out_specs=[
                own, own, pl.BlockSpec((1, depth), const),
                pl.BlockSpec((1, rows, q_cols), lambda i, p: (p[i], 0, 0)),
            ],
            scratch_shapes=[pltpu.VMEM((rows, depth), bf16)],
        ),
        out_shape=[
            jax.ShapeDtypeStruct((rows, depth), f32),
            jax.ShapeDtypeStruct((rows, depth), bf16),
            jax.ShapeDtypeStruct((1, depth), f32),
            jax.ShapeDtypeStruct((n, rows, q_cols), bf16),
        ],
        compiler_params=pltpu.CompilerParams(vmem_limit_bytes=VMEM_LIMIT),
        cost_estimate=cost_of(13.0),
        name="branch_back",
    )(order, dxn, h1, dy, gain, wo_slots)


def feed_kernel(count, *refs):
    x_pieces, y_pieces = refs[:count], refs[count : 2 * count]
    w_ref, d_ref, hm_ref, x_all, y_all, x_sem, y_sem = refs[2 * count :]
    step = pl.program_id(0)
    _, rows, depth = x_all.shape
    ff = hm_ref.shape[2]

    @pl.when(step == 0)
    def _():
        for xc, yc in zip(
            piece_copies(x_pieces, x_all, x_sem, rows), piece_copies(y_pieces, y_all, y_sem, rows)
        ):
            xc.start()
            yc.start()

    for k in range(2):
        slot = 2 * step + k
        pltpu.make_async_copy(x_all.at[slot], x_all.at[slot], x_sem.at[slot]).wait()
    at = pl.ds(2 * step, 2)
    y = dot_nn(x_all[at].reshape(2 * rows, depth), w_ref[:, : 2 * ff])
    for k in range(2):
        slot = 2 * step + k
        pltpu.make_async_copy(y_all.at[slot], y_all.at[slot], y_sem.at[slot]).wait()
    dhm = dot_nn(y_all[at].reshape(2 * rows, depth), w_ref[:, 2 * ff :])
    g, u = y[:, :ff], y[:, ff:]
    sigma = jax.nn.sigmoid(g)
    silu = g * sigma
    hm_ref[...] = (silu * u).astype(bf16).reshape(2, rows, ff)
    d_ref[:, :, :ff] = (
        (dhm * u * sigma * (1.0 + g * (1.0 - sigma))).astype(bf16).reshape(2, rows, ff)
    )
    d_ref[:, :, ff:] = (dhm * silu).astype(bf16).reshape(2, rows, ff)


def feed(x_pieces, y_pieces, n, w):
    depth, ff = w.shape[0], w.shape[1] // 3
    total = sum(p.shape[0] for p in x_pieces)
    rows = total // n
    return pl.pallas_call(
        functools.partial(feed_kernel, len(x_pieces)),
        grid=(n // 2,),
        in_specs=[any_spec() for _ in x_pieces + y_pieces]
        + [pl.BlockSpec(w.shape, lambda i: (0, 0))],
        out_specs=[
            pl.BlockSpec((2, rows, 2 * ff), lambda i: (i, 0, 0)),
            pl.BlockSpec((2, rows, ff), lambda i: (i, 0, 0)),
        ],
        out_shape=[
            jax.ShapeDtypeStruct((n, rows, 2 * ff), bf16),
            jax.ShapeDtypeStruct((n, rows, ff), bf16),
        ],
        scratch_shapes=[
            pltpu.VMEM((n, rows, depth), bf16),
            pltpu.VMEM((n, rows, depth), bf16),
            pltpu.SemaphoreType.DMA((n,)),
            pltpu.SemaphoreType.DMA((n,)),
        ],
        compiler_params=pltpu.CompilerParams(vmem_limit_bytes=VMEM_LIMIT),
        cost_estimate=cost_of(0.05 * 17.0 * total * ff / (2048 * 384)),
        name="feed",
    )(*x_pieces, *y_pieces, w)


def per_device(
    n, n_fsdp, layer_input, dy, block_order, lengths, attn_gain, wq, wk, wv, q_gain, k_gain, wo,
    mlp_gain, wg, wu, wd,
):
    me = lax.axis_index("ctx")
    x, dy = layer_input[0], dy[0]
    rows, depth = x.shape
    total = n * rows
    shard = wq.shape[0]
    heads = QUERY_HEADS // n
    kv_share = max(n // KEY_VALUE_HEADS, 1)
    ff = wg.shape[1] // n
    q_cols = heads * HEAD_SIZE
    parts = [2 * ff // 3, ff // 3] if ff % 384 == 0 and ff > 384 else [ff]

    def cols(w, width, index):
        return lax.dynamic_slice_in_dim(w, index * width, width, axis=1)

    def whole(w):
        return lax.all_gather(w, "fsdp", axis=0, tiled=True)

    kv_index = me // kv_share
    w_in = jnp.concatenate(
        [cols(wq, q_cols, me), cols(wk, HEAD_SIZE, kv_index), cols(wv, HEAD_SIZE, kv_index)], axis=1
    )
    in_cols = w_in.shape[1]
    w_attn = jnp.concatenate([w_in, cols(wo, q_cols, me)], axis=1)
    width = w_attn.shape[1]
    gains = jnp.concatenate([attn_gain, mlp_gain])
    gain_rows = -(-gains.shape[0] // (16 * width)) * 16
    gains = jnp.pad(gains, (0, gain_rows * width - gains.shape[0])).reshape(gain_rows, width)
    pack = lax.all_gather(jnp.concatenate([w_attn, gains], axis=0), "fsdp", axis=0)
    x_pair = gather_pair(x, n)
    dy_pair = gather_pair(after(dy, x_pair), n)
    x_pieces = gather_rest(x_pair, n, last=[dy_pair])

    def feed_weights(part, gate):
        at = ff * me + sum(parts[:part])
        w = [lax.dynamic_slice_in_dim(w, at, parts[part], axis=1) for w in (wg, wu, wd)]
        return whole(after(jnp.concatenate(w, axis=1), gate))

    w_ff = [feed_weights(0, x_pair)]
    dy_pieces = gather_rest(dy_pair, n, [x_pieces[-1]])
    w_in = pack[:, :shard, :in_cols].reshape(depth, in_cols)
    wo_c = pack[:, :shard, in_cols:].reshape(depth, q_cols)
    gains = pack[:, shard:].reshape(n_fsdp, -1)
    attn_gain = gains[:, :shard].reshape(1, depth).astype(f32)
    mlp_gain = gains[:, shard : 2 * shard].reshape(1, depth).astype(f32)

    order = slot_order(n)
    by_index = block_order.reshape(-1)
    places = jnp.take(block_order, order, axis=0).reshape(-1)
    half = HEAD_SIZE // 2
    lane = jnp.arange(HEAD_SIZE, dtype=jnp.int32)
    frequency = jnp.exp(-math.log(rope_base) * 2.0 * (lane % half).astype(f32) / HEAD_SIZE)
    angle = jnp.arange(total, dtype=f32)[:, None] * frequency[None, :]
    cosine = jnp.cos(angle)
    sine = jnp.sin(angle) * jnp.where(lane < half, -1.0, 1.0)[None, :]
    qg = q_gain.astype(f32).reshape(1, HEAD_SIZE)
    kg = k_gain.astype(f32).reshape(1, HEAD_SIZE)

    xn, q_raw, k_raw, qb, kb, vb = project(
        x_pieces, n, places, attn_gain, pack, qg, kg, cosine, sine, heads
    )
    w_ff += [feed_weights(part, qb) for part in range(1, len(parts))]
    o, a, a_index, lse = attend(
        lengths, places, by_index, after(qb, dy_pieces[len(dy_pieces) // 4]), kb, vb, heads
    )
    a_tok = exchange(a_index.reshape(n, rows, q_cols))
    wo_slots = assemble(gather_rest(gather_pair(after(wo_c, x_pieces[-1]), n), n, [qb], [a_index]), n)
    h1, xn2 = branch(order, a_tok, wo_slots, x, mlp_gain)

    xn2_pieces = gather_rest(gather_pair(xn2, n), n)
    xn2_pieces = [after(xn2_pieces[0], w_in)] + xn2_pieces[1:]
    d_gu, hm, grads = [], [], []

    def ff_grad(d_part, hm_part, cover):
        return weight_grad(
            [
                (xn2_pieces, d_part.reshape(total, -1)),
                (dy_pieces, hm_part.reshape(total, -1)),
            ],
            n, n_fsdp, cover=cover,
        )

    for w in w_ff:
        if d_gu:
            grads += ff_grad(d_gu[-1], hm[-1], 0.05)
            xn2_pieces = [after(xn2_pieces[0], grads[-1])] + xn2_pieces[1:]
        d_part, hm_part = feed(xn2_pieces, dy_pieces, n, w)
        d_gu.append(d_part)
        hm.append(hm_part)
    to_xn2 = SumScatter(d_gu, w_ff, 0, n, halves=True)
    send = to_xn2.add_send(d_gu)
    grads += ff_grad(after(d_gu[-1], send), hm[-1], 1.0)
    d_ff = [reduce_rows(grad, n) for grad in grads]
    to_xn2.add_keep([after(d_gu[0], send)] + d_gu[1:])
    to_xn2.second(held=grads[-1])
    hm = [after(hm[0], to_xn2.last)] + hm[1:]
    to_m = SumScatter(hm, w_ff, 2, n)
    d_xn2 = after(to_xn2.result(), grads[-1], to_m.far)

    d_h1, dz, d_mlp_gain, da = branch_back(
        order, d_xn2, h1, dy, mlp_gain, wo_slots
    )
    da = exchange(da).reshape(total, q_cols)
    hm = [after(hm[0], d_h1)] + hm[1:]
    dz_pair = after(gather_pair(dz, n, [to_m.add_send(hm)]), da)
    dz_other = swap_first(dz_pair, n, False) if n == 8 else dz_pair
    da = after(da, dz_pair, d_ff[0])
    to_m.step(dz_pair)
    d_ff[0] = exchange(after(d_ff[0], da))
    d_qkv, d_qg, d_kg, *key_sums = attend_back(
        lengths, places, by_index, qb, kb, vb, da, o, lse, q_raw, k_raw, qg, kg, cosine, sine,
        heads, kv_share == 1,
    )
    if kv_share > 1:
        groups = [list(range(g, g + kv_share)) for g in range(0, n, kv_share)]
        first = (me % kv_share == 0).astype(f32)
        dk, dv = (
            lax.psum(t, "ctx", axis_index_groups=groups).astype(bf16).astype(f32) * first
            for t in key_sums
        )
        grad = dk * cosine - jnp.roll(dk, half, axis=1) * sine
        scale = rms_scale(k_raw)
        hat = k_raw * scale
        d_kg = jnp.sum(grad * hat, axis=0, keepdims=True)
        grad = grad * kg
        dk = scale * (grad - hat * jnp.mean(grad * hat, axis=-1, keepdims=True))
        d_kv = jnp.concatenate([dk, dv], axis=1).astype(bf16).reshape(2 * n, -1, 2 * HEAD_SIZE)
        d_qkv = jnp.concatenate([d_qkv, d_kv[places].reshape(total, -1)], axis=1)
    dz_pieces = gather_rest(dz_pair, n, last=[d_qkv], other=dz_other)
    d_attn, d_attn_gain = weight_grad(
        [([after(xn, d_ff[-1]).reshape(total, depth)], d_qkv), (dz_pieces, a)], n, n_fsdp, w_in,
        attn_gain.reshape(depth, 1),
    )
    d_attn_sum = reduce_rows(d_attn, n)
    to_m.second(held=d_attn, stepped=True)
    sums = jnp.concatenate([d_attn_gain[:, 0], d_mlp_gain[0], d_qg[0], d_kg[0]])
    sums = sum_across(sums.reshape(-1, HEAD_SIZE), n, 2, "ctx")
    left = after(d_qkv, d_attn, to_m.last, sums).reshape(n, rows, in_cols)
    to_xn = SumScatter([left], [w_in], 0, n, cover=0.1)
    to_xn.add_send([left])
    to_xn.second(d_ff[0])
    d_ff = d_ff[:1] + [exchange(after(d, to_xn.last)) for d in d_ff[1:]]
    sums = sum_across(sums + swap(sums, n, 1), n_fsdp, 1, "fsdp")
    d_xn = to_xn.result()
    output = (h1 + to_m.result()).astype(bf16)
    sums = sums.reshape(-1)
    x_float = x.astype(f32)
    scale_one = rms_scale(x_float)
    hat_one = x_float * scale_one
    e = d_xn * attn_gain
    dx = d_h1 + scale_one * (e - hat_one * jnp.mean(e * hat_one, axis=-1, keepdims=True))

    d_attn = exchange(after(d_attn_sum, d_xn))
    d_wg, d_wu, d_wd = join_columns(
        d_ff,
        [[(p, k * size, (k + 1) * size) for p, size in enumerate(parts)] for k in range(3)],
    )
    k_cols, v_cols = q_cols + HEAD_SIZE, q_cols + 2 * HEAD_SIZE
    kv_parts = [[(0, q_cols, k_cols)], [(0, k_cols, v_cols)]]
    d_wq, d_wo, *d_kv = join_columns(
        [d_attn],
        [[(0, 0, q_cols)], [(0, v_cols, v_cols + q_cols)]] + (kv_parts if kv_share == 1 else []),
    )
    d_wk, d_wv = d_kv or join_columns([d_attn[::kv_share]], kv_parts)
    return (
        output[None],
        dx[None],
        d_wq,
        d_wk,
        d_wv,
        d_wo,
        d_wg,
        d_wu,
        d_wd,
        sums[:depth],
        sums[depth : 2 * depth],
        sums[2 * depth : 2 * depth + HEAD_SIZE],
        sums[2 * depth + HEAD_SIZE :],
    )


def solution(mesh):
    n, n_fsdp = mesh.shape["ctx"], mesh.shape["fsdp"]
    row, act = P("fsdp", None), P("fsdp", "ctx", None)
    own = P(("ctx", "fsdp"), None)
    return jax.shard_map(
        functools.partial(per_device, n, n_fsdp),
        mesh=mesh,
        in_specs=(
            act, act, P(), P("fsdp"), P("fsdp"), row, row, row, P(), P(), row, P("fsdp"), row, row, row,
        ),
        out_specs=(act, act) + (own,) * 7 + (P(),) * 4,
        check_vma=False,
    )
```
